256 devices in a mesh: gx: 16 (over y_lo, x, core), ch: 16 (over z, y_hi).
Axes of the slice: x: 4, y: 4 (y_hi: 2, y_lo: 2; y = y_hi * 2 + y_lo), z: 8, core: 2. Of those that a mesh axis runs over, the one named last changes fastest.
Arguments:
- activations: bfloat16 [128, 256, 4, 128], P('ch', 'gx'), may hold values from -6 to 6
- conv_weight: bfloat16 [27, 128, 128], P(None, None, 'ch'), may hold values from -0.109375 to 0.109375
- out_grad: bfloat16 [128, 256, 4, 128], P('ch', 'gx'), may hold values from -6 to 6
Outputs:
- features_out: bfloat16 [128, 256, 4, 128], P('ch', 'gx')
- input_grad: bfloat16 [128, 256, 4, 128], P('ch', 'gx')
The draws below stay inside these ranges and needn't reach their ends.
All inputs are finite; a program needn't handle non-finite values.
Results may differ from the reference program's by a relative error of at most 0.001.
Values may be sent and summed in bfloat16 or wider, within the bound.
No kernel may reach another device: no remote copies, remote signals or barrier semaphores. Data moves between devices by JAX's collectives and lax.ppermute only.
A program may use at most 64 MiB of HBM per device.

```python
import jax
import jax.numpy as jnp

C = 128
YW = 128
ZW = 4
X = 256


def levels(key, shape, split, least, high):
    gain, own = 1.0, jax.random.fold_in(key, 6)
    for axis_at, parts in split:
        draws = jnp.exp(jax.random.uniform(jax.random.fold_in(own, axis_at), (parts,), jnp.float32, least / len(split), high / len(split)))
        gain = gain * jnp.repeat(draws, shape[axis_at] // parts).reshape([-1 if axis == axis_at else 1 for axis in range(len(shape))])
    return gain


def gaussian(own_key, dims, width, bound, pieces=(), dtype=jnp.bfloat16):
    result = jax.random.normal(own_key, dims, jnp.float32) * width
    if len(pieces) > 0:
        result = levels(own_key, dims, pieces, -0.22, 0.18) * result
    return jnp.clip(result, min=-bound, max=bound).astype(dtype)


def setup_inputs(seed: int = 0) -> dict:
    streams_of = jax.random.split(jax.random.key(seed), 4)
    return {
        "activations": gaussian(streams_of[0], (C, X, ZW, YW), 1.0, 6.0, ((0, 16), (1, 16))),
        "conv_weight": gaussian(streams_of[1], (27, C, C), (27 * C) ** -0.5, 0.109375, ((2, 16),)),
        "out_grad": gaussian(streams_of[2], (C, X, ZW, YW), 1.0, 6.0, ((0, 16), (1, 16))),
    }


def shifted(field, along_x, along_y, along_z):
    rolled = jnp.roll(field, -along_x, axis=1)
    padded = jnp.pad(rolled, ((0, 0), (0, 0), (1, 1), (1, 1)))
    return padded[:, :, 1 + along_z:1 + along_z + ZW, 1 + along_y:1 + along_y + YW]


def reference(activations, conv_weight, out_grad):
    summed_out = jnp.zeros((C, X * ZW * YW), jnp.float32)
    summed_grad = jnp.zeros((C, X * ZW * YW), jnp.float32)
    for first in range(3):
        for second in range(3):
            for third in range(3):
                tap = 9 * first + 3 * second + third
                source = shifted(activations, first - 1, second - 1, third - 1).reshape(C, -1)
                summed_out = summed_out + jnp.dot(conv_weight[tap].T, source, preferred_element_type=jnp.float32)
                back = shifted(out_grad, 1 - first, 1 - second, 1 - third).reshape(C, -1)
                summed_grad = summed_grad + jnp.dot(conv_weight[tap], back, preferred_element_type=jnp.float32)
    features_out = summed_out.reshape(C, X, ZW, YW).astype(jnp.bfloat16)
    input_grad = summed_grad.reshape(C, X, ZW, YW).astype(jnp.bfloat16)
    return features_out, input_grad
```

```python
import functools

import jax
import jax.numpy as jnp
from jax import lax
from jax.experimental import pallas as pl
from jax.experimental.pallas import tpu as pltpu
from jax.sharding import PartitionSpec as P


VMEM = pl.BlockSpec(memory_space=pltpu.VMEM)
SMEM = pl.BlockSpec(memory_space=pltpu.SMEM)


def position(chip, count):
    return chip // 2 if chip % 2 == 0 else count - 1 - chip // 2


def pack_kernel(half_ref, act_ref, grad_ref, weight_ref, send_ref):
    count, (rows, _, depth, height) = send_ref.shape[0], act_ref.shape
    taps, _, fan = weight_ref.shape
    shared = (taps + 1) // 2
    first = half_ref[0] * (taps - shared)
    filters = weight_ref[pl.ds(first, shared)].reshape(shared * rows, fan)
    block = rows * depth
    for chip in range(count):
        plane = position(chip, count)
        send_ref[chip, 0:block, :] = act_ref[:, plane].reshape(block, height)
        send_ref[chip, block : 2 * block, :] = grad_ref[:, plane].reshape(block, height)
        send_ref[chip, 2 * block :, :] = filters


def conv_kernel(half_ref, own_ref, low_ref, high_ref, own_filters_ref, other_filters_ref, send_ref,
                filters_ref, forward_ref, backward_ref, cells_ref, wide_ref, *, depth, height):
    count, both, _ = own_ref.shape
    block = both // 2
    rows = block // depth
    channels = count * rows
    shared = own_filters_ref.shape[1] // rows
    taps = 27
    half = half_ref[0]
    filters_ref[half] = own_filters_ref[...]
    filters_ref[1 - half] = other_filters_ref[...]

    def spot(index):
        return slice(index * channels, (index + 1) * channels)

    for a in range(3):
        for b in range(3):
            for c in range(3):
                tap = 9 * a + 3 * b + c
                part = 0 if tap < shared else 1
                at = tap - part * (taps - shared)
                matrix = filters_ref[part, :, at * rows : (at + 1) * rows, :].reshape(channels, channels)
                forward_ref[spot(b), spot(3 * c + a)] = matrix
                backward_ref[spot(3 * c + a), spot(b)] = matrix

    lane = lax.broadcasted_iota(jnp.int32, (channels, height), 1)
    for tensor in range(2):
        direction = 1 - 2 * tensor
        cells_ref[...] = jnp.zeros_like(cells_ref)
        for a in range(3):
            source = (low_ref, own_ref, high_ref)[1 + direction * (a - 1)]
            piece = source[:, tensor * block : (tensor + 1) * block, :]
            wide_ref[...] = piece.astype(jnp.float32).reshape(channels * depth, height)
            for z in range(depth):
                values = wide_ref[pl.ds(z, channels, stride=depth), :].astype(jnp.bfloat16)
                for c in range(3):
                    target = z - direction * (c - 1)
                    if 0 <= target < depth:
                        cells_ref[spot(3 * c + a), target * height : (target + 1) * height] = values
        if tensor == 0:
            sums = jnp.dot(forward_ref[...], cells_ref[...], preferred_element_type=jnp.float32)
        else:
            sums = lax.dot_general(backward_ref[...], cells_ref[...], (((0,), (0,)), ((), ())),
                                   preferred_element_type=jnp.float32)
        for z in range(depth):
            columns = slice(z * height, (z + 1) * height)
            before, middle, after = (sums[spot(b), columns] for b in (1 - direction, 1, 1 + direction))
            before = jnp.where(lane == 0, 0.0, pltpu.roll(before, 1, 1))
            after = jnp.where(lane == height - 1, 0.0, pltpu.roll(after, height - 1, 1))
            wide_ref[pl.ds(z, channels, stride=depth), :] = before + middle + after
        result = wide_ref[...].astype(jnp.bfloat16).reshape(count, block, height)
        send_ref[:, tensor * block : (tensor + 1) * block, :] = result


def unpack_kernel(got_ref, features_ref, gradient_ref):
    count, both, height = got_ref.shape
    rows, _, depth, _ = features_ref.shape
    block = both // 2
    for chip in range(count):
        plane = position(chip, count)
        features_ref[:, plane] = got_ref[chip, 0:block, :].reshape(rows, depth, height)
        gradient_ref[:, plane] = got_ref[chip, block : 2 * block, :].reshape(rows, depth, height)


def local(slabs, count, activations, conv_weight, out_grad):
    rows, _, depth, height = activations.shape
    channels = conv_weight.shape[1]
    block = rows * depth
    shared = (conv_weight.shape[0] + 1) // 2
    half = (lax.axis_index("gx") % 2).astype(jnp.int32).reshape(1)
    bf16 = jnp.bfloat16
    send = pl.pallas_call(
        pack_kernel,
        out_shape=jax.ShapeDtypeStruct((count, 2 * block + shared * rows, height), bf16),
        in_specs=[SMEM, VMEM, VMEM, VMEM],
        out_specs=VMEM,
        name="pack",
    )(half, activations, out_grad, jnp.swapaxes(conv_weight, 1, 2))
    got = lax.all_to_all(send, "ch", 0, 0, tiled=True)
    own, own_filters = got[:, : 2 * block], got[:, 2 * block :]
    place = {position(chip, count): chip for chip in range(count)}
    order = [slab * count + place[plane] for slab in range(slabs) for plane in range(count)]
    ring = list(zip(order, order[1:] + order[:1]))
    low = lax.ppermute(own, ("gx", "ch"), ring)
    high = lax.ppermute(own, ("gx", "ch"), [(to, at) for at, to in ring])
    other_filters = lax.ppermute(own_filters, "gx", [(slab, slab ^ 1) for slab in range(slabs)])
    result = pl.pallas_call(
        functools.partial(conv_kernel, depth=depth, height=height),
        out_shape=jax.ShapeDtypeStruct((count, 2 * block, height), bf16),
        in_specs=[SMEM, VMEM, VMEM, VMEM, VMEM, VMEM],
        out_specs=VMEM,
        scratch_shapes=[
            pltpu.VMEM((2, count, shared * rows, channels), bf16),
            pltpu.VMEM((3 * channels, 9 * channels), bf16),
            pltpu.VMEM((9 * channels, 3 * channels), bf16),
            pltpu.VMEM((9 * channels, depth * height), bf16),
            pltpu.VMEM((channels * depth, height), jnp.float32),
        ],
        name="conv",
    )(half, own, low, high, own_filters, other_filters)
    back = lax.all_to_all(result, "ch", 0, 0, tiled=True)
    return pl.pallas_call(
        unpack_kernel,
        out_shape=(jax.ShapeDtypeStruct(activations.shape, bf16), jax.ShapeDtypeStruct(out_grad.shape, bf16)),
        in_specs=[VMEM],
        out_specs=(VMEM, VMEM),
        name="unpack",
    )(back)


def solution(mesh):
    return jax.shard_map(
        functools.partial(local, mesh.shape["gx"], mesh.shape["ch"]),
        mesh=mesh,
        in_specs=(P("ch", "gx", None, None), P(None, None, "ch"), P("ch", "gx", None, None)),
        out_specs=(P("ch", "gx", None, None), P("ch", "gx", None, None)),
        check_vma=False,
    )
```

```python
import functools

import jax
import jax.numpy as jnp
from jax import lax
from jax.experimental import pallas as pl
from jax.experimental.pallas import tpu as pltpu
from jax.sharding import PartitionSpec as P


VMEM = pl.BlockSpec(memory_space=pltpu.VMEM)
SMEM = pl.BlockSpec(memory_space=pltpu.SMEM)
PARAMS = pltpu.CompilerParams(vmem_limit_bytes=16 * 2**20)


def position(chip, count):
    return chip // 2 if chip % 2 == 0 else count - 1 - chip // 2


def pack_kernel(half_ref, act_ref, grad_ref, weight_ref, send_ref):
    count, (rows, _, depth, height) = send_ref.shape[0], act_ref.shape
    taps, _, fan = weight_ref.shape
    shared = (taps + 1) // 2
    first = half_ref[0] * (taps - shared)
    filters = weight_ref[pl.ds(first, shared)].reshape(shared * rows, fan)
    block = rows * depth
    for chip in range(count):
        plane = position(chip, count)
        send_ref[chip, 0:block, :] = act_ref[:, plane].reshape(block, height)
        send_ref[chip, block : 2 * block, :] = grad_ref[:, plane].reshape(block, height)
        send_ref[chip, 2 * block :, :] = filters


def conv_kernel(half_ref, own_ref, low_ref, high_ref, own_filters_ref, other_filters_ref, send_ref,
                filters_ref, forward_ref, backward_ref, cells_ref, wide_ref, *, depth, height):
    count, both, _ = own_ref.shape
    block = both // 2
    rows = block // depth
    channels = count * rows
    shared = own_filters_ref.shape[1] // rows
    taps = 27
    half = half_ref[0]
    filters_ref[half] = own_filters_ref[...]
    filters_ref[1 - half] = other_filters_ref[...]

    def spot(index):
        return slice(index * channels, (index + 1) * channels)

    for a in range(3):
        for b in range(3):
            for c in range(3):
                tap = 9 * a + 3 * b + c
                part = 0 if tap < shared else 1
                at = tap - part * (taps - shared)
                matrix = filters_ref[part, :, at * rows : (at + 1) * rows, :].reshape(channels, channels)
                forward_ref[spot(b), spot(3 * c + a)] = matrix
                backward_ref[spot(3 * c + a), spot(b)] = matrix

    lane = lax.broadcasted_iota(jnp.int32, (channels, height), 1)
    for tensor in range(2):
        direction = 1 - 2 * tensor
        cells_ref[...] = jnp.zeros_like(cells_ref)
        for a in range(3):
            source = (low_ref, own_ref, high_ref)[1 + direction * (a - 1)]
            piece = source[:, tensor * block : (tensor + 1) * block, :]
            wide_ref[...] = piece.astype(jnp.float32).reshape(channels * depth, height)
            for z in range(depth):
                values = wide_ref[pl.ds(z, channels, stride=depth), :].astype(jnp.bfloat16)
                for c in range(3):
                    target = z - direction * (c - 1)
                    if 0 <= target < depth:
                        cells_ref[spot(3 * c + a), target * height : (target + 1) * height] = values
        if tensor == 0:
            sums = jnp.dot(forward_ref[...], cells_ref[...], preferred_element_type=jnp.float32)
        else:
            sums = lax.dot_general(backward_ref[...], cells_ref[...], (((0,), (0,)), ((), ())),
                                   preferred_element_type=jnp.float32)
        for z in range(depth):
            columns = slice(z * height, (z + 1) * height)
            before, middle, after = (sums[spot(b), columns] for b in (1 - direction, 1, 1 + direction))
            before = jnp.where(lane == 0, 0.0, pltpu.roll(before, 1, 1))
            after = jnp.where(lane == height - 1, 0.0, pltpu.roll(after, height - 1, 1))
            wide_ref[pl.ds(z, channels, stride=depth), :] = before + middle + after
        result = wide_ref[...].astype(jnp.bfloat16).reshape(count, block, height)
        send_ref[:, tensor * block : (tensor + 1) * block, :] = result


def unpack_kernel(got_ref, features_ref, gradient_ref):
    count, both, height = got_ref.shape
    rows, _, depth, _ = features_ref.shape
    block = both // 2
    for chip in range(count):
        plane = position(chip, count)
        features_ref[:, plane] = got_ref[chip, 0:block, :].reshape(rows, depth, height)
        gradient_ref[:, plane] = got_ref[chip, block : 2 * block, :].reshape(rows, depth, height)


def local(slabs, count, activations, conv_weight, out_grad):
    rows, _, depth, height = activations.shape
    channels = conv_weight.shape[1]
    block = rows * depth
    shared = (conv_weight.shape[0] + 1) // 2
    half = (lax.axis_index("gx") % 2).astype(jnp.int32).reshape(1)
    bf16 = jnp.bfloat16
    send = pl.pallas_call(
        pack_kernel,
        out_shape=jax.ShapeDtypeStruct((count, 2 * block + shared * rows, height), bf16),
        in_specs=[SMEM, VMEM, VMEM, VMEM],
        out_specs=VMEM,
        compiler_params=PARAMS,
        name="pack",
    )(half, activations, out_grad, jnp.swapaxes(conv_weight, 1, 2))
    got = lax.all_to_all(send, "ch", 0, 0, tiled=True)
    own, own_filters = got[:, : 2 * block], got[:, 2 * block :]
    place = {position(chip, count): chip for chip in range(count)}
    order = [slab * count + place[plane] for slab in range(slabs) for plane in range(count)]
    ring = list(zip(order, order[1:] + order[:1]))
    low = lax.ppermute(own, ("gx", "ch"), ring)
    high = lax.ppermute(own, ("gx", "ch"), [(to, at) for at, to in ring])
    other_filters = lax.ppermute(own_filters, "gx", [(slab, slab ^ 1) for slab in range(slabs)])
    result = pl.pallas_call(
        functools.partial(conv_kernel, depth=depth, height=height),
        out_shape=jax.ShapeDtypeStruct((count, 2 * block, height), bf16),
        in_specs=[SMEM, VMEM, VMEM, VMEM, VMEM, VMEM],
        out_specs=VMEM,
        scratch_shapes=[
            pltpu.VMEM((2, count, shared * rows, channels), bf16),
            pltpu.VMEM((3 * channels, 9 * channels), bf16),
            pltpu.VMEM((9 * channels, 3 * channels), bf16),
            pltpu.VMEM((9 * channels, depth * height), bf16),
            pltpu.VMEM((channels * depth, height), jnp.float32),
        ],
        compiler_params=PARAMS,
        name="conv",
    )(half, own, low, high, own_filters, other_filters)
    back = lax.all_to_all(result, "ch", 0, 0, tiled=True)
    return pl.pallas_call(
        unpack_kernel,
        out_shape=(jax.ShapeDtypeStruct(activations.shape, bf16), jax.ShapeDtypeStruct(out_grad.shape, bf16)),
        in_specs=[VMEM],
        out_specs=(VMEM, VMEM),
        compiler_params=PARAMS,
        name="unpack",
    )(back)


def solution(mesh):
    return jax.shard_map(
        functools.partial(local, mesh.shape["gx"], mesh.shape["ch"]),
        mesh=mesh,
        in_specs=(P("ch", "gx", None, None), P(None, None, "ch"), P("ch", "gx", None, None)),
        out_specs=(P("ch", "gx", None, None), P("ch", "gx", None, None)),
        check_vma=False,
    )
```

```python
import functools

import jax
import jax.numpy as jnp
from jax import lax
from jax.experimental import pallas as pl
from jax.experimental.pallas import tpu as pltpu
from jax.sharding import PartitionSpec as P


VMEM = pl.BlockSpec(memory_space=pltpu.VMEM)
SMEM = pl.BlockSpec(memory_space=pltpu.SMEM)
HBM = pl.BlockSpec(memory_space=pltpu.HBM)
PARAMS = pltpu.CompilerParams(vmem_limit_bytes=16 * 2**20)
F32 = jnp.float32
BF16 = jnp.bfloat16


def lanes(shape):
    return lax.broadcasted_iota(jnp.int32, shape, len(shape) - 1)


def both(first, second):
    size = first.shape[-1]
    early = lanes(first.shape) < size // 2
    turned_first, turned_second = (pltpu.roll(x, size // 2, x.ndim - 1) for x in (first, second))
    return jnp.where(early, first, turned_second), jnp.where(early, turned_first, second)


def pack_kernel(half_ref, act_hbm, grad_hbm, weight_hbm, send_ref, act_ref, grad_ref, weight_ref, rows_ref, sems):
    copies = [
        pltpu.make_async_copy(source, target, sems.at[at])
        for at, (source, target) in enumerate(
            ((act_hbm, act_ref), (grad_hbm, grad_ref), (weight_hbm, weight_ref))
        )
    ]
    for copy in copies:
        copy.start()
    count, (rows, _, depth, height) = send_ref.shape[0], act_ref.shape
    taps, _, fan = weight_ref.shape
    shared = (taps + 1) // 2
    block = rows * depth
    side = height // 2
    copies[0].wait()
    copies[1].wait()
    lane = lanes((rows, height))
    for pair in range(count // 2):
        edges = [jnp.zeros((rows, height), F32) for _ in range(2)]
        for plane in range(2):
            maps = []
            for tensor, ref in enumerate((act_ref, grad_ref)):
                values = ref[:, 2 * pair + plane].reshape(block, height).astype(F32)
                maps.append(values)
                rows_ref[...] = values
                for z in range(depth):
                    column = rows_ref[pl.ds(z, rows, stride=depth), :]
                    spot = side * plane + 8 * tensor + z
                    for half in range(2):
                        edge = side - half
                        turned = pltpu.roll(column, (spot - edge) % height, 1)
                        edges[half] = jnp.where(lane == spot, turned, edges[half])
            start = plane * (block + rows)
            for half, values in enumerate(both(*maps)):
                send_ref[2 * pair + half, start : start + block, :] = values.astype(BF16)
        for half in range(2):
            send_ref[2 * pair + half, block : block + rows, :] = edges[half].astype(BF16)
    copies[2].wait()
    first = half_ref[0] * (taps - shared)
    filters = weight_ref[pl.ds(first, shared)].reshape(shared * rows, fan)
    for chip in range(count):
        send_ref[chip, 2 * block + rows :, :] = filters


def conv_kernel(half_ref, own_ref, low_ref, high_ref, own_filters_ref, other_filters_ref, send_ref,
                filters_ref, forward_ref, backward_ref, cells_ref, wide_ref, *, depth):
    count, span, height = own_ref.shape
    rows = span // (2 * depth + 1)
    block = rows * depth
    channels = count * rows
    side = height // 2
    shared = own_filters_ref.shape[1] // rows
    taps = 27
    half, right = half_ref[0], half_ref[1]
    filters_ref[half] = own_filters_ref[...]
    filters_ref[1 - half] = other_filters_ref[...]

    def spot(index):
        return slice(index * channels, (index + 1) * channels)

    for a in range(3):
        for b in range(3):
            for c in range(3):
                tap = 9 * a + 3 * b + c
                part = 0 if tap < shared else 1
                at = tap - part * (taps - shared)
                matrix = filters_ref[part, :, at * rows : (at + 1) * rows, :].reshape(channels, channels)
                forward_ref[spot(b), spot(3 * c + a)] = matrix
                backward_ref[spot(3 * c + a), spot(b)] = matrix

    lane = lanes((channels, height))
    early = lane < side
    within = lane % side

    def edge_of(ref, start):
        return ref[:, start : start + rows, :].astype(F32).reshape(channels, height)

    own_edge, low_edge, high_edge = edge_of(own_ref, block), edge_of(low_ref, 0), edge_of(high_ref, block)
    edges = (
        pltpu.roll(jnp.where(early, own_edge, low_edge), side, 1),
        own_edge,
        pltpu.roll(jnp.where(early, high_edge, own_edge), side, 1),
    )
    planes = (
        low_ref[:, rows : rows + block, :],
        own_ref[:, 0:block, :],
        own_ref[:, block + rows : 2 * block + rows, :],
        high_ref[:, 0:block, :],
    )
    for at, values in enumerate(planes):
        wide_ref[at] = values.astype(F32).reshape(channels * depth, height)

    for c in range(3):
        for tensor in range(2):
            direction = 1 - 2 * tensor
            outside = 0 if direction * (c - 1) < 0 else depth - 1
            if c != 1:
                cells_ref[tensor, 3 * c * channels : 3 * (c + 1) * channels, outside * height : (outside + 1) * height] = (
                    jnp.zeros((3 * channels, height), BF16)
                )
            for a in range(3):
                edge = edges[1 + direction * (a - 1)]
                shift = 8 * tensor + direction * (c - 1)
                source = within + direction * (c - 1)
                inside = (within < depth) & (source >= 0) & (source < depth)
                moved = pltpu.roll(edge, -shift % height, 1)
                cells_ref[tensor, spot(3 * c + a), depth * height :] = jnp.where(inside, moved, 0.0).astype(BF16)
    for z in range(depth):
        pieces = [wide_ref[at, pl.ds(z, channels, stride=depth), :] for at in range(4)]
        for step in range(3):
            for tensor, values in enumerate(both_planes(pieces[step], pieces[step + 1], early, side)):
                direction = 1 - 2 * tensor
                a = 1 + direction * (step - 1)
                values = values.astype(BF16)
                for c in range(3):
                    target = z - direction * (c - 1)
                    if 0 <= target < depth:
                        cells_ref[tensor, spot(3 * c + a), target * height : (target + 1) * height] = values

    for tensor in range(2):
        direction = 1 - 2 * tensor
        if tensor == 0:
            sums = jnp.dot(forward_ref[...], cells_ref[0], preferred_element_type=F32)
        else:
            sums = lax.dot_general(backward_ref[...], cells_ref[1], (((0,), (0,)), ((), ())),
                                   preferred_element_type=F32)
        beyond = sums[:, depth * height :]
        beyond = jnp.where(right == 1, beyond[spot(1 - direction)], beyond[spot(1 + direction)])
        border = jnp.where(right == 1, 0, side - 1)
        for z in range(depth):
            columns = slice(z * height, (z + 1) * height)
            before, middle, after = (sums[spot(b), columns] for b in (1 - direction, 1, 1 + direction))
            before = jnp.where(within == 0, 0.0, pltpu.roll(before, 1, 1))
            after = jnp.where(within == side - 1, 0.0, pltpu.roll(after, height - 1, 1))
            extra = jnp.where(within == border, pltpu.roll(beyond, border + (height - z), 1), 0.0)
            wide_ref[tensor, pl.ds(z, channels, stride=depth), :] = before + middle + after + extra
        result = wide_ref[tensor].astype(BF16).reshape(count, block, height)
        send_ref[:, tensor * block : (tensor + 1) * block, :] = result


def both_planes(first, second, early, side):
    turned_first, turned_second = pltpu.roll(first, side, 1), pltpu.roll(second, side, 1)
    return jnp.where(early, first, turned_second), jnp.where(early, turned_first, second)


def unpack_kernel(got_ref, features_ref, gradient_ref):
    count, span, height = got_ref.shape
    rows, _, depth, _ = features_ref.shape
    block = rows * depth
    for pair in range(count // 2):
        for tensor, ref in enumerate((features_ref, gradient_ref)):
            start = tensor * block
            halves = [got_ref[2 * pair + side, start : start + block, :].astype(F32) for side in range(2)]
            for plane, values in enumerate(both(*halves)):
                ref[:, 2 * pair + plane] = values.astype(BF16).reshape(rows, depth, height)


def local(slabs, count, activations, conv_weight, out_grad):
    rows, _, depth, height = activations.shape
    taps, channels, _ = conv_weight.shape
    block = rows * depth
    span = 2 * block + rows
    shared = (taps + 1) // 2
    pairs = count // 2
    half = jnp.stack([lax.axis_index("gx") % 2, lax.axis_index("ch") % 2]).astype(jnp.int32)
    send = pl.pallas_call(
        pack_kernel,
        out_shape=jax.ShapeDtypeStruct((count, span + shared * rows, height), BF16),
        in_specs=[SMEM, HBM, HBM, HBM],
        out_specs=VMEM,
        scratch_shapes=[
            pltpu.VMEM(activations.shape, BF16),
            pltpu.VMEM(out_grad.shape, BF16),
            pltpu.VMEM((taps, rows, channels), BF16),
            pltpu.VMEM((block, height), F32),
            pltpu.SemaphoreType.DMA((3,)),
        ],
        compiler_params=PARAMS,
        name="pack",
    )(half, activations, out_grad, jnp.swapaxes(conv_weight, 1, 2))
    got = lax.all_to_all(send, "ch", 0, 0, tiled=True)
    own, own_filters = got[:, :span], got[:, span:]
    ring = []
    for side in range(2):
        order = [slab * count + 2 * pair + side for slab in range(slabs) for pair in range(pairs)]
        ring += zip(order, order[1:] + order[:1])
    low = lax.ppermute(got[:, block:span], ("gx", "ch"), ring)
    high = lax.ppermute(got[:, : block + rows], ("gx", "ch"), [(to, at) for at, to in ring])
    other_filters = lax.ppermute(own_filters, "gx", [(slab, slab ^ 1) for slab in range(slabs)])
    result = pl.pallas_call(
        functools.partial(conv_kernel, depth=depth),
        out_shape=jax.ShapeDtypeStruct((count, 2 * block, height), BF16),
        in_specs=[SMEM, VMEM, VMEM, VMEM, VMEM, VMEM],
        out_specs=VMEM,
        scratch_shapes=[
            pltpu.VMEM((2, count, shared * rows, channels), BF16),
            pltpu.VMEM((3 * channels, 9 * channels), BF16),
            pltpu.VMEM((9 * channels, 3 * channels), BF16),
            pltpu.VMEM((2, 9 * channels, (depth + 1) * height), BF16),
            pltpu.VMEM((4, channels * depth, height), F32),
        ],
        compiler_params=PARAMS,
        name="conv",
    )(half, own, low, high, own_filters, other_filters)
    back = lax.all_to_all(result, "ch", 0, 0, tiled=True)
    return pl.pallas_call(
        unpack_kernel,
        out_shape=(jax.ShapeDtypeStruct(activations.shape, BF16), jax.ShapeDtypeStruct(out_grad.shape, BF16)),
        in_specs=[VMEM],
        out_specs=(VMEM, VMEM),
        compiler_params=PARAMS,
        name="unpack",
    )(back)


def solution(mesh):
    return jax.shard_map(
        functools.partial(local, mesh.shape["gx"], mesh.shape["ch"]),
        mesh=mesh,
        in_specs=(P("ch", "gx", None, None), P(None, None, "ch"), P("ch", "gx", None, None)),
        out_specs=(P("ch", "gx", None, None), P("ch", "gx", None, None)),
        check_vma=False,
    )
```

```python
import functools

import jax
import jax.numpy as jnp
from jax import lax
from jax.experimental import pallas as pl
from jax.experimental.pallas import tpu as pltpu
from jax.sharding import PartitionSpec as P


VMEM = pl.BlockSpec(memory_space=pltpu.VMEM)
SMEM = pl.BlockSpec(memory_space=pltpu.SMEM)
HBM = pl.BlockSpec(memory_space=pltpu.HBM)
PARAMS = pltpu.CompilerParams(vmem_limit_bytes=16 * 2**20)
F32 = jnp.float32
BF16 = jnp.bfloat16


def lanes(shape):
    return lax.broadcasted_iota(jnp.int32, shape, len(shape) - 1)


def pair_of(level, core, count):
    return level + core * (count // 2 - 1 - 2 * level)


def both(first, second):
    size = first.shape[-1]
    early = lanes(first.shape) < size // 2
    turned_first, turned_second = (pltpu.roll(x, size // 2, x.ndim - 1) for x in (first, second))
    return jnp.where(early, first, turned_second), jnp.where(early, turned_first, second)


def pack_kernel(half_ref, act_hbm, grad_hbm, weight_hbm, send_ref, act_ref, grad_ref, weight_ref, rows_ref, sems):
    copies = [
        pltpu.make_async_copy(source, target, sems.at[at])
        for at, (source, target) in enumerate(
            ((act_hbm, act_ref), (grad_hbm, grad_ref), (weight_hbm, weight_ref))
        )
    ]
    for copy in copies:
        copy.start()
    count, (rows, _, depth, height) = send_ref.shape[0], act_ref.shape
    taps, _, fan = weight_ref.shape
    shared = (taps + 1) // 2
    block = rows * depth
    side = height // 2
    copies[0].wait()
    copies[1].wait()
    lane = lanes((rows, height))
    for level in range(count // 2):
        pair = pair_of(level, half_ref[0], count)
        edges = [jnp.zeros((rows, height), F32) for _ in range(2)]
        for plane in range(2):
            maps = []
            for tensor, ref in enumerate((act_ref, grad_ref)):
                values = ref[:, 2 * pair + plane].reshape(block, height).astype(F32)
                maps.append(values)
                rows_ref[...] = values
                for z in range(depth):
                    column = rows_ref[pl.ds(z, rows, stride=depth), :]
                    spot = side * plane + 8 * tensor + z
                    for half in range(2):
                        edge = side - half
                        turned = pltpu.roll(column, (spot - edge) % height, 1)
                        edges[half] = jnp.where(lane == spot, turned, edges[half])
            start = plane * (block + rows)
            for half, values in enumerate(both(*maps)):
                send_ref[2 * level + half, start : start + block, :] = values.astype(BF16)
        for half in range(2):
            send_ref[2 * level + half, block : block + rows, :] = edges[half].astype(BF16)
    copies[2].wait()
    first = half_ref[0] * (taps - shared)
    filters = weight_ref[pl.ds(first, shared)].reshape(shared * rows, fan)
    for chip in range(count):
        send_ref[chip, 2 * block + rows :, :] = filters


def prepare_kernel(half_ref, own_ref, other_ref, forward_ref, backward_ref, filters_ref):
    count, shared, channels = own_ref.shape
    rows = channels // count
    shared //= rows
    taps = 27
    filters_ref[half_ref[0]] = own_ref[...]
    filters_ref[1 - half_ref[0]] = other_ref[...]

    def spot(index):
        return slice(index * channels, (index + 1) * channels)

    for a in range(3):
        for b in range(3):
            for c in range(3):
                tap = 9 * a + 3 * b + c
                part = 0 if tap < shared else 1
                at = tap - part * (taps - shared)
                matrix = filters_ref[part, :, at * rows : (at + 1) * rows, :].reshape(channels, channels)
                forward_ref[spot(b), spot(3 * c + a)] = matrix
                backward_ref[spot(b), spot(3 * c + a)] = matrix.T


def conv_kernel(half_ref, own_ref, low_ref, high_ref, forward_ref, backward_ref, send_ref, cells_ref, wide_ref, *, depth):
    count, span, height = own_ref.shape
    rows = span // (2 * depth + 1)
    block = rows * depth
    channels = count * rows
    side = height // 2
    right = half_ref[1]

    def spot(index):
        return slice(index * channels, (index + 1) * channels)

    lane = lanes((channels, height))
    early = lane < side
    within = lane % side

    def edge_of(ref, start):
        return ref[:, start : start + rows, :].astype(F32).reshape(channels, height)

    own_edge, low_edge, high_edge = edge_of(own_ref, block), edge_of(low_ref, 0), edge_of(high_ref, block)
    edges = (
        pltpu.roll(jnp.where(early, own_edge, low_edge), side, 1),
        own_edge,
        pltpu.roll(jnp.where(early, high_edge, own_edge), side, 1),
    )
    planes = (
        low_ref[:, rows : rows + block, :],
        own_ref[:, 0:block, :],
        own_ref[:, block + rows : 2 * block + rows, :],
        high_ref[:, 0:block, :],
    )
    for at, values in enumerate(planes):
        wide_ref[at] = values.astype(F32).reshape(channels * depth, height)

    for c in range(3):
        for tensor in range(2):
            direction = 1 - 2 * tensor
            outside = 0 if direction * (c - 1) < 0 else depth - 1
            if c != 1:
                cells_ref[tensor, 3 * c * channels : 3 * (c + 1) * channels, outside * height : (outside + 1) * height] = (
                    jnp.zeros((3 * channels, height), BF16)
                )
            for a in range(3):
                edge = edges[1 + direction * (a - 1)]
                shift = 8 * tensor + direction * (c - 1)
                source = within + direction * (c - 1)
                inside = (within < depth) & (source >= 0) & (source < depth)
                moved = pltpu.roll(edge, -shift % height, 1)
                cells_ref[tensor, spot(3 * c + a), depth * height :] = jnp.where(inside, moved, 0.0).astype(BF16)
    for z in range(depth):
        pieces = [wide_ref[at, pl.ds(z, channels, stride=depth), :] for at in range(4)]
        for step in range(3):
            for tensor, values in enumerate(both_planes(pieces[step], pieces[step + 1], early, side)):
                direction = 1 - 2 * tensor
                a = 1 + direction * (step - 1)
                values = values.astype(BF16)
                for c in range(3):
                    target = z - direction * (c - 1)
                    if 0 <= target < depth:
                        cells_ref[tensor, spot(3 * c + a), target * height : (target + 1) * height] = values

    for tensor in range(2):
        direction = 1 - 2 * tensor
        filters = (forward_ref, backward_ref)[tensor][...]
        sums = jnp.dot(filters, cells_ref[tensor], preferred_element_type=F32)
        beyond = sums[:, depth * height :]
        beyond = jnp.where(right == 1, beyond[spot(1 - direction)], beyond[spot(1 + direction)])
        border = jnp.where(right == 1, 0, side - 1)
        for z in range(depth):
            columns = slice(z * height, (z + 1) * height)
            before, middle, after = (sums[spot(b), columns] for b in (1 - direction, 1, 1 + direction))
            before = jnp.where(within == 0, 0.0, pltpu.roll(before, 1, 1))
            after = jnp.where(within == side - 1, 0.0, pltpu.roll(after, height - 1, 1))
            extra = jnp.where(within == border, pltpu.roll(beyond, border + (height - z), 1), 0.0)
            wide_ref[tensor, pl.ds(z, channels, stride=depth), :] = before + middle + after + extra
        result = wide_ref[tensor].astype(BF16).reshape(count, block, height)
        send_ref[:, tensor * block : (tensor + 1) * block, :] = result


def both_planes(first, second, early, side):
    turned_first, turned_second = pltpu.roll(first, side, 1), pltpu.roll(second, side, 1)
    return jnp.where(early, first, turned_second), jnp.where(early, turned_first, second)


def unpack_kernel(half_ref, got_ref, features_ref, gradient_ref):
    count, span, height = got_ref.shape
    rows, _, depth, _ = features_ref.shape
    block = rows * depth
    for level in range(count // 2):
        pair = pair_of(level, half_ref[0], count)
        for tensor, ref in enumerate((features_ref, gradient_ref)):
            start = tensor * block
            halves = [got_ref[2 * level + side, start : start + block, :].astype(F32) for side in range(2)]
            for plane, values in enumerate(both(*halves)):
                ref[:, 2 * pair + plane] = values.astype(BF16).reshape(rows, depth, height)


def local(slabs, count, activations, conv_weight, out_grad):
    rows, _, depth, height = activations.shape
    taps, channels, _ = conv_weight.shape
    block = rows * depth
    span = 2 * block + rows
    shared = (taps + 1) // 2
    pairs = count // 2
    half = jnp.stack([lax.axis_index("gx") % 2, lax.axis_index("ch") % 2]).astype(jnp.int32)
    send = pl.pallas_call(
        pack_kernel,
        out_shape=jax.ShapeDtypeStruct((count, span + shared * rows, height), BF16),
        in_specs=[SMEM, HBM, HBM, HBM],
        out_specs=VMEM,
        scratch_shapes=[
            pltpu.VMEM(activations.shape, BF16),
            pltpu.VMEM(out_grad.shape, BF16),
            pltpu.VMEM((taps, rows, channels), BF16),
            pltpu.VMEM((block, height), F32),
            pltpu.SemaphoreType.DMA((3,)),
        ],
        compiler_params=PARAMS,
        name="pack",
    )(half, *(pltpu.with_memory_space_constraint(x, pltpu.HBM) for x in (activations, out_grad, jnp.swapaxes(conv_weight, 1, 2))))
    got = lax.all_to_all(send, "ch", 0, 0, tiled=True)
    own, own_filters = got[:, :span], got[:, span:]
    ring = []
    for side in range(2):
        order = [
            slab * count + 2 * pair_of(pair, slab % 2, count) + side for slab in range(slabs) for pair in range(pairs)
        ]
        ring += zip(order, order[1:] + order[:1])
    low = lax.ppermute(got[:, block:span], ("gx", "ch"), ring)
    high = lax.ppermute(got[:, : block + rows], ("gx", "ch"), [(to, at) for at, to in ring])
    other_filters = lax.ppermute(own_filters, "gx", [(slab, slab ^ 1) for slab in range(slabs)])
    forward, backward = pl.pallas_call(
        prepare_kernel,
        out_shape=[jax.ShapeDtypeStruct((3 * channels, 9 * channels), BF16)] * 2,
        in_specs=[SMEM, VMEM, VMEM],
        out_specs=[VMEM, VMEM],
        scratch_shapes=[pltpu.VMEM((2, count, shared * rows, channels), BF16)],
        cost_estimate=pl.CostEstimate(flops=0, bytes_accessed=4 * 2**20, transcendentals=0),
        compiler_params=PARAMS,
        name="prepare",
    )(half, own_filters, other_filters)
    result = pl.pallas_call(
        functools.partial(conv_kernel, depth=depth),
        out_shape=jax.ShapeDtypeStruct((count, 2 * block, height), BF16),
        in_specs=[SMEM, VMEM, VMEM, VMEM, VMEM, VMEM],
        out_specs=VMEM,
        scratch_shapes=[
            pltpu.VMEM((2, 9 * channels, (depth + 1) * height), BF16),
            pltpu.VMEM((4, channels * depth, height), F32),
        ],
        compiler_params=PARAMS,
        name="conv",
    )(half, own, low, high, forward, backward)
    back = lax.all_to_all(result, "ch", 0, 0, tiled=True)
    return pl.pallas_call(
        unpack_kernel,
        out_shape=(jax.ShapeDtypeStruct(activations.shape, BF16), jax.ShapeDtypeStruct(out_grad.shape, BF16)),
        in_specs=[SMEM, VMEM],
        out_specs=(VMEM, VMEM),
        compiler_params=PARAMS,
        name="unpack",
    )(half, back)


def solution(mesh):
    return jax.shard_map(
        functools.partial(local, mesh.shape["gx"], mesh.shape["ch"]),
        mesh=mesh,
        in_specs=(P("ch", "gx", None, None), P(None, None, "ch"), P("ch", "gx", None, None)),
        out_specs=(P("ch", "gx", None, None), P("ch", "gx", None, None)),
        check_vma=False,
    )
```

```python
import functools

import jax
import jax.numpy as jnp
from jax import lax
from jax.experimental import pallas as pl
from jax.experimental.pallas import tpu as pltpu
from jax.sharding import PartitionSpec as P


VMEM = pl.BlockSpec(memory_space=pltpu.VMEM)
HBM = pl.BlockSpec(memory_space=pltpu.HBM)
PARAMS = pltpu.CompilerParams(vmem_limit_bytes=16 * 2**20)
F32 = jnp.float32
BF16 = jnp.bfloat16


def lanes(shape):
    return lax.broadcasted_iota(jnp.int32, shape, len(shape) - 1)


def pair_of(level, core, count):
    return level + core * (count // 2 - 1 - 2 * level)


def quarter(taps, index):
    size = (taps + 3) // 4
    return (min(index * size, taps - size) if isinstance(index, int) else jnp.minimum(index * size, taps - size)), size


def both(first, second):
    size = first.shape[-1]
    early = lanes(first.shape) < size // 2
    turned_first, turned_second = (pltpu.roll(x, size // 2, x.ndim - 1) for x in (first, second))
    return jnp.where(early, first, turned_second), jnp.where(early, turned_first, second)


def pack_kernel(act_hbm, grad_hbm, weight_hbm, send_ref, act_ref, grad_ref, weight_ref, rows_ref, sems):
    copies = [
        pltpu.make_async_copy(source, target, sems.at[at])
        for at, (source, target) in enumerate(
            ((act_hbm, act_ref), (grad_hbm, grad_ref), (weight_hbm, weight_ref))
        )
    ]
    for copy in copies:
        copy.start()
    core = lax.rem(lax.axis_index("gx"), 2)
    count, (rows, _, depth, height) = send_ref.shape[0], act_ref.shape
    taps, _, fan = weight_ref.shape
    block = rows * depth
    side = height // 2
    copies[0].wait()
    copies[1].wait()
    lane = lanes((rows, height))
    for level in range(count // 2):
        pair = pair_of(level, core, count)
        edges = [jnp.zeros((rows, height), F32) for _ in range(2)]
        for plane in range(2):
            maps = []
            for tensor, ref in enumerate((act_ref, grad_ref)):
                values = ref[:, 2 * pair + plane].reshape(block, height).astype(F32)
                maps.append(values)
                rows_ref[...] = values
                for z in range(depth):
                    column = rows_ref[pl.ds(z, rows, stride=depth), :]
                    spot = side * plane + 8 * tensor + z
                    for half in range(2):
                        edge = side - half
                        turned = pltpu.roll(column, (spot - edge) % height, 1)
                        edges[half] = jnp.where(lane == spot, turned, edges[half])
            start = plane * (block + rows)
            for half, values in enumerate(both(*maps)):
                send_ref[2 * level + half, start : start + block, :] = values.astype(BF16)
        for half in range(2):
            send_ref[2 * level + half, block : block + rows, :] = edges[half].astype(BF16)
    copies[2].wait()
    first, shared = quarter(taps, lax.rem(lax.axis_index("gx"), 4))
    filters = weight_ref[pl.ds(first, shared)].reshape(shared * rows, fan)
    for chip in range(count):
        send_ref[chip, 2 * block + rows :, :] = filters


def prepare_kernel(own_ref, core_ref, x_ref, diagonal_ref, forward_ref, backward_ref, filters_ref, *, taps):
    count, _, channels = own_ref.shape
    rows = channels // count
    mine = lax.rem(lax.axis_index("gx"), 4)
    core, x = lax.rem(mine, 2), mine // 2
    for at, ref in ((2 * x + core, own_ref), (2 * x + 1 - core, core_ref),
                    (2 - 2 * x + core, x_ref), (3 - 2 * x - core, diagonal_ref)):
        filters_ref[at] = ref[...]

    def spot(index):
        return slice(index * channels, (index + 1) * channels)

    for a in range(3):
        for b in range(3):
            for c in range(3):
                tap = 9 * a + 3 * b + c
                part = tap // quarter(taps, 0)[1]
                at = tap - quarter(taps, part)[0]
                matrix = filters_ref[part, :, at * rows : (at + 1) * rows, :].reshape(channels, channels)
                forward_ref[spot(b), spot(3 * c + a)] = matrix
                backward_ref[spot(b), spot(3 * c + a)] = matrix.T


def conv_kernel(own_ref, low_ref, high_ref, forward_ref, backward_ref, send_ref, cells_ref, wide_ref, *, depth):
    count, span, height = own_ref.shape
    rows = span // (2 * depth + 1)
    block = rows * depth
    channels = count * rows
    side = height // 2
    right = lax.rem(lax.axis_index("ch"), 2)

    def spot(index):
        return slice(index * channels, (index + 1) * channels)

    lane = lanes((channels, height))
    early = lane < side
    within = lane % side

    def edge_of(ref, start):
        return ref[:, start : start + rows, :].astype(F32).reshape(channels, height)

    own_edge, low_edge, high_edge = edge_of(own_ref, block), edge_of(low_ref, 0), edge_of(high_ref, block)
    edges = (
        pltpu.roll(jnp.where(early, own_edge, low_edge), side, 1),
        own_edge,
        pltpu.roll(jnp.where(early, high_edge, own_edge), side, 1),
    )
    planes = (
        low_ref[:, rows : rows + block, :],
        own_ref[:, 0:block, :],
        own_ref[:, block + rows : 2 * block + rows, :],
        high_ref[:, 0:block, :],
    )
    for at, values in enumerate(planes):
        wide_ref[at] = values.astype(F32).reshape(channels * depth, height)

    for c in range(3):
        for tensor in range(2):
            direction = 1 - 2 * tensor
            outside = 0 if direction * (c - 1) < 0 else depth - 1
            if c != 1:
                cells_ref[tensor, 3 * c * channels : 3 * (c + 1) * channels, outside * height : (outside + 1) * height] = (
                    jnp.zeros((3 * channels, height), BF16)
                )
            for a in range(3):
                edge = edges[1 + direction * (a - 1)]
                shift = 8 * tensor + direction * (c - 1)
                source = within + direction * (c - 1)
                inside = (within < depth) & (source >= 0) & (source < depth)
                moved = pltpu.roll(edge, -shift % height, 1)
                cells_ref[tensor, spot(3 * c + a), depth * height :] = jnp.where(inside, moved, 0.0).astype(BF16)
    for z in range(depth):
        pieces = [wide_ref[at, pl.ds(z, channels, stride=depth), :] for at in range(4)]
        for step in range(3):
            for tensor, values in enumerate(both_planes(pieces[step], pieces[step + 1], early, side)):
                direction = 1 - 2 * tensor
                a = 1 + direction * (step - 1)
                values = values.astype(BF16)
                for c in range(3):
                    target = z - direction * (c - 1)
                    if 0 <= target < depth:
                        cells_ref[tensor, spot(3 * c + a), target * height : (target + 1) * height] = values

    for tensor in range(2):
        direction = 1 - 2 * tensor
        filters = (forward_ref, backward_ref)[tensor][...]
        sums = jnp.dot(filters, cells_ref[tensor], preferred_element_type=F32)
        beyond = sums[:, depth * height :]
        beyond = jnp.where(right == 1, beyond[spot(1 - direction)], beyond[spot(1 + direction)])
        border = jnp.where(right == 1, 0, side - 1)
        for z in range(depth):
            columns = slice(z * height, (z + 1) * height)
            before, middle, after = (sums[spot(b), columns] for b in (1 - direction, 1, 1 + direction))
            before = jnp.where(within == 0, 0.0, pltpu.roll(before, 1, 1))
            after = jnp.where(within == side - 1, 0.0, pltpu.roll(after, height - 1, 1))
            extra = jnp.where(within == border, pltpu.roll(beyond, border + (height - z), 1), 0.0)
            wide_ref[tensor, pl.ds(z, channels, stride=depth), :] = before + middle + after + extra
        result = wide_ref[tensor].astype(BF16).reshape(count, block, height)
        send_ref[:, tensor * block : (tensor + 1) * block, :] = result


def both_planes(first, second, early, side):
    turned_first, turned_second = pltpu.roll(first, side, 1), pltpu.roll(second, side, 1)
    return jnp.where(early, first, turned_second), jnp.where(early, turned_first, second)


def unpack_kernel(got_ref, features_ref, gradient_ref):
    core = lax.rem(lax.axis_index("gx"), 2)
    count, _, height = got_ref.shape
    rows, _, depth, _ = features_ref.shape
    block = rows * depth
    for level in range(count // 2):
        pair = pair_of(level, core, count)
        for tensor, ref in enumerate((features_ref, gradient_ref)):
            start = tensor * block
            halves = [got_ref[2 * level + side, start : start + block, :].astype(F32) for side in range(2)]
            for plane, values in enumerate(both(*halves)):
                ref[:, 2 * pair + plane] = values.astype(BF16).reshape(rows, depth, height)


def local(slabs, count, activations, conv_weight, out_grad):
    rows, _, depth, height = activations.shape
    taps, channels, _ = conv_weight.shape
    block = rows * depth
    span = 2 * block + rows
    shared = quarter(taps, 0)[1]
    pairs = count // 2
    send = pl.pallas_call(
        pack_kernel,
        out_shape=jax.ShapeDtypeStruct((count, span + shared * rows, height), BF16),
        in_specs=[HBM, HBM, HBM],
        out_specs=VMEM,
        scratch_shapes=[
            pltpu.VMEM(activations.shape, BF16),
            pltpu.VMEM(out_grad.shape, BF16),
            pltpu.VMEM((taps, rows, channels), BF16),
            pltpu.VMEM((block, height), F32),
            pltpu.SemaphoreType.DMA((3,)),
        ],
        compiler_params=PARAMS,
        name="pack",
    )(*(pltpu.with_memory_space_constraint(x, pltpu.HBM) for x in (activations, out_grad, jnp.swapaxes(conv_weight, 1, 2))))
    got = lax.all_to_all(send, "ch", 0, 0, tiled=True)
    own, own_filters = got[:, :span], got[:, span:]
    across_core, across_x = ([(slab, slab ^ step) for slab in range(slabs)] for step in (1, 2))
    x_filters = lax.ppermute(own_filters, "gx", across_x)
    core_filters = lax.ppermute(own_filters, "gx", across_core)
    diagonal_filters = lax.ppermute(x_filters, "gx", across_core)
    ring = []
    for side in range(2):
        order = [
            slab * count + 2 * pair_of(pair, slab % 2, count) + side for slab in range(slabs) for pair in range(pairs)
        ]
        ring += zip(order, order[1:] + order[:1])
    low = lax.ppermute(got[:, block:span], ("gx", "ch"), ring)
    high = lax.ppermute(got[:, : block + rows], ("gx", "ch"), [(to, at) for at, to in ring])
    forward, backward = pl.pallas_call(
        functools.partial(prepare_kernel, taps=taps),
        out_shape=[jax.ShapeDtypeStruct((3 * channels, 9 * channels), BF16)] * 2,
        in_specs=[VMEM, VMEM, VMEM, VMEM],
        out_specs=[VMEM, VMEM],
        scratch_shapes=[pltpu.VMEM((4, count, shared * rows, channels), BF16)],
        cost_estimate=pl.CostEstimate(flops=0, bytes_accessed=4 * 2**20, transcendentals=0),
        compiler_params=PARAMS,
        name="prepare",
    )(own_filters, core_filters, x_filters, diagonal_filters)
    result = pl.pallas_call(
        functools.partial(conv_kernel, depth=depth),
        out_shape=jax.ShapeDtypeStruct((count, 2 * block, height), BF16),
        in_specs=[VMEM, VMEM, VMEM, VMEM, VMEM],
        out_specs=VMEM,
        scratch_shapes=[
            pltpu.VMEM((2, 9 * channels, (depth + 1) * height), BF16),
            pltpu.VMEM((4, channels * depth, height), F32),
        ],
        compiler_params=PARAMS,
        name="conv",
    )(own, low, high, forward, backward)
    back = lax.all_to_all(result, "ch", 0, 0, tiled=True)
    return pl.pallas_call(
        unpack_kernel,
        out_shape=(jax.ShapeDtypeStruct(activations.shape, BF16), jax.ShapeDtypeStruct(out_grad.shape, BF16)),
        in_specs=[VMEM],
        out_specs=(VMEM, VMEM),
        compiler_params=PARAMS,
        name="unpack",
    )(back)


def solution(mesh):
    return jax.shard_map(
        functools.partial(local, mesh.shape["gx"], mesh.shape["ch"]),
        mesh=mesh,
        in_specs=(P("ch", "gx", None, None), P(None, None, "ch"), P("ch", "gx", None, None)),
        out_specs=(P("ch", "gx", None, None), P("ch", "gx", None, None)),
        check_vma=False,
    )
```

```python
import functools

import jax
import jax.numpy as jnp
from jax import lax
from jax.experimental import pallas as pl
from jax.experimental.pallas import tpu as pltpu
from jax.sharding import PartitionSpec as P


VMEM = pl.BlockSpec(memory_space=pltpu.VMEM)
HBM = pl.BlockSpec(memory_space=pltpu.HBM)
PARAMS = pltpu.CompilerParams(vmem_limit_bytes=16 * 2**20)
F32 = jnp.float32
BF16 = jnp.bfloat16


def lanes(shape):
    return lax.broadcasted_iota(jnp.int32, shape, len(shape) - 1)


def pair_of(level, core, count):
    return level + core * (count // 2 - 1 - 2 * level)


def share(taps, index):
    size = (taps + 7) // 8
    return (min(index * size, taps - size) if isinstance(index, int) else jnp.minimum(index * size, taps - size)), size


def share_of(slab):
    return lax.rem(slab, 4) + 4 * (slab // 8)


def flip(index, bits):
    for bit in (1, 2, 4):
        if bits & bit:
            index = index + bit - 2 * bit * lax.rem(index // bit, 2)
    return index


def both(first, second):
    size = first.shape[-1]
    early = lanes(first.shape) < size // 2
    turned_first, turned_second = (pltpu.roll(x, size // 2, x.ndim - 1) for x in (first, second))
    return jnp.where(early, first, turned_second), jnp.where(early, turned_first, second)


def pack_kernel(act_hbm, grad_hbm, weight_hbm, send_ref, act_ref, grad_ref, weight_ref, rows_ref, sems):
    copies = [
        pltpu.make_async_copy(source, target, sems.at[at])
        for at, (source, target) in enumerate(
            ((act_hbm, act_ref), (grad_hbm, grad_ref), (weight_hbm, weight_ref))
        )
    ]
    for copy in copies:
        copy.start()
    core = lax.rem(lax.axis_index("gx"), 2)
    count, (rows, _, depth, height) = send_ref.shape[0], act_ref.shape
    taps, _, fan = weight_ref.shape
    block = rows * depth
    side = height // 2
    copies[0].wait()
    copies[1].wait()
    lane = lanes((rows, height))
    for level in range(count // 2):
        pair = pair_of(level, core, count)
        edges = [jnp.zeros((rows, height), F32) for _ in range(2)]
        for plane in range(2):
            maps = []
            for tensor, ref in enumerate((act_ref, grad_ref)):
                values = ref[:, 2 * pair + plane].reshape(block, height).astype(F32)
                maps.append(values)
                rows_ref[...] = values
                for z in range(depth):
                    column = rows_ref[pl.ds(z, rows, stride=depth), :]
                    spot = side * plane + 8 * tensor + z
                    for half in range(2):
                        edge = side - half
                        turned = pltpu.roll(column, (spot - edge) % height, 1)
                        edges[half] = jnp.where(lane == spot, turned, edges[half])
            start = plane * (block + rows)
            for half, values in enumerate(both(*maps)):
                send_ref[2 * level + half, start : start + block, :] = values.astype(BF16)
        for half in range(2):
            send_ref[2 * level + half, block : block + rows, :] = edges[half].astype(BF16)
    copies[2].wait()
    first, shared = share(taps, share_of(lax.axis_index("gx")))
    filters = weight_ref[pl.ds(first, shared)].reshape(shared * rows, fan)
    for chip in range(count):
        send_ref[chip, 2 * block + rows :, :] = filters


def prepare_kernel(own_ref, core_ref, near_ref, across_ref, forward_ref, backward_ref, filters_ref, *, taps):
    count, _, channels = own_ref.shape
    rows = channels // count
    mine = share_of(lax.axis_index("gx"))
    filters_ref[mine] = own_ref[...]
    filters_ref[flip(mine, 1)] = core_ref[...]
    for at, step in enumerate((2, 4, 6)):
        there = flip(mine, step)
        filters_ref[there] = near_ref[at * count : (at + 1) * count]
        filters_ref[flip(there, 1)] = across_ref[at * count : (at + 1) * count]

    def spot(index):
        return slice(index * channels, (index + 1) * channels)

    for a in range(3):
        for b in range(3):
            for c in range(3):
                tap = 9 * a + 3 * b + c
                part = tap // share(taps, 0)[1]
                at = tap - share(taps, part)[0]
                matrix = filters_ref[part, :, at * rows : (at + 1) * rows, :].reshape(channels, channels)
                forward_ref[spot(b), spot(3 * c + a)] = matrix
                backward_ref[spot(b), spot(3 * c + a)] = matrix.T


def conv_kernel(own_ref, low_ref, high_ref, forward_ref, backward_ref, send_ref, cells_ref, wide_ref, *, depth):
    count, span, height = own_ref.shape
    rows = span // (2 * depth + 1)
    block = rows * depth
    channels = count * rows
    side = height // 2
    right = lax.rem(lax.axis_index("ch"), 2)

    def spot(index):
        return slice(index * channels, (index + 1) * channels)

    lane = lanes((channels, height))
    early = lane < side
    within = lane % side

    def edge_of(ref, start):
        return ref[:, start : start + rows, :].astype(F32).reshape(channels, height)

    own_edge, low_edge, high_edge = edge_of(own_ref, block), edge_of(low_ref, 0), edge_of(high_ref, block)
    edges = (
        pltpu.roll(jnp.where(early, own_edge, low_edge), side, 1),
        own_edge,
        pltpu.roll(jnp.where(early, high_edge, own_edge), side, 1),
    )
    planes = (
        low_ref[:, rows : rows + block, :],
        own_ref[:, 0:block, :],
        own_ref[:, block + rows : 2 * block + rows, :],
        high_ref[:, 0:block, :],
    )
    for at, values in enumerate(planes):
        wide_ref[at] = values.astype(F32).reshape(channels * depth, height)

    for c in range(3):
        for tensor in range(2):
            direction = 1 - 2 * tensor
            outside = 0 if direction * (c - 1) < 0 else depth - 1
            if c != 1:
                cells_ref[tensor, 3 * c * channels : 3 * (c + 1) * channels, outside * height : (outside + 1) * height] = (
                    jnp.zeros((3 * channels, height), BF16)
                )
            for a in range(3):
                edge = edges[1 + direction * (a - 1)]
                shift = 8 * tensor + direction * (c - 1)
                source = within + direction * (c - 1)
                inside = (within < depth) & (source >= 0) & (source < depth)
                moved = pltpu.roll(edge, -shift % height, 1)
                cells_ref[tensor, spot(3 * c + a), depth * height :] = jnp.where(inside, moved, 0.0).astype(BF16)
    for z in range(depth):
        pieces = [wide_ref[at, pl.ds(z, channels, stride=depth), :] for at in range(4)]
        for step in range(3):
            for tensor, values in enumerate(both_planes(pieces[step], pieces[step + 1], early, side)):
                direction = 1 - 2 * tensor
                a = 1 + direction * (step - 1)
                values = values.astype(BF16)
                for c in range(3):
                    target = z - direction * (c - 1)
                    if 0 <= target < depth:
                        cells_ref[tensor, spot(3 * c + a), target * height : (target + 1) * height] = values

    for tensor in range(2):
        direction = 1 - 2 * tensor
        filters = (forward_ref, backward_ref)[tensor][...]
        sums = jnp.dot(filters, cells_ref[tensor], preferred_element_type=F32)
        beyond = sums[:, depth * height :]
        beyond = jnp.where(right == 1, beyond[spot(1 - direction)], beyond[spot(1 + direction)])
        border = jnp.where(right == 1, 0, side - 1)
        for z in range(depth):
            columns = slice(z * height, (z + 1) * height)
            before, middle, after = (sums[spot(b), columns] for b in (1 - direction, 1, 1 + direction))
            before = jnp.where(within == 0, 0.0, pltpu.roll(before, 1, 1))
            after = jnp.where(within == side - 1, 0.0, pltpu.roll(after, height - 1, 1))
            extra = jnp.where(within == border, pltpu.roll(beyond, border + (height - z), 1), 0.0)
            wide_ref[tensor, pl.ds(z, channels, stride=depth), :] = before + middle + after + extra
        result = wide_ref[tensor].astype(BF16).reshape(count, block, height)
        send_ref[:, tensor * block : (tensor + 1) * block, :] = result


def both_planes(first, second, early, side):
    turned_first, turned_second = pltpu.roll(first, side, 1), pltpu.roll(second, side, 1)
    return jnp.where(early, first, turned_second), jnp.where(early, turned_first, second)


def unpack_kernel(got_ref, features_ref, gradient_ref):
    core = lax.rem(lax.axis_index("gx"), 2)
    count, _, height = got_ref.shape
    rows, _, depth, _ = features_ref.shape
    block = rows * depth
    for level in range(count // 2):
        pair = pair_of(level, core, count)
        for tensor, ref in enumerate((features_ref, gradient_ref)):
            start = tensor * block
            halves = [got_ref[2 * level + side, start : start + block, :].astype(F32) for side in range(2)]
            for plane, values in enumerate(both(*halves)):
                ref[:, 2 * pair + plane] = values.astype(BF16).reshape(rows, depth, height)


def local(slabs, count, activations, conv_weight, out_grad):
    rows, _, depth, height = activations.shape
    taps, channels, _ = conv_weight.shape
    block = rows * depth
    span = 2 * block + rows
    shared = share(taps, 0)[1]
    pairs = count // 2
    send = pl.pallas_call(
        pack_kernel,
        out_shape=jax.ShapeDtypeStruct((count, span + shared * rows, height), BF16),
        in_specs=[HBM, HBM, HBM],
        out_specs=VMEM,
        scratch_shapes=[
            pltpu.VMEM(activations.shape, BF16),
            pltpu.VMEM(out_grad.shape, BF16),
            pltpu.VMEM((taps, rows, channels), BF16),
            pltpu.VMEM((block, height), F32),
            pltpu.SemaphoreType.DMA((3,)),
        ],
        compiler_params=PARAMS,
        name="pack",
    )(*(pltpu.with_memory_space_constraint(x, pltpu.HBM) for x in (activations, out_grad, jnp.swapaxes(conv_weight, 1, 2))))
    got = lax.all_to_all(send, "ch", 0, 0, tiled=True)
    own, own_filters = got[:, :span], got[:, span:]
    across_core, *pairs_near = ([(slab, slab ^ step) for slab in range(slabs)] for step in (1, 2, 8, 10))
    near_filters = []
    for route in pairs_near:
        near_filters.append(lax.ppermute(own_filters, "gx", route))
    near_filters = jnp.concatenate(near_filters)
    core_filters = lax.ppermute(own_filters, "gx", across_core)
    diagonal_filters = lax.ppermute(near_filters, "gx", across_core)
    ring = []
    for side in range(2):
        order = [
            slab * count + 2 * pair_of(pair, slab % 2, count) + side for slab in range(slabs) for pair in range(pairs)
        ]
        ring += zip(order, order[1:] + order[:1])
    low = lax.ppermute(got[:, block:span], ("gx", "ch"), ring)
    high = lax.ppermute(got[:, : block + rows], ("gx", "ch"), [(to, at) for at, to in ring])
    forward, backward = pl.pallas_call(
        functools.partial(prepare_kernel, taps=taps),
        out_shape=[jax.ShapeDtypeStruct((3 * channels, 9 * channels), BF16)] * 2,
        in_specs=[VMEM, VMEM, VMEM, VMEM],
        out_specs=[VMEM, VMEM],
        scratch_shapes=[pltpu.VMEM((8, count, shared * rows, channels), BF16)],
        cost_estimate=pl.CostEstimate(flops=0, bytes_accessed=4 * 2**20, transcendentals=0),
        compiler_params=PARAMS,
        name="prepare",
    )(own_filters, core_filters, near_filters, diagonal_filters)
    result = pl.pallas_call(
        functools.partial(conv_kernel, depth=depth),
        out_shape=jax.ShapeDtypeStruct((count, 2 * block, height), BF16),
        in_specs=[VMEM, VMEM, VMEM, VMEM, VMEM],
        out_specs=VMEM,
        scratch_shapes=[
            pltpu.VMEM((2, 9 * channels, (depth + 1) * height), BF16),
            pltpu.VMEM((4, channels * depth, height), F32),
        ],
        compiler_params=PARAMS,
        name="conv",
    )(own, low, high, forward, backward)
    back = lax.all_to_all(result, "ch", 0, 0, tiled=True)
    return pl.pallas_call(
        unpack_kernel,
        out_shape=(jax.ShapeDtypeStruct(activations.shape, BF16), jax.ShapeDtypeStruct(out_grad.shape, BF16)),
        in_specs=[VMEM],
        out_specs=(VMEM, VMEM),
        compiler_params=PARAMS,
        name="unpack",
    )(back)


def solution(mesh):
    return jax.shard_map(
        functools.partial(local, mesh.shape["gx"], mesh.shape["ch"]),
        mesh=mesh,
        in_specs=(P("ch", "gx", None, None), P(None, None, "ch"), P("ch", "gx", None, None)),
        out_specs=(P("ch", "gx", None, None), P("ch", "gx", None, None)),
        check_vma=False,
    )
```

```python
import functools

import jax
import jax.numpy as jnp
from jax import lax
from jax.experimental import pallas as pl
from jax.experimental.pallas import tpu as pltpu
from jax.sharding import PartitionSpec as P


VMEM = pl.BlockSpec(memory_space=pltpu.VMEM)
HBM = pl.BlockSpec(memory_space=pltpu.HBM)
PARAMS = pltpu.CompilerParams(vmem_limit_bytes=16 * 2**20)
F32 = jnp.float32
BF16 = jnp.bfloat16


def lanes(shape):
    return lax.broadcasted_iota(jnp.int32, shape, len(shape) - 1)


def pair_of(level, core, count):
    return level + core * (count // 2 - 1 - 2 * level)


GROUPS = ((0, 4), (15, 3))


def place_of(slab):
    core, x, y = lax.rem(slab, 2), lax.rem(slab // 2, 2), slab // 8
    return core, (x, y)


def both(first, second):
    size = first.shape[-1]
    early = lanes(first.shape) < size // 2
    turned_first, turned_second = (pltpu.roll(x, size // 2, x.ndim - 1) for x in (first, second))
    return jnp.where(early, first, turned_second), jnp.where(early, turned_first, second)


def pack_kernel(act_hbm, grad_hbm, weight_hbm, send_ref, act_ref, grad_ref, weight_ref, rows_ref, sems):
    copies = [
        pltpu.make_async_copy(source, target, sems.at[at])
        for at, (source, target) in enumerate(
            ((act_hbm, act_ref), (grad_hbm, grad_ref), (weight_hbm, weight_ref))
        )
    ]
    for copy in copies:
        copy.start()
    core = lax.rem(lax.axis_index("gx"), 2)
    count, (rows, _, depth, height) = send_ref.shape[0], act_ref.shape
    _, _, fan = weight_ref.shape
    block = rows * depth
    side = height // 2
    copies[0].wait()
    copies[1].wait()
    lane = lanes((rows, height))
    for level in range(count // 2):
        pair = pair_of(level, core, count)
        edges = [jnp.zeros((rows, height), F32) for _ in range(2)]
        for plane in range(2):
            maps = []
            for tensor, ref in enumerate((act_ref, grad_ref)):
                values = ref[:, 2 * pair + plane].reshape(block, height).astype(F32)
                maps.append(values)
                rows_ref[...] = values
                for z in range(depth):
                    column = rows_ref[pl.ds(z, rows, stride=depth), :]
                    spot = side * plane + 8 * tensor + z
                    for half in range(2):
                        edge = side - half
                        turned = pltpu.roll(column, (spot - edge) % height, 1)
                        edges[half] = jnp.where(lane == spot, turned, edges[half])
            start = plane * (block + rows)
            for half, values in enumerate(both(*maps)):
                send_ref[2 * level + half, start : start + block, :] = values.astype(BF16)
        for half in range(2):
            send_ref[2 * level + half, block : block + rows, :] = edges[half].astype(BF16)
    copies[2].wait()
    start = 2 * block + rows
    for (first, size), place in zip(GROUPS, place_of(lax.axis_index("gx"))[1]):
        filters = weight_ref[pl.ds(first + size * (core + 2 * place), size)].reshape(size * rows, fan)
        for chip in range(count):
            send_ref[chip, start : start + size * rows, :] = filters
        start += size * rows


def prepare_kernel(own_ref, core_ref, x_ref, y_ref, diagonal_ref, forward_ref, backward_ref, *filters_refs):
    count, _, channels = own_ref.shape
    rows = channels // count
    core, places = place_of(lax.axis_index("gx"))
    start = 0
    for (_, size), place, filters_ref, near_ref in zip(GROUPS, places, filters_refs, (x_ref, y_ref)):
        span = slice(start, start + size * rows)
        filters_ref[2 * place + core] = own_ref[:, span, :]
        filters_ref[2 * place + 1 - core] = core_ref[:, span, :]
        filters_ref[2 - 2 * place + core] = near_ref[...]
        filters_ref[3 - 2 * place - core] = diagonal_ref[:, span, :]
        start += size * rows

    def spot(index):
        return slice(index * channels, (index + 1) * channels)

    for a in range(3):
        for b in range(3):
            for c in range(3):
                tap = 9 * a + 3 * b + c
                group = 0 if tap < GROUPS[1][0] else 1
                part, at = divmod(tap - GROUPS[group][0], GROUPS[group][1])
                matrix = filters_refs[group][part, :, at * rows : (at + 1) * rows, :].reshape(channels, channels)
                forward_ref[spot(b), spot(3 * c + a)] = matrix
                backward_ref[spot(b), spot(3 * c + a)] = matrix.T


def conv_kernel(own_ref, low_ref, high_ref, forward_ref, backward_ref, send_ref,
                forward_cells_ref, backward_cells_ref, wide_ref, *, depth):
    count, span, height = own_ref.shape
    rows = span // (2 * depth + 1)
    block = rows * depth
    channels = count * rows
    side = height // 2
    right = lax.rem(lax.axis_index("ch"), 2)
    cells_refs = (forward_cells_ref, backward_cells_ref)

    def spot(index):
        return slice(index * channels, (index + 1) * channels)

    lane = lanes((channels, height))
    early = lane < side
    within = lane % side

    def edge_of(ref, start):
        return ref[:, start : start + rows, :].astype(F32).reshape(channels, height)

    own_edge, low_edge, high_edge = edge_of(own_ref, block), edge_of(low_ref, 0), edge_of(high_ref, block)
    edges = (
        pltpu.roll(jnp.where(early, own_edge, low_edge), side, 1),
        own_edge,
        pltpu.roll(jnp.where(early, high_edge, own_edge), side, 1),
    )
    planes = (
        low_ref[:, rows : rows + block, :],
        own_ref[:, 0:block, :],
        own_ref[:, block + rows : 2 * block + rows, :],
        high_ref[:, 0:block, :],
    )
    for at, values in enumerate(planes):
        wide_ref[at] = values.astype(F32).reshape(channels * depth, height)

    for c in range(3):
        for tensor in range(2):
            direction = 1 - 2 * tensor
            outside = 0 if direction * (c - 1) < 0 else depth - 1
            if c != 1:
                cells_refs[tensor][3 * c * channels : 3 * (c + 1) * channels, outside * height : (outside + 1) * height] = (
                    jnp.zeros((3 * channels, height), BF16)
                )
            for a in range(3):
                edge = edges[1 + direction * (a - 1)]
                shift = 8 * tensor + direction * (c - 1)
                source = within + direction * (c - 1)
                inside = (within < depth) & (source >= 0) & (source < depth)
                moved = pltpu.roll(edge, -shift % height, 1)
                cells_refs[tensor][spot(3 * c + a), depth * height :] = jnp.where(inside, moved, 0.0).astype(BF16)
    for z in range(depth):
        pieces = [wide_ref[at, pl.ds(z, channels, stride=depth), :] for at in range(4)]
        for step in range(3):
            for tensor, values in enumerate(both_planes(pieces[step], pieces[step + 1], early, side)):
                direction = 1 - 2 * tensor
                a = 1 + direction * (step - 1)
                values = values.astype(BF16)
                for c in range(3):
                    target = z - direction * (c - 1)
                    if 0 <= target < depth:
                        cells_refs[tensor][spot(3 * c + a), target * height : (target + 1) * height] = values

    for tensor in range(2):
        direction = 1 - 2 * tensor
        filters_ref = (forward_ref, backward_ref)[tensor]
        sums = jnp.dot(filters_ref[...], cells_refs[tensor][:, : depth * height], preferred_element_type=F32)
        b = pl.multiple_of((1 + direction - 2 * direction * right) * channels, channels)
        beyond = jnp.dot(filters_ref[pl.ds(b, channels), :], cells_refs[tensor][:, depth * height :],
                         preferred_element_type=F32)
        border = jnp.where(right == 1, 0, side - 1)
        for z in range(depth):
            columns = slice(z * height, (z + 1) * height)
            before, middle, after = (sums[spot(b), columns] for b in (1 - direction, 1, 1 + direction))
            before = jnp.where(within == 0, 0.0, pltpu.roll(before, 1, 1))
            after = jnp.where(within == side - 1, 0.0, pltpu.roll(after, height - 1, 1))
            extra = jnp.where(within == border, pltpu.roll(beyond, border + (height - z), 1), 0.0)
            wide_ref[tensor, pl.ds(z, channels, stride=depth), :] = before + middle + after + extra
        result = wide_ref[tensor].astype(BF16).reshape(count, block, height)
        send_ref[:, tensor * block : (tensor + 1) * block, :] = result


def both_planes(first, second, early, side):
    turned_first, turned_second = pltpu.roll(first, side, 1), pltpu.roll(second, side, 1)
    return jnp.where(early, first, turned_second), jnp.where(early, turned_first, second)


def unpack_kernel(got_ref, features_ref, gradient_ref):
    core = lax.rem(lax.axis_index("gx"), 2)
    count, _, height = got_ref.shape
    rows, _, depth, _ = features_ref.shape
    block = rows * depth
    for level in range(count // 2):
        pair = pair_of(level, core, count)
        for tensor, ref in enumerate((features_ref, gradient_ref)):
            start = tensor * block
            halves = [got_ref[2 * level + side, start : start + block, :].astype(F32) for side in range(2)]
            for plane, values in enumerate(both(*halves)):
                ref[:, 2 * pair + plane] = values.astype(BF16).reshape(rows, depth, height)


def local(slabs, count, activations, conv_weight, out_grad):
    rows, _, depth, height = activations.shape
    taps, channels, _ = conv_weight.shape
    block = rows * depth
    span = 2 * block + rows
    sizes = [size * rows for _, size in GROUPS]
    shared = sum(sizes)
    pairs = count // 2
    send = pl.pallas_call(
        pack_kernel,
        out_shape=jax.ShapeDtypeStruct((count, span + shared, height), BF16),
        in_specs=[HBM, HBM, HBM],
        out_specs=VMEM,
        scratch_shapes=[
            pltpu.VMEM(activations.shape, BF16),
            pltpu.VMEM(out_grad.shape, BF16),
            pltpu.VMEM((taps, rows, channels), BF16),
            pltpu.VMEM((block, height), F32),
            pltpu.SemaphoreType.DMA((3,)),
        ],
        compiler_params=PARAMS,
        name="pack",
    )(*(pltpu.with_memory_space_constraint(x, pltpu.HBM) for x in (activations, out_grad, jnp.swapaxes(conv_weight, 1, 2))))
    got = lax.all_to_all(send, "ch", 0, 0, tiled=True)
    own, own_filters = got[:, :span], got[:, span:]
    across_core, across_x, across_y = ([(slab, slab ^ step) for slab in range(slabs)] for step in (1, 2, 8))
    x_filters = lax.ppermute(got[:, span : span + sizes[0]], "gx", across_x)
    y_filters = lax.ppermute(got[:, span + sizes[0] :], "gx", across_y)
    core_filters = lax.ppermute(own_filters, "gx", across_core)
    diagonal_filters = lax.ppermute(jnp.concatenate([x_filters, y_filters], axis=1), "gx", across_core)
    ring = []
    for side in range(2):
        order = [
            slab * count + 2 * pair_of(pair, slab % 2, count) + side for slab in range(slabs) for pair in range(pairs)
        ]
        ring += zip(order, order[1:] + order[:1])
    low = lax.ppermute(got[:, block:span], ("gx", "ch"), ring)
    high = lax.ppermute(got[:, : block + rows], ("gx", "ch"), [(to, at) for at, to in ring])
    forward, backward = pl.pallas_call(
        prepare_kernel,
        out_shape=[jax.ShapeDtypeStruct((3 * channels, 9 * channels), BF16)] * 2,
        in_specs=[VMEM] * 5,
        out_specs=[VMEM, VMEM],
        scratch_shapes=[pltpu.VMEM((4, count, size, channels), BF16) for size in sizes],
        cost_estimate=pl.CostEstimate(flops=0, bytes_accessed=4 * 2**20, transcendentals=0),
        compiler_params=PARAMS,
        name="prepare",
    )(own_filters, core_filters, x_filters, y_filters, diagonal_filters)
    result = pl.pallas_call(
        functools.partial(conv_kernel, depth=depth),
        out_shape=jax.ShapeDtypeStruct((count, 2 * block, height), BF16),
        in_specs=[VMEM, VMEM, VMEM, VMEM, VMEM],
        out_specs=VMEM,
        scratch_shapes=[
            pltpu.VMEM((9 * channels, (depth + 1) * height), BF16),
            pltpu.VMEM((9 * channels, (depth + 1) * height), BF16),
            pltpu.VMEM((4, channels * depth, height), F32),
        ],
        compiler_params=PARAMS,
        name="conv",
    )(own, low, high, forward, backward)
    back = lax.all_to_all(result, "ch", 0, 0, tiled=True)
    return pl.pallas_call(
        unpack_kernel,
        out_shape=(jax.ShapeDtypeStruct(activations.shape, BF16), jax.ShapeDtypeStruct(out_grad.shape, BF16)),
        in_specs=[VMEM],
        out_specs=(VMEM, VMEM),
        compiler_params=PARAMS,
        name="unpack",
    )(back)


def solution(mesh):
    return jax.shard_map(
        functools.partial(local, mesh.shape["gx"], mesh.shape["ch"]),
        mesh=mesh,
        in_specs=(P("ch", "gx", None, None), P(None, None, "ch"), P("ch", "gx", None, None)),
        out_specs=(P("ch", "gx", None, None), P("ch", "gx", None, None)),
        check_vma=False,
    )
```

```python
import functools

import jax
import jax.numpy as jnp
from jax import lax
from jax.experimental import pallas as pl
from jax.experimental.pallas import tpu as pltpu
from jax.sharding import PartitionSpec as P


VMEM = pl.BlockSpec(memory_space=pltpu.VMEM)
HBM = pl.BlockSpec(memory_space=pltpu.HBM)
PARAMS = pltpu.CompilerParams(vmem_limit_bytes=16 * 2**20)
F32 = jnp.float32
BF16 = jnp.bfloat16


def lanes(shape):
    return lax.broadcasted_iota(jnp.int32, shape, len(shape) - 1)


def pair_of(level, core, count):
    return level + core * (count // 2 - 1 - 2 * level)


def pieces(taps):
    return (0, taps // 2), (taps + 3) // 4


def places_of(slab):
    core, x, y = lax.rem(slab, 2), lax.rem(slab // 2, 2), slab // 8
    return core, y + core * (x - y), x + core * (y - x)


def both(first, second):
    size = first.shape[-1]
    early = lanes(first.shape) < size // 2
    turned_first, turned_second = (pltpu.roll(x, size // 2, x.ndim - 1) for x in (first, second))
    return jnp.where(early, first, turned_second), jnp.where(early, turned_first, second)


def pack_kernel(act_hbm, grad_hbm, weight_hbm, send_ref, act_ref, grad_ref, weight_ref, rows_ref, sems):
    copies = [
        pltpu.make_async_copy(source, target, sems.at[at])
        for at, (source, target) in enumerate(
            ((act_hbm, act_ref), (grad_hbm, grad_ref), (weight_hbm, weight_ref))
        )
    ]
    for copy in copies:
        copy.start()
    core = lax.rem(lax.axis_index("gx"), 2)
    count, (rows, _, depth, height) = send_ref.shape[0], act_ref.shape
    taps, _, fan = weight_ref.shape
    block = rows * depth
    side = height // 2
    copies[0].wait()
    copies[1].wait()
    lane = lanes((rows, height))
    for level in range(count // 2):
        pair = pair_of(level, core, count)
        edges = [jnp.zeros((rows, height), F32) for _ in range(2)]
        for plane in range(2):
            maps = []
            for tensor, ref in enumerate((act_ref, grad_ref)):
                values = ref[:, 2 * pair + plane].reshape(block, height).astype(F32)
                maps.append(values)
                rows_ref[...] = values
                for z in range(depth):
                    column = rows_ref[pl.ds(z, rows, stride=depth), :]
                    spot = side * plane + 8 * tensor + z
                    for half in range(2):
                        edge = side - half
                        turned = pltpu.roll(column, (spot - edge) % height, 1)
                        edges[half] = jnp.where(lane == spot, turned, edges[half])
            start = plane * (block + rows)
            for half, values in enumerate(both(*maps)):
                send_ref[2 * level + half, start : start + block, :] = values.astype(BF16)
        for half in range(2):
            send_ref[2 * level + half, block : block + rows, :] = edges[half].astype(BF16)
    copies[2].wait()
    _, place, _ = places_of(lax.axis_index("gx"))
    (_, second), size = pieces(taps)
    filters = weight_ref[pl.ds(core * second + place * size, size)].reshape(size * rows, fan)
    for chip in range(count):
        send_ref[chip, 2 * block + rows :, :] = filters


def prepare_kernel(own_ref, core_ref, near_ref, diagonal_ref, forward_ref, backward_ref, filters_ref, *, taps):
    count, _, channels = own_ref.shape
    rows = channels // count
    core, place, other = places_of(lax.axis_index("gx"))
    (_, second), size = pieces(taps)
    filters_ref[2 * core + place] = own_ref[...]
    filters_ref[2 * core + 1 - place] = near_ref[...]
    filters_ref[2 - 2 * core + other] = core_ref[...]
    filters_ref[3 - 2 * core - other] = diagonal_ref[...]

    def spot(index):
        return slice(index * channels, (index + 1) * channels)

    for a in range(3):
        for b in range(3):
            for c in range(3):
                tap = 9 * a + 3 * b + c
                half = 0 if tap < 2 * size else 1
                part, at = divmod(tap - half * second, size)
                matrix = filters_ref[2 * half + part, :, at * rows : (at + 1) * rows, :].reshape(channels, channels)
                forward_ref[spot(b), spot(3 * c + a)] = matrix
                backward_ref[spot(b), spot(3 * c + a)] = matrix.T


def conv_kernel(own_ref, low_ref, high_ref, forward_ref, backward_ref, send_ref,
                forward_cells_ref, backward_cells_ref, wide_ref, *, depth):
    count, span, height = own_ref.shape
    rows = span // (2 * depth + 1)
    block = rows * depth
    channels = count * rows
    side = height // 2
    right = lax.rem(lax.axis_index("ch"), 2)
    cells_refs = (forward_cells_ref, backward_cells_ref)

    def spot(index):
        return slice(index * channels, (index + 1) * channels)

    lane = lanes((channels, height))
    early = lane < side
    within = lane % side

    def edge_of(ref, start):
        return ref[:, start : start + rows, :].astype(F32).reshape(channels, height)

    own_edge, low_edge, high_edge = edge_of(own_ref, block), edge_of(low_ref, 0), edge_of(high_ref, block)
    edges = (
        pltpu.roll(jnp.where(early, own_edge, low_edge), side, 1),
        own_edge,
        pltpu.roll(jnp.where(early, high_edge, own_edge), side, 1),
    )
    planes = (
        low_ref[:, rows : rows + block, :],
        own_ref[:, 0:block, :],
        own_ref[:, block + rows : 2 * block + rows, :],
        high_ref[:, 0:block, :],
    )
    for at, values in enumerate(planes):
        wide_ref[at] = values.astype(F32).reshape(channels * depth, height)

    for c in range(3):
        for tensor in range(2):
            direction = 1 - 2 * tensor
            outside = 0 if direction * (c - 1) < 0 else depth - 1
            if c != 1:
                cells_refs[tensor][3 * c * channels : 3 * (c + 1) * channels, outside * height : (outside + 1) * height] = (
                    jnp.zeros((3 * channels, height), BF16)
                )
            for a in range(3):
                edge = edges[1 + direction * (a - 1)]
                shift = 8 * tensor + direction * (c - 1)
                source = within + direction * (c - 1)
                inside = (within < depth) & (source >= 0) & (source < depth)
                moved = pltpu.roll(edge, -shift % height, 1)
                cells_refs[tensor][spot(3 * c + a), depth * height :] = jnp.where(inside, moved, 0.0).astype(BF16)
    for z in range(depth):
        pieces = [wide_ref[at, pl.ds(z, channels, stride=depth), :] for at in range(4)]
        for step in range(3):
            for tensor, values in enumerate(both_planes(pieces[step], pieces[step + 1], early, side)):
                direction = 1 - 2 * tensor
                a = 1 + direction * (step - 1)
                values = values.astype(BF16)
                for c in range(3):
                    target = z - direction * (c - 1)
                    if 0 <= target < depth:
                        cells_refs[tensor][spot(3 * c + a), target * height : (target + 1) * height] = values

    for tensor in range(2):
        direction = 1 - 2 * tensor
        filters_ref = (forward_ref, backward_ref)[tensor]
        sums = jnp.dot(filters_ref[...], cells_refs[tensor][:, : depth * height], preferred_element_type=F32)
        b = pl.multiple_of((1 + direction - 2 * direction * right) * channels, channels)
        beyond = jnp.dot(filters_ref[pl.ds(b, channels), :], cells_refs[tensor][:, depth * height :],
                         preferred_element_type=F32)
        border = jnp.where(right == 1, 0, side - 1)
        for z in range(depth):
            columns = slice(z * height, (z + 1) * height)
            before, middle, after = (sums[spot(b), columns] for b in (1 - direction, 1, 1 + direction))
            before = jnp.where(within == 0, 0.0, pltpu.roll(before, 1, 1))
            after = jnp.where(within == side - 1, 0.0, pltpu.roll(after, height - 1, 1))
            extra = jnp.where(within == border, pltpu.roll(beyond, border + (height - z), 1), 0.0)
            wide_ref[tensor, pl.ds(z, channels, stride=depth), :] = before + middle + after + extra
        result = wide_ref[tensor].astype(BF16).reshape(count, block, height)
        send_ref[:, tensor * block : (tensor + 1) * block, :] = result


def both_planes(first, second, early, side):
    turned_first, turned_second = pltpu.roll(first, side, 1), pltpu.roll(second, side, 1)
    return jnp.where(early, first, turned_second), jnp.where(early, turned_first, second)


def unpack_kernel(got_ref, features_ref, gradient_ref):
    core = lax.rem(lax.axis_index("gx"), 2)
    count, _, height = got_ref.shape
    rows, _, depth, _ = features_ref.shape
    block = rows * depth
    for level in range(count // 2):
        pair = pair_of(level, core, count)
        for tensor, ref in enumerate((features_ref, gradient_ref)):
            start = tensor * block
            halves = [got_ref[2 * level + side, start : start + block, :].astype(F32) for side in range(2)]
            for plane, values in enumerate(both(*halves)):
                ref[:, 2 * pair + plane] = values.astype(BF16).reshape(rows, depth, height)


def local(slabs, count, activations, conv_weight, out_grad):
    rows, _, depth, height = activations.shape
    taps, channels, _ = conv_weight.shape
    block = rows * depth
    span = 2 * block + rows
    shared = pieces(taps)[1] * rows
    pairs = count // 2
    send = pl.pallas_call(
        pack_kernel,
        out_shape=jax.ShapeDtypeStruct((count, span + shared, height), BF16),
        in_specs=[HBM, HBM, HBM],
        out_specs=VMEM,
        scratch_shapes=[
            pltpu.VMEM(activations.shape, BF16),
            pltpu.VMEM(out_grad.shape, BF16),
            pltpu.VMEM((taps, rows, channels), BF16),
            pltpu.VMEM((block, height), F32),
            pltpu.SemaphoreType.DMA((3,)),
        ],
        compiler_params=PARAMS,
        name="pack",
    )(*(pltpu.with_memory_space_constraint(x, pltpu.HBM) for x in (activations, out_grad, jnp.swapaxes(conv_weight, 1, 2))))
    got = lax.all_to_all(send, "ch", 0, 0, tiled=True)
    own, own_filters = got[:, :span], got[:, span:]
    across_core = [(slab, slab ^ 1) for slab in range(slabs)]
    across = [(slab, slab ^ (2 if slab % 2 else 8)) for slab in range(slabs)]
    near_filters = lax.ppermute(own_filters, "gx", across)
    core_filters = lax.ppermute(own_filters, "gx", across_core)
    diagonal_filters = lax.ppermute(near_filters, "gx", across_core)
    ring = []
    for side in range(2):
        order = [
            slab * count + 2 * pair_of(pair, slab % 2, count) + side for slab in range(slabs) for pair in range(pairs)
        ]
        ring += zip(order, order[1:] + order[:1])
    low = lax.ppermute(got[:, block:span], ("gx", "ch"), ring)
    high = lax.ppermute(got[:, : block + rows], ("gx", "ch"), [(to, at) for at, to in ring])
    forward, backward = pl.pallas_call(
        functools.partial(prepare_kernel, taps=taps),
        out_shape=[jax.ShapeDtypeStruct((3 * channels, 9 * channels), BF16)] * 2,
        in_specs=[VMEM] * 4,
        out_specs=[VMEM, VMEM],
        scratch_shapes=[pltpu.VMEM((4, count, shared, channels), BF16)],
        cost_estimate=pl.CostEstimate(flops=0, bytes_accessed=4 * 2**20, transcendentals=0),
        compiler_params=PARAMS,
        name="prepare",
    )(own_filters, core_filters, near_filters, diagonal_filters)
    result = pl.pallas_call(
        functools.partial(conv_kernel, depth=depth),
        out_shape=jax.ShapeDtypeStruct((count, 2 * block, height), BF16),
        in_specs=[VMEM, VMEM, VMEM, VMEM, VMEM],
        out_specs=VMEM,
        scratch_shapes=[
            pltpu.VMEM((9 * channels, (depth + 1) * height), BF16),
            pltpu.VMEM((9 * channels, (depth + 1) * height), BF16),
            pltpu.VMEM((4, channels * depth, height), F32),
        ],
        compiler_params=PARAMS,
        name="conv",
    )(own, low, high, forward, backward)
    back = lax.all_to_all(result, "ch", 0, 0, tiled=True)
    return pl.pallas_call(
        unpack_kernel,
        out_shape=(jax.ShapeDtypeStruct(activations.shape, BF16), jax.ShapeDtypeStruct(out_grad.shape, BF16)),
        in_specs=[VMEM],
        out_specs=(VMEM, VMEM),
        compiler_params=PARAMS,
        name="unpack",
    )(back)


def solution(mesh):
    return jax.shard_map(
        functools.partial(local, mesh.shape["gx"], mesh.shape["ch"]),
        mesh=mesh,
        in_specs=(P("ch", "gx", None, None), P(None, None, "ch"), P("ch", "gx", None, None)),
        out_specs=(P("ch", "gx", None, None), P("ch", "gx", None, None)),
        check_vma=False,
    )
```

```python
import functools

import jax
import jax.numpy as jnp
from jax import lax
from jax.experimental import pallas as pl
from jax.experimental.pallas import tpu as pltpu
from jax.sharding import Mesh, PartitionSpec as P


VMEM = pl.BlockSpec(memory_space=pltpu.VMEM)
HBM = pl.BlockSpec(memory_space=pltpu.HBM)
PARAMS = pltpu.CompilerParams(vmem_limit_bytes=16 * 2**20)
CH = ("level", "side")
F32 = jnp.float32
BF16 = jnp.bfloat16


def lanes(shape):
    return lax.broadcasted_iota(jnp.int32, shape, len(shape) - 1)


def pair_of(level, core, count):
    return level + core * (count // 2 - 1 - 2 * level)


def pieces(taps):
    return (0, taps // 2), (taps + 3) // 4


def places_of(slab):
    core, x, y = lax.rem(slab, 2), lax.rem(slab // 2, 2), slab // 8
    return core, y + core * (x - y), x + core * (y - x)


def turned(chip, count):
    return chip % 2 * (count // 2) + chip // 2


def both(first, second):
    size = first.shape[-1]
    early = lanes(first.shape) < size // 2
    turned_first, turned_second = (pltpu.roll(x, size // 2, x.ndim - 1) for x in (first, second))
    return jnp.where(early, first, turned_second), jnp.where(early, turned_first, second)


def pack_kernel(act_hbm, grad_hbm, weight_hbm, send_ref, act_ref, grad_ref, weight_ref, rows_ref, sems):
    copies = [
        pltpu.make_async_copy(source, target, sems.at[at])
        for at, (source, target) in enumerate(
            ((act_hbm, act_ref), (grad_hbm, grad_ref), (weight_hbm, weight_ref))
        )
    ]
    for copy in copies:
        copy.start()
    core = lax.rem(lax.axis_index("gx"), 2)
    count, (rows, _, depth, height) = send_ref.shape[0], act_ref.shape
    taps, _, fan = weight_ref.shape
    block = rows * depth
    side = height // 2
    copies[0].wait()
    copies[1].wait()
    lane = lanes((rows, height))
    for level in range(count // 2):
        pair = pair_of(level, core, count)
        edges = [jnp.zeros((rows, height), F32) for _ in range(2)]
        for plane in range(2):
            maps = []
            for tensor, ref in enumerate((act_ref, grad_ref)):
                values = ref[:, 2 * pair + plane].reshape(block, height).astype(F32)
                maps.append(values)
                rows_ref[...] = values
                for z in range(depth):
                    column = rows_ref[pl.ds(z, rows, stride=depth), :]
                    spot = side * plane + 8 * tensor + z
                    for half in range(2):
                        edge = side - half
                        turned = pltpu.roll(column, (spot - edge) % height, 1)
                        edges[half] = jnp.where(lane == spot, turned, edges[half])
            start = plane * (block + rows)
            for half, values in enumerate(both(*maps)):
                send_ref[2 * level + half, start : start + block, :] = values.astype(BF16)
        for half in range(2):
            send_ref[2 * level + half, block : block + rows, :] = edges[half].astype(BF16)
    copies[2].wait()
    _, place, _ = places_of(lax.axis_index("gx"))
    (_, second), size = pieces(taps)
    filters = weight_ref[pl.ds(core * second + place * size, size)].reshape(size * rows, fan)
    for chip in range(count):
        send_ref[chip, 2 * block + rows :, :] = filters


def prepare_kernel(own_ref, core_ref, near_ref, diagonal_ref, forward_ref, backward_ref, filters_ref, *, taps):
    count, _, channels = own_ref.shape
    rows = channels // count
    core, place, other = places_of(lax.axis_index("gx"))
    (_, second), size = pieces(taps)
    filters_ref[2 * core + place] = own_ref[...]
    filters_ref[2 * core + 1 - place] = near_ref[...]
    filters_ref[2 - 2 * core + other] = core_ref[...]
    filters_ref[3 - 2 * core - other] = diagonal_ref[...]

    def spot(index):
        return slice(index * channels, (index + 1) * channels)

    for a in range(3):
        for b in range(3):
            for c in range(3):
                tap = 9 * a + 3 * b + c
                half = 0 if tap < 2 * size else 1
                part, at = divmod(tap - half * second, size)
                matrix = filters_ref[2 * half + part, :, at * rows : (at + 1) * rows, :].reshape(channels, channels)
                forward_ref[spot(b), spot(3 * c + a)] = matrix
                backward_ref[spot(b), spot(3 * c + a)] = matrix.T


def conv_kernel(own_ref, low_ref, high_ref, forward_ref, backward_ref, send_ref,
                forward_cells_ref, backward_cells_ref, wide_ref, *, depth):
    count, span, height = own_ref.shape
    rows = span // (2 * depth + 1)
    block = rows * depth
    channels = count * rows
    side = height // 2
    right = lax.axis_index("side")
    cells_refs = (forward_cells_ref, backward_cells_ref)

    def spot(index):
        return slice(index * channels, (index + 1) * channels)

    lane = lanes((channels, height))
    early = lane < side
    within = lane % side

    def edge_of(ref, start):
        return ref[:, start : start + rows, :].astype(F32).reshape(channels, height)

    own_edge, low_edge, high_edge = edge_of(own_ref, block), edge_of(low_ref, 0), edge_of(high_ref, block)
    edges = (
        pltpu.roll(jnp.where(early, own_edge, low_edge), side, 1),
        own_edge,
        pltpu.roll(jnp.where(early, high_edge, own_edge), side, 1),
    )
    planes = (
        low_ref[:, rows : rows + block, :],
        own_ref[:, 0:block, :],
        own_ref[:, block + rows : 2 * block + rows, :],
        high_ref[:, 0:block, :],
    )
    for at, values in enumerate(planes):
        wide_ref[at] = values.astype(F32).reshape(channels * depth, height)

    for c in range(3):
        for tensor in range(2):
            direction = 1 - 2 * tensor
            outside = 0 if direction * (c - 1) < 0 else depth - 1
            if c != 1:
                cells_refs[tensor][3 * c * channels : 3 * (c + 1) * channels, outside * height : (outside + 1) * height] = (
                    jnp.zeros((3 * channels, height), BF16)
                )
            for a in range(3):
                edge = edges[1 + direction * (a - 1)]
                shift = 8 * tensor + direction * (c - 1)
                source = within + direction * (c - 1)
                inside = (within < depth) & (source >= 0) & (source < depth)
                moved = pltpu.roll(edge, -shift % height, 1)
                cells_refs[tensor][spot(3 * c + a), depth * height :] = jnp.where(inside, moved, 0.0).astype(BF16)
    for z in range(depth):
        pieces = [wide_ref[at, pl.ds(z, channels, stride=depth), :] for at in range(4)]
        for step in range(3):
            for tensor, values in enumerate(both_planes(pieces[step], pieces[step + 1], early, side)):
                direction = 1 - 2 * tensor
                a = 1 + direction * (step - 1)
                values = values.astype(BF16)
                for c in range(3):
                    target = z - direction * (c - 1)
                    if 0 <= target < depth:
                        cells_refs[tensor][spot(3 * c + a), target * height : (target + 1) * height] = values

    for tensor in range(2):
        direction = 1 - 2 * tensor
        filters_ref = (forward_ref, backward_ref)[tensor]
        sums = jnp.dot(filters_ref[...], cells_refs[tensor][:, : depth * height], preferred_element_type=F32)
        b = pl.multiple_of((1 + direction - 2 * direction * right) * channels, channels)
        beyond = jnp.dot(filters_ref[pl.ds(b, channels), :], cells_refs[tensor][:, depth * height :],
                         preferred_element_type=F32)
        border = jnp.where(right == 1, 0, side - 1)
        for z in range(depth):
            columns = slice(z * height, (z + 1) * height)
            before, middle, after = (sums[spot(b), columns] for b in (1 - direction, 1, 1 + direction))
            before = jnp.where(within == 0, 0.0, pltpu.roll(before, 1, 1))
            after = jnp.where(within == side - 1, 0.0, pltpu.roll(after, height - 1, 1))
            extra = jnp.where(within == border, pltpu.roll(beyond, border + (height - z), 1), 0.0)
            wide_ref[tensor, pl.ds(z, channels, stride=depth), :] = before + middle + after + extra
        for chip in range(count):
            result = wide_ref[tensor, chip * block : (chip + 1) * block, :].astype(BF16)
            send_ref[turned(chip, count), tensor * block : (tensor + 1) * block, :] = result


def both_planes(first, second, early, side):
    turned_first, turned_second = pltpu.roll(first, side, 1), pltpu.roll(second, side, 1)
    return jnp.where(early, first, turned_second), jnp.where(early, turned_first, second)


def unpack_kernel(got_ref, features_ref, gradient_ref):
    core = lax.rem(lax.axis_index("gx"), 2)
    count, _, height = got_ref.shape
    rows, _, depth, _ = features_ref.shape
    block = rows * depth
    for level in range(count // 2):
        pair = pair_of(level, core, count)
        for tensor, ref in enumerate((features_ref, gradient_ref)):
            start = tensor * block
            halves = [got_ref[turned(2 * level + side, count), start : start + block, :].astype(F32) for side in range(2)]
            for plane, values in enumerate(both(*halves)):
                ref[:, 2 * pair + plane] = values.astype(BF16).reshape(rows, depth, height)


def local(slabs, count, activations, conv_weight, out_grad):
    rows, _, depth, height = activations.shape
    taps, channels, _ = conv_weight.shape
    block = rows * depth
    span = 2 * block + rows
    shared = pieces(taps)[1] * rows
    pairs = count // 2
    send = pl.pallas_call(
        pack_kernel,
        out_shape=jax.ShapeDtypeStruct((count, span + shared, height), BF16),
        in_specs=[HBM, HBM, HBM],
        out_specs=VMEM,
        scratch_shapes=[
            pltpu.VMEM(activations.shape, BF16),
            pltpu.VMEM(out_grad.shape, BF16),
            pltpu.VMEM((taps, rows, channels), BF16),
            pltpu.VMEM((block, height), F32),
            pltpu.SemaphoreType.DMA((3,)),
        ],
        compiler_params=PARAMS,
        name="pack",
    )(*(pltpu.with_memory_space_constraint(x, pltpu.HBM) for x in (activations, out_grad, jnp.swapaxes(conv_weight, 1, 2))))
    got = lax.all_to_all(send, CH, 0, 0, tiled=True)
    own, own_filters = got[:, :span], got[:, span:]
    across_core = [(slab, slab ^ 1) for slab in range(slabs)]
    across = [(slab, slab ^ (2 if slab % 2 else 8)) for slab in range(slabs)]
    near_filters = lax.ppermute(own_filters, "gx", across)
    core_filters = lax.ppermute(own_filters, "gx", across_core)
    diagonal_filters = lax.ppermute(near_filters, "gx", across_core)
    ring = []
    for side in range(2):
        order = [
            slab * count + 2 * pair_of(pair, slab % 2, count) + side for slab in range(slabs) for pair in range(pairs)
        ]
        ring += zip(order, order[1:] + order[:1])
    low = lax.ppermute(got[:, block:span], ("gx", *CH), ring)
    high = lax.ppermute(got[:, : block + rows], ("gx", *CH), [(to, at) for at, to in ring])
    forward, backward = pl.pallas_call(
        functools.partial(prepare_kernel, taps=taps),
        out_shape=[jax.ShapeDtypeStruct((3 * channels, 9 * channels), BF16)] * 2,
        in_specs=[VMEM] * 4,
        out_specs=[VMEM, VMEM],
        scratch_shapes=[pltpu.VMEM((4, count, shared, channels), BF16)],
        cost_estimate=pl.CostEstimate(flops=0, bytes_accessed=4 * 2**20, transcendentals=0),
        compiler_params=PARAMS,
        name="prepare",
    )(own_filters, core_filters, near_filters, diagonal_filters)
    result = pl.pallas_call(
        functools.partial(conv_kernel, depth=depth),
        out_shape=jax.ShapeDtypeStruct((count, 2 * block, height), BF16),
        in_specs=[VMEM, VMEM, VMEM, VMEM, VMEM],
        out_specs=VMEM,
        scratch_shapes=[
            pltpu.VMEM((9 * channels, (depth + 1) * height), BF16),
            pltpu.VMEM((9 * channels, (depth + 1) * height), BF16),
            pltpu.VMEM((4, channels * depth, height), F32),
        ],
        compiler_params=PARAMS,
        name="conv",
    )(own, low, high, forward, backward)
    back = lax.all_to_all(result, CH[::-1], 0, 0, tiled=True)
    return pl.pallas_call(
        unpack_kernel,
        out_shape=(jax.ShapeDtypeStruct(activations.shape, BF16), jax.ShapeDtypeStruct(out_grad.shape, BF16)),
        in_specs=[VMEM],
        out_specs=(VMEM, VMEM),
        compiler_params=PARAMS,
        name="unpack",
    )(back)


def solution(mesh):
    slabs, count = mesh.shape["gx"], mesh.shape["ch"]
    mesh = Mesh(mesh.devices.reshape(slabs, count // 2, 2), ("gx", *CH))
    return jax.shard_map(
        functools.partial(local, slabs, count),
        mesh=mesh,
        in_specs=(P(CH, "gx", None, None), P(None, None, CH), P(CH, "gx", None, None)),
        out_specs=(P(CH, "gx", None, None), P(CH, "gx", None, None)),
        check_vma=False,
    )
```

```python
import functools

import jax
import jax.numpy as jnp
from jax import lax
from jax.experimental import pallas as pl
from jax.experimental.pallas import tpu as pltpu
from jax.sharding import Mesh, PartitionSpec as P


VMEM = pl.BlockSpec(memory_space=pltpu.VMEM)
HBM = pl.BlockSpec(memory_space=pltpu.HBM)
PARAMS = pltpu.CompilerParams(vmem_limit_bytes=16 * 2**20)
CH = ("level", "side")
F32 = jnp.float32
BF16 = jnp.bfloat16


def lanes(shape):
    return lax.broadcasted_iota(jnp.int32, shape, len(shape) - 1)


def pair_of(level, core, count):
    return level + core * (count // 2 - 1 - 2 * level)


def pieces(taps):
    return (0, taps // 2), (taps + 3) // 4


def places_of(slab):
    core, x, y = lax.rem(slab, 2), lax.rem(slab // 2, 2), slab // 8
    return core, y + core * (x - y), x + core * (y - x)


def rank_of(chip, count):
    return chip % 2 * (count // 2) + chip // 2


def both(first, second):
    size = first.shape[-1]
    early = lanes(first.shape) < size // 2
    turned_first, turned_second = (pltpu.roll(x, size // 2, x.ndim - 1) for x in (first, second))
    return jnp.where(early, first, turned_second), jnp.where(early, turned_first, second)


def pack_kernel(act_hbm, grad_hbm, weight_hbm, send_ref, act_ref, grad_ref, weight_ref, rows_ref, sems):
    copies = [
        pltpu.make_async_copy(source, target, sems.at[at])
        for at, (source, target) in enumerate(
            ((act_hbm, act_ref), (grad_hbm, grad_ref), (weight_hbm, weight_ref))
        )
    ]
    for copy in copies:
        copy.start()
    core = lax.rem(lax.axis_index("gx"), 2)
    count, (rows, _, depth, height) = send_ref.shape[0], act_ref.shape
    taps, _, fan = weight_ref.shape
    block = rows * depth
    side = height // 2
    copies[0].wait()
    copies[1].wait()
    lane = lanes((rows, height))
    for level in range(count // 2):
        pair = pair_of(level, core, count)
        edges = [jnp.zeros((rows, height), F32) for _ in range(2)]
        for plane in range(2):
            maps = []
            for tensor, ref in enumerate((act_ref, grad_ref)):
                values = ref[:, 2 * pair + plane].reshape(block, height).astype(F32)
                maps.append(values)
                rows_ref[...] = values
                for z in range(depth):
                    column = rows_ref[pl.ds(z, rows, stride=depth), :]
                    spot = side * plane + 8 * tensor + z
                    for half in range(2):
                        edge = side - half
                        turned = pltpu.roll(column, (spot - edge) % height, 1)
                        edges[half] = jnp.where(lane == spot, turned, edges[half])
            start = plane * (block + rows)
            for half, values in enumerate(both(*maps)):
                send_ref[rank_of(2 * level + half, count), start : start + block, :] = values.astype(BF16)
        for half in range(2):
            send_ref[rank_of(2 * level + half, count), block : block + rows, :] = edges[half].astype(BF16)
    copies[2].wait()
    _, place, _ = places_of(lax.axis_index("gx"))
    (_, second), size = pieces(taps)
    filters = weight_ref[pl.ds(core * second + place * size, size)].reshape(size * rows, fan)
    for chip in range(count):
        send_ref[chip, 2 * block + rows :, :] = filters


def prepare_kernel(own_ref, core_ref, near_ref, diagonal_ref, forward_ref, backward_ref, filters_ref, *, taps):
    count, _, channels = own_ref.shape
    rows = channels // count
    core, place, other = places_of(lax.axis_index("gx"))
    (_, second), size = pieces(taps)
    for chip in range(count):
        at = rank_of(chip, count)
        filters_ref[2 * core + place, chip] = own_ref[at]
        filters_ref[2 * core + 1 - place, chip] = near_ref[at]
        filters_ref[2 - 2 * core + other, chip] = core_ref[at]
        filters_ref[3 - 2 * core - other, chip] = diagonal_ref[at]

    def spot(index):
        return slice(index * channels, (index + 1) * channels)

    for a in range(3):
        for b in range(3):
            for c in range(3):
                tap = 9 * a + 3 * b + c
                half = 0 if tap < 2 * size else 1
                part, at = divmod(tap - half * second, size)
                matrix = filters_ref[2 * half + part, :, at * rows : (at + 1) * rows, :].reshape(channels, channels)
                forward_ref[spot(b), spot(3 * c + a)] = matrix
                backward_ref[spot(b), spot(3 * c + a)] = matrix.T


def conv_kernel(own_ref, low_ref, high_ref, forward_ref, backward_ref, send_ref,
                forward_cells_ref, backward_cells_ref, wide_ref, *, depth):
    count, span, height = own_ref.shape
    rows = span // (2 * depth + 1)
    block = rows * depth
    channels = count * rows
    side = height // 2
    right = lax.axis_index("side")
    cells_refs = (forward_cells_ref, backward_cells_ref)

    def spot(index):
        return slice(index * channels, (index + 1) * channels)

    lane = lanes((channels, height))
    early = lane < side
    within = lane % side

    def edge_of(ref, start):
        parts = [ref[rank_of(chip, count), start : start + rows, :] for chip in range(count)]
        return jnp.concatenate(parts).astype(F32)

    own_edge, low_edge, high_edge = edge_of(own_ref, block), edge_of(low_ref, 0), edge_of(high_ref, block)
    edges = (
        pltpu.roll(jnp.where(early, own_edge, low_edge), side, 1),
        own_edge,
        pltpu.roll(jnp.where(early, high_edge, own_edge), side, 1),
    )
    planes = ((low_ref, rows), (own_ref, 0), (own_ref, block + rows), (high_ref, 0))
    for at, (ref, start) in enumerate(planes):
        for chip in range(count):
            values = ref[rank_of(chip, count), start : start + block, :].astype(F32)
            wide_ref[at, chip * block : (chip + 1) * block, :] = values

    for c in range(3):
        for tensor in range(2):
            direction = 1 - 2 * tensor
            outside = 0 if direction * (c - 1) < 0 else depth - 1
            if c != 1:
                cells_refs[tensor][3 * c * channels : 3 * (c + 1) * channels, outside * height : (outside + 1) * height] = (
                    jnp.zeros((3 * channels, height), BF16)
                )
            for a in range(3):
                edge = edges[1 + direction * (a - 1)]
                shift = 8 * tensor + direction * (c - 1)
                source = within + direction * (c - 1)
                inside = (within < depth) & (source >= 0) & (source < depth)
                moved = pltpu.roll(edge, -shift % height, 1)
                cells_refs[tensor][spot(3 * c + a), depth * height :] = jnp.where(inside, moved, 0.0).astype(BF16)
    for z in range(depth):
        pieces = [wide_ref[at, pl.ds(z, channels, stride=depth), :] for at in range(4)]
        for step in range(3):
            for tensor, values in enumerate(both_planes(pieces[step], pieces[step + 1], early, side)):
                direction = 1 - 2 * tensor
                a = 1 + direction * (step - 1)
                values = values.astype(BF16)
                for c in range(3):
                    target = z - direction * (c - 1)
                    if 0 <= target < depth:
                        cells_refs[tensor][spot(3 * c + a), target * height : (target + 1) * height] = values

    for tensor in range(2):
        direction = 1 - 2 * tensor
        filters_ref = (forward_ref, backward_ref)[tensor]
        sums = jnp.dot(filters_ref[...], cells_refs[tensor][:, : depth * height], preferred_element_type=F32)
        b = pl.multiple_of((1 + direction - 2 * direction * right) * channels, channels)
        beyond = jnp.dot(filters_ref[pl.ds(b, channels), :], cells_refs[tensor][:, depth * height :],
                         preferred_element_type=F32)
        border = jnp.where(right == 1, 0, side - 1)
        for z in range(depth):
            columns = slice(z * height, (z + 1) * height)
            before, middle, after = (sums[spot(b), columns] for b in (1 - direction, 1, 1 + direction))
            before = jnp.where(within == 0, 0.0, pltpu.roll(before, 1, 1))
            after = jnp.where(within == side - 1, 0.0, pltpu.roll(after, height - 1, 1))
            extra = jnp.where(within == border, pltpu.roll(beyond, border + (height - z), 1), 0.0)
            wide_ref[tensor, pl.ds(z, channels, stride=depth), :] = before + middle + after + extra
        for chip in range(count):
            result = wide_ref[tensor, chip * block : (chip + 1) * block, :].astype(BF16)
            send_ref[rank_of(chip, count), tensor * block : (tensor + 1) * block, :] = result


def both_planes(first, second, early, side):
    turned_first, turned_second = pltpu.roll(first, side, 1), pltpu.roll(second, side, 1)
    return jnp.where(early, first, turned_second), jnp.where(early, turned_first, second)


def unpack_kernel(got_ref, features_ref, gradient_ref):
    core = lax.rem(lax.axis_index("gx"), 2)
    count, _, height = got_ref.shape
    rows, _, depth, _ = features_ref.shape
    block = rows * depth
    for level in range(count // 2):
        pair = pair_of(level, core, count)
        for tensor, ref in enumerate((features_ref, gradient_ref)):
            start = tensor * block
            halves = [got_ref[rank_of(2 * level + side, count), start : start + block, :].astype(F32) for side in range(2)]
            for plane, values in enumerate(both(*halves)):
                ref[:, 2 * pair + plane] = values.astype(BF16).reshape(rows, depth, height)


def local(slabs, count, activations, conv_weight, out_grad):
    rows, _, depth, height = activations.shape
    taps, channels, _ = conv_weight.shape
    block = rows * depth
    span = 2 * block + rows
    shared = pieces(taps)[1] * rows
    pairs = count // 2
    send = pl.pallas_call(
        pack_kernel,
        out_shape=jax.ShapeDtypeStruct((count, span + shared, height), BF16),
        in_specs=[HBM, HBM, HBM],
        out_specs=VMEM,
        scratch_shapes=[
            pltpu.VMEM(activations.shape, BF16),
            pltpu.VMEM(out_grad.shape, BF16),
            pltpu.VMEM((taps, rows, channels), BF16),
            pltpu.VMEM((block, height), F32),
            pltpu.SemaphoreType.DMA((3,)),
        ],
        compiler_params=PARAMS,
        name="pack",
    )(*(pltpu.with_memory_space_constraint(x, pltpu.HBM) for x in (activations, out_grad, jnp.swapaxes(conv_weight, 1, 2))))
    got = lax.all_to_all(send, CH[::-1], 0, 0, tiled=True)
    own, own_filters = got[:, :span], got[:, span:]
    across_core = [(slab, slab ^ 1) for slab in range(slabs)]
    across = [(slab, slab ^ (2 if slab % 2 else 8)) for slab in range(slabs)]
    near_filters = lax.ppermute(own_filters, "gx", across)
    core_filters = lax.ppermute(own_filters, "gx", across_core)
    diagonal_filters = lax.ppermute(near_filters, "gx", across_core)
    ring = []
    for side in range(2):
        order = [
            slab * count + 2 * pair_of(pair, slab % 2, count) + side for slab in range(slabs) for pair in range(pairs)
        ]
        ring += zip(order, order[1:] + order[:1])
    low = lax.ppermute(got[:, block:span], ("gx", *CH), ring)
    high = lax.ppermute(got[:, : block + rows], ("gx", *CH), [(to, at) for at, to in ring])
    forward, backward = pl.pallas_call(
        functools.partial(prepare_kernel, taps=taps),
        out_shape=[jax.ShapeDtypeStruct((3 * channels, 9 * channels), BF16)] * 2,
        in_specs=[VMEM] * 4,
        out_specs=[VMEM, VMEM],
        scratch_shapes=[pltpu.VMEM((4, count, shared, channels), BF16)],
        cost_estimate=pl.CostEstimate(flops=0, bytes_accessed=4 * 2**20, transcendentals=0),
        compiler_params=PARAMS,
        name="prepare",
    )(own_filters, core_filters, near_filters, diagonal_filters)
    result = pl.pallas_call(
        functools.partial(conv_kernel, depth=depth),
        out_shape=jax.ShapeDtypeStruct((count, 2 * block, height), BF16),
        in_specs=[VMEM, VMEM, VMEM, VMEM, VMEM],
        out_specs=VMEM,
        scratch_shapes=[
            pltpu.VMEM((9 * channels, (depth + 1) * height), BF16),
            pltpu.VMEM((9 * channels, (depth + 1) * height), BF16),
            pltpu.VMEM((4, channels * depth, height), F32),
        ],
        compiler_params=PARAMS,
        name="conv",
    )(own, low, high, forward, backward)
    back = lax.all_to_all(result, CH[::-1], 0, 0, tiled=True)
    return pl.pallas_call(
        unpack_kernel,
        out_shape=(jax.ShapeDtypeStruct(activations.shape, BF16), jax.ShapeDtypeStruct(out_grad.shape, BF16)),
        in_specs=[VMEM],
        out_specs=(VMEM, VMEM),
        compiler_params=PARAMS,
        name="unpack",
    )(back)


def solution(mesh):
    slabs, count = mesh.shape["gx"], mesh.shape["ch"]
    mesh = Mesh(mesh.devices.reshape(slabs, count // 2, 2), ("gx", *CH))
    return jax.shard_map(
        functools.partial(local, slabs, count),
        mesh=mesh,
        in_specs=(P(CH, "gx", None, None), P(None, None, CH), P(CH, "gx", None, None)),
        out_specs=(P(CH, "gx", None, None), P(CH, "gx", None, None)),
        check_vma=False,
    )
```

```python
import functools

import jax
import jax.numpy as jnp
from jax import lax
from jax.experimental import pallas as pl
from jax.experimental.pallas import tpu as pltpu
from jax.sharding import Mesh, PartitionSpec as P


VMEM = pl.BlockSpec(memory_space=pltpu.VMEM)
HBM = pl.BlockSpec(memory_space=pltpu.HBM)
PARAMS = pltpu.CompilerParams(vmem_limit_bytes=16 * 2**20)
CH = ("level", "turn")
F32 = jnp.float32
BF16 = jnp.bfloat16


def lanes(shape):
    return lax.broadcasted_iota(jnp.int32, shape, len(shape) - 1)


def pair_of(step, core, count):
    return step + core * (count // 2 - 1 - 2 * step)


def chip_of(step, side, count):
    levels = count // 4
    turn = step // levels
    level = side * levels + (step if turn == 0 else 2 * levels - 1 - step)
    return 2 * level + turn


def pieces(taps):
    return (0, taps // 2), (taps + 3) // 4


def places_of(slab):
    core, x, y = lax.rem(slab, 2), lax.rem(slab // 2, 2), slab // 8
    return core, y + core * (x - y), x + core * (y - x)


def rank_of(chip, count):
    return chip % 2 * (count // 2) + chip // 2


def both(first, second):
    size = first.shape[-1]
    early = lanes(first.shape) < size // 2
    turned_first, turned_second = (pltpu.roll(x, size // 2, x.ndim - 1) for x in (first, second))
    return jnp.where(early, first, turned_second), jnp.where(early, turned_first, second)


def pack_kernel(act_hbm, grad_hbm, weight_hbm, send_ref, act_ref, grad_ref, weight_ref, rows_ref, sems):
    copies = [
        pltpu.make_async_copy(source, target, sems.at[at])
        for at, (source, target) in enumerate(
            ((act_hbm, act_ref), (grad_hbm, grad_ref), (weight_hbm, weight_ref))
        )
    ]
    for copy in copies:
        copy.start()
    core = lax.rem(lax.axis_index("gx"), 2)
    count, (rows, _, depth, height) = send_ref.shape[0], act_ref.shape
    taps, _, fan = weight_ref.shape
    block = rows * depth
    side = height // 2
    copies[0].wait()
    copies[1].wait()
    lane = lanes((rows, height))
    for step in range(count // 2):
        pair = pair_of(step, core, count)
        edges = [jnp.zeros((rows, height), F32) for _ in range(2)]
        for plane in range(2):
            maps = []
            for tensor, ref in enumerate((act_ref, grad_ref)):
                values = ref[:, 2 * pair + plane].reshape(block, height).astype(F32)
                maps.append(values)
                rows_ref[...] = values
                for z in range(depth):
                    column = rows_ref[pl.ds(z, rows, stride=depth), :]
                    spot = side * plane + 8 * tensor + z
                    for half in range(2):
                        edge = side - half
                        turned = pltpu.roll(column, (spot - edge) % height, 1)
                        edges[half] = jnp.where(lane == spot, turned, edges[half])
            start = plane * (block + rows)
            for half, values in enumerate(both(*maps)):
                send_ref[rank_of(chip_of(step, half, count), count), start : start + block, :] = values.astype(BF16)
        for half in range(2):
            send_ref[rank_of(chip_of(step, half, count), count), block : block + rows, :] = edges[half].astype(BF16)
    copies[2].wait()
    _, place, _ = places_of(lax.axis_index("gx"))
    (_, second), size = pieces(taps)
    filters = weight_ref[pl.ds(core * second + place * size, size)].reshape(size * rows, fan)
    for chip in range(count):
        send_ref[chip, 2 * block + rows :, :] = filters


def prepare_kernel(own_ref, core_ref, near_ref, diagonal_ref, forward_ref, backward_ref, filters_ref, *, taps):
    count, _, channels = own_ref.shape
    rows = channels // count
    core, place, other = places_of(lax.axis_index("gx"))
    (_, second), size = pieces(taps)
    for chip in range(count):
        at = rank_of(chip, count)
        filters_ref[2 * core + place, chip] = own_ref[at]
        filters_ref[2 * core + 1 - place, chip] = near_ref[at]
        filters_ref[2 - 2 * core + other, chip] = core_ref[at]
        filters_ref[3 - 2 * core - other, chip] = diagonal_ref[at]

    def spot(index):
        return slice(index * channels, (index + 1) * channels)

    for a in range(3):
        for b in range(3):
            for c in range(3):
                tap = 9 * a + 3 * b + c
                half = 0 if tap < 2 * size else 1
                part, at = divmod(tap - half * second, size)
                matrix = filters_ref[2 * half + part, :, at * rows : (at + 1) * rows, :].reshape(channels, channels)
                forward_ref[spot(b), spot(3 * c + a)] = matrix
                backward_ref[spot(b), spot(3 * c + a)] = matrix.T


def conv_kernel(own_ref, low_ref, high_ref, forward_ref, backward_ref, send_ref,
                forward_cells_ref, backward_cells_ref, wide_ref, *, depth):
    count, span, height = own_ref.shape
    rows = span // (2 * depth + 1)
    block = rows * depth
    channels = count * rows
    side = height // 2
    right = lax.axis_index("level") // (count // 4)
    cells_refs = (forward_cells_ref, backward_cells_ref)

    def spot(index):
        return slice(index * channels, (index + 1) * channels)

    lane = lanes((channels, height))
    early = lane < side
    within = lane % side

    def edge_of(ref, start):
        parts = [ref[rank_of(chip, count), start : start + rows, :] for chip in range(count)]
        return jnp.concatenate(parts).astype(F32)

    own_edge, low_edge, high_edge = edge_of(own_ref, block), edge_of(low_ref, 0), edge_of(high_ref, block)
    edges = (
        pltpu.roll(jnp.where(early, own_edge, low_edge), side, 1),
        own_edge,
        pltpu.roll(jnp.where(early, high_edge, own_edge), side, 1),
    )
    planes = ((low_ref, rows), (own_ref, 0), (own_ref, block + rows), (high_ref, 0))
    for at, (ref, start) in enumerate(planes):
        for chip in range(count):
            values = ref[rank_of(chip, count), start : start + block, :].astype(F32)
            wide_ref[at, chip * block : (chip + 1) * block, :] = values

    for c in range(3):
        for tensor in range(2):
            direction = 1 - 2 * tensor
            outside = 0 if direction * (c - 1) < 0 else depth - 1
            if c != 1:
                cells_refs[tensor][3 * c * channels : 3 * (c + 1) * channels, outside * height : (outside + 1) * height] = (
                    jnp.zeros((3 * channels, height), BF16)
                )
            for a in range(3):
                edge = edges[1 + direction * (a - 1)]
                shift = 8 * tensor + direction * (c - 1)
                source = within + direction * (c - 1)
                inside = (within < depth) & (source >= 0) & (source < depth)
                moved = pltpu.roll(edge, -shift % height, 1)
                cells_refs[tensor][spot(3 * c + a), depth * height :] = jnp.where(inside, moved, 0.0).astype(BF16)
    for z in range(depth):
        pieces = [wide_ref[at, pl.ds(z, channels, stride=depth), :] for at in range(4)]
        for step in range(3):
            for tensor, values in enumerate(both_planes(pieces[step], pieces[step + 1], early, side)):
                direction = 1 - 2 * tensor
                a = 1 + direction * (step - 1)
                values = values.astype(BF16)
                for c in range(3):
                    target = z - direction * (c - 1)
                    if 0 <= target < depth:
                        cells_refs[tensor][spot(3 * c + a), target * height : (target + 1) * height] = values

    for tensor in range(2):
        direction = 1 - 2 * tensor
        filters_ref = (forward_ref, backward_ref)[tensor]
        sums = jnp.dot(filters_ref[...], cells_refs[tensor][:, : depth * height], preferred_element_type=F32)
        b = pl.multiple_of((1 + direction - 2 * direction * right) * channels, channels)
        beyond = jnp.dot(filters_ref[pl.ds(b, channels), :], cells_refs[tensor][:, depth * height :],
                         preferred_element_type=F32)
        border = jnp.where(right == 1, 0, side - 1)
        for z in range(depth):
            columns = slice(z * height, (z + 1) * height)
            before, middle, after = (sums[spot(b), columns] for b in (1 - direction, 1, 1 + direction))
            before = jnp.where(within == 0, 0.0, pltpu.roll(before, 1, 1))
            after = jnp.where(within == side - 1, 0.0, pltpu.roll(after, height - 1, 1))
            extra = jnp.where(within == border, pltpu.roll(beyond, border + (height - z), 1), 0.0)
            wide_ref[tensor, pl.ds(z, channels, stride=depth), :] = before + middle + after + extra
        for chip in range(count):
            result = wide_ref[tensor, chip * block : (chip + 1) * block, :].astype(BF16)
            send_ref[rank_of(chip, count), tensor * block : (tensor + 1) * block, :] = result


def both_planes(first, second, early, side):
    turned_first, turned_second = pltpu.roll(first, side, 1), pltpu.roll(second, side, 1)
    return jnp.where(early, first, turned_second), jnp.where(early, turned_first, second)


def unpack_kernel(got_ref, features_ref, gradient_ref):
    core = lax.rem(lax.axis_index("gx"), 2)
    count, _, height = got_ref.shape
    rows, _, depth, _ = features_ref.shape
    block = rows * depth
    for step in range(count // 2):
        pair = pair_of(step, core, count)
        for tensor, ref in enumerate((features_ref, gradient_ref)):
            start = tensor * block
            halves = [got_ref[rank_of(chip_of(step, side, count), count), start : start + block, :].astype(F32) for side in range(2)]
            for plane, values in enumerate(both(*halves)):
                ref[:, 2 * pair + plane] = values.astype(BF16).reshape(rows, depth, height)


def local(slabs, count, activations, conv_weight, out_grad):
    rows, _, depth, height = activations.shape
    taps, channels, _ = conv_weight.shape
    block = rows * depth
    span = 2 * block + rows
    shared = pieces(taps)[1] * rows
    pairs = count // 2
    send = pl.pallas_call(
        pack_kernel,
        out_shape=jax.ShapeDtypeStruct((count, span + shared, height), BF16),
        in_specs=[HBM, HBM, HBM],
        out_specs=VMEM,
        scratch_shapes=[
            pltpu.VMEM(activations.shape, BF16),
            pltpu.VMEM(out_grad.shape, BF16),
            pltpu.VMEM((taps, rows, channels), BF16),
            pltpu.VMEM((block, height), F32),
            pltpu.SemaphoreType.DMA((3,)),
        ],
        compiler_params=PARAMS,
        name="pack",
    )(*(pltpu.with_memory_space_constraint(x, pltpu.HBM) for x in (activations, out_grad, jnp.swapaxes(conv_weight, 1, 2))))
    got = lax.all_to_all(send, CH[::-1], 0, 0, tiled=True)
    own, own_filters = got[:, :span], got[:, span:]
    across_core = [(slab, slab ^ 1) for slab in range(slabs)]
    across = [(slab, slab ^ (2 if slab % 2 else 8)) for slab in range(slabs)]
    near_filters = lax.ppermute(own_filters, "gx", across)
    core_filters = lax.ppermute(own_filters, "gx", across_core)
    diagonal_filters = lax.ppermute(near_filters, "gx", across_core)
    ring = []
    for side in range(2):
        order = [
            slab * count + chip_of(pair_of(pair, slab % 2, count), side, count)
            for slab in range(slabs)
            for pair in range(pairs)
        ]
        ring += zip(order, order[1:] + order[:1])
    low = lax.ppermute(got[:, block:span], ("gx", *CH), ring)
    high = lax.ppermute(got[:, : block + rows], ("gx", *CH), [(to, at) for at, to in ring])
    forward, backward = pl.pallas_call(
        functools.partial(prepare_kernel, taps=taps),
        out_shape=[jax.ShapeDtypeStruct((3 * channels, 9 * channels), BF16)] * 2,
        in_specs=[VMEM] * 4,
        out_specs=[VMEM, VMEM],
        scratch_shapes=[pltpu.VMEM((4, count, shared, channels), BF16)],
        cost_estimate=pl.CostEstimate(flops=0, bytes_accessed=4 * 2**20, transcendentals=0),
        compiler_params=PARAMS,
        name="prepare",
    )(own_filters, core_filters, near_filters, diagonal_filters)
    result = pl.pallas_call(
        functools.partial(conv_kernel, depth=depth),
        out_shape=jax.ShapeDtypeStruct((count, 2 * block, height), BF16),
        in_specs=[VMEM, VMEM, VMEM, VMEM, VMEM],
        out_specs=VMEM,
        scratch_shapes=[
            pltpu.VMEM((9 * channels, (depth + 1) * height), BF16),
            pltpu.VMEM((9 * channels, (depth + 1) * height), BF16),
            pltpu.VMEM((4, channels * depth, height), F32),
        ],
        compiler_params=PARAMS,
        name="conv",
    )(own, low, high, forward, backward)
    back = lax.all_to_all(result, CH[::-1], 0, 0, tiled=True)
    return pl.pallas_call(
        unpack_kernel,
        out_shape=(jax.ShapeDtypeStruct(activations.shape, BF16), jax.ShapeDtypeStruct(out_grad.shape, BF16)),
        in_specs=[VMEM],
        out_specs=(VMEM, VMEM),
        compiler_params=PARAMS,
        name="unpack",
    )(back)


def solution(mesh):
    slabs, count = mesh.shape["gx"], mesh.shape["ch"]
    mesh = Mesh(mesh.devices.reshape(slabs, count // 2, 2), ("gx", *CH))
    return jax.shard_map(
        functools.partial(local, slabs, count),
        mesh=mesh,
        in_specs=(P(CH, "gx", None, None), P(None, None, CH), P(CH, "gx", None, None)),
        out_specs=(P(CH, "gx", None, None), P(CH, "gx", None, None)),
        check_vma=False,
    )
```

```python
import functools

import jax
import jax.numpy as jnp
from jax import lax
from jax.experimental import pallas as pl
from jax.experimental.pallas import tpu as pltpu
from jax.sharding import Mesh, PartitionSpec as P


VMEM = pl.BlockSpec(memory_space=pltpu.VMEM)
HBM = pl.BlockSpec(memory_space=pltpu.HBM)
PARAMS = pltpu.CompilerParams(vmem_limit_bytes=16 * 2**20)
CH = ("level", "side")
F32 = jnp.float32
BF16 = jnp.bfloat16


def lanes(shape):
    return lax.broadcasted_iota(jnp.int32, shape, len(shape) - 1)


def pair_of(level, core, count):
    return level + core * (count // 2 - 1 - 2 * level)


def pieces(taps):
    return (0, taps // 2), (taps + 3) // 4


def places_of(slab):
    core, x, y = lax.rem(slab, 2), lax.rem(slab // 2, 2), slab // 8
    return core, y + core * (x - y), x + core * (y - x)


def odd(slab, level):
    return lax.rem(slab + level, 2)


def rank_of(chip, count):
    return chip % 2 * (count // 2) + chip // 2


def both(first, second):
    size = first.shape[-1]
    early = lanes(first.shape) < size // 2
    turned_first, turned_second = (pltpu.roll(x, size // 2, x.ndim - 1) for x in (first, second))
    return jnp.where(early, first, turned_second), jnp.where(early, turned_first, second)


def pack_kernel(act_hbm, grad_hbm, weight_hbm, send_ref, act_ref, grad_ref, weight_ref, rows_ref, sems):
    copies = [
        pltpu.make_async_copy(source, target, sems.at[at])
        for at, (source, target) in enumerate(
            ((act_hbm, act_ref), (grad_hbm, grad_ref), (weight_hbm, weight_ref))
        )
    ]
    for copy in copies:
        copy.start()
    core = lax.rem(lax.axis_index("gx"), 2)
    count, (rows, _, depth, height) = send_ref.shape[0], act_ref.shape
    taps, _, fan = weight_ref.shape
    block = rows * depth
    side = height // 2
    copies[0].wait()
    copies[1].wait()
    lane = lanes((rows, height))
    for level in range(count // 2):
        pair = pair_of(level, core, count)
        edges = [jnp.zeros((rows, height), F32) for _ in range(2)]
        for plane in range(2):
            maps = []
            for tensor, ref in enumerate((act_ref, grad_ref)):
                values = ref[:, 2 * pair + plane].reshape(block, height).astype(F32)
                maps.append(values)
                rows_ref[...] = values
                for z in range(depth):
                    column = rows_ref[pl.ds(z, rows, stride=depth), :]
                    spot = side * plane + 8 * tensor + z
                    for half in range(2):
                        edge = side - half
                        turned = pltpu.roll(column, (spot - edge) % height, 1)
                        edges[half] = jnp.where(lane == spot, turned, edges[half])
            start = plane * (block + rows)
            for half, values in enumerate(both(*maps)):
                send_ref[rank_of(2 * level + half, count), start : start + block, :] = values.astype(BF16)
        for half in range(2):
            send_ref[rank_of(2 * level + half, count), block : block + rows, :] = edges[half].astype(BF16)
    copies[2].wait()
    _, place, _ = places_of(lax.axis_index("gx"))
    (_, second), size = pieces(taps)
    filters = weight_ref[pl.ds(core * second + place * size, size)].reshape(size * rows, fan)
    for chip in range(count):
        send_ref[chip, 2 * block + rows :, :] = filters


def prepare_kernel(own_ref, core_ref, near_ref, diagonal_ref, forward_ref, backward_ref, filters_ref, *, taps):
    count, _, channels = own_ref.shape
    rows = channels // count
    core, place, other = places_of(lax.axis_index("gx"))
    (_, second), size = pieces(taps)
    for chip in range(count):
        at = rank_of(chip, count)
        filters_ref[2 * core + place, chip] = own_ref[at]
        filters_ref[2 * core + 1 - place, chip] = near_ref[at]
        filters_ref[2 - 2 * core + other, chip] = core_ref[at]
        filters_ref[3 - 2 * core - other, chip] = diagonal_ref[at]

    def spot(index):
        return slice(index * channels, (index + 1) * channels)

    for a in range(3):
        for b in range(3):
            for c in range(3):
                tap = 9 * a + 3 * b + c
                half = 0 if tap < 2 * size else 1
                part, at = divmod(tap - half * second, size)
                matrix = filters_ref[2 * half + part, :, at * rows : (at + 1) * rows, :].reshape(channels, channels)
                forward_ref[spot(b), spot(3 * c + a)] = matrix
                backward_ref[spot(b), spot(3 * c + a)] = matrix.T


def conv_kernel(own_ref, outer_ref, inner_ref, forward_ref, backward_ref, send_ref,
                forward_cells_ref, backward_cells_ref, wide_ref, *, depth):
    count, span, height = own_ref.shape
    rows = span // (2 * depth + 1)
    block = rows * depth
    channels = count * rows
    side = height // 2
    right = lax.axis_index("side")
    cells_refs = (forward_cells_ref, backward_cells_ref)

    def spot(index):
        return slice(index * channels, (index + 1) * channels)

    lane = lanes((channels, height))
    early = lane < side
    within = lane % side

    is_odd = odd(lax.axis_index("gx"), lax.axis_index("level")) == 1

    def own_part(start, size):
        return lambda at: own_ref[at, start : start + size, :].astype(F32)

    def halo_part(first_ref, second_ref, start, size):
        def part(at):
            first, second = (ref[at, start : start + size, :].astype(F32) for ref in (first_ref, second_ref))
            return jnp.where(is_odd, first, second)

        return part

    def edge_of(part):
        return jnp.concatenate([part(rank_of(chip, count)) for chip in range(count)])

    own_edge = edge_of(own_part(block, rows))
    low_edge = edge_of(halo_part(inner_ref, outer_ref, 0, rows))
    high_edge = edge_of(halo_part(outer_ref, inner_ref, block, rows))
    edges = (
        pltpu.roll(jnp.where(early, own_edge, low_edge), side, 1),
        own_edge,
        pltpu.roll(jnp.where(early, high_edge, own_edge), side, 1),
    )
    planes = (
        halo_part(inner_ref, outer_ref, rows, block),
        own_part(0, block),
        own_part(block + rows, block),
        halo_part(outer_ref, inner_ref, 0, block),
    )
    for at, part in enumerate(planes):
        for chip in range(count):
            wide_ref[at, chip * block : (chip + 1) * block, :] = part(rank_of(chip, count))

    for c in range(3):
        for tensor in range(2):
            direction = 1 - 2 * tensor
            outside = 0 if direction * (c - 1) < 0 else depth - 1
            if c != 1:
                cells_refs[tensor][3 * c * channels : 3 * (c + 1) * channels, outside * height : (outside + 1) * height] = (
                    jnp.zeros((3 * channels, height), BF16)
                )
            for a in range(3):
                edge = edges[1 + direction * (a - 1)]
                shift = 8 * tensor + direction * (c - 1)
                source = within + direction * (c - 1)
                inside = (within < depth) & (source >= 0) & (source < depth)
                moved = pltpu.roll(edge, -shift % height, 1)
                cells_refs[tensor][spot(3 * c + a), depth * height :] = jnp.where(inside, moved, 0.0).astype(BF16)
    for z in range(depth):
        pieces = [wide_ref[at, pl.ds(z, channels, stride=depth), :] for at in range(4)]
        for step in range(3):
            for tensor, values in enumerate(both_planes(pieces[step], pieces[step + 1], early, side)):
                direction = 1 - 2 * tensor
                a = 1 + direction * (step - 1)
                values = values.astype(BF16)
                for c in range(3):
                    target = z - direction * (c - 1)
                    if 0 <= target < depth:
                        cells_refs[tensor][spot(3 * c + a), target * height : (target + 1) * height] = values

    for tensor in range(2):
        direction = 1 - 2 * tensor
        filters_ref = (forward_ref, backward_ref)[tensor]
        sums = jnp.dot(filters_ref[...], cells_refs[tensor][:, : depth * height], preferred_element_type=F32)
        b = pl.multiple_of((1 + direction - 2 * direction * right) * channels, channels)
        beyond = jnp.dot(filters_ref[pl.ds(b, channels), :], cells_refs[tensor][:, depth * height :],
                         preferred_element_type=F32)
        border = jnp.where(right == 1, 0, side - 1)
        for z in range(depth):
            columns = slice(z * height, (z + 1) * height)
            before, middle, after = (sums[spot(b), columns] for b in (1 - direction, 1, 1 + direction))
            before = jnp.where(within == 0, 0.0, pltpu.roll(before, 1, 1))
            after = jnp.where(within == side - 1, 0.0, pltpu.roll(after, height - 1, 1))
            extra = jnp.where(within == border, pltpu.roll(beyond, border + (height - z), 1), 0.0)
            wide_ref[tensor, pl.ds(z, channels, stride=depth), :] = before + middle + after + extra
        for chip in range(count):
            result = wide_ref[tensor, chip * block : (chip + 1) * block, :].astype(BF16)
            send_ref[rank_of(chip, count), tensor * block : (tensor + 1) * block, :] = result


def both_planes(first, second, early, side):
    turned_first, turned_second = pltpu.roll(first, side, 1), pltpu.roll(second, side, 1)
    return jnp.where(early, first, turned_second), jnp.where(early, turned_first, second)


def unpack_kernel(got_ref, features_ref, gradient_ref):
    core = lax.rem(lax.axis_index("gx"), 2)
    count, _, height = got_ref.shape
    rows, _, depth, _ = features_ref.shape
    block = rows * depth
    for level in range(count // 2):
        pair = pair_of(level, core, count)
        for tensor, ref in enumerate((features_ref, gradient_ref)):
            start = tensor * block
            halves = [got_ref[rank_of(2 * level + side, count), start : start + block, :].astype(F32) for side in range(2)]
            for plane, values in enumerate(both(*halves)):
                ref[:, 2 * pair + plane] = values.astype(BF16).reshape(rows, depth, height)


def local(slabs, count, activations, conv_weight, out_grad):
    rows, _, depth, height = activations.shape
    taps, channels, _ = conv_weight.shape
    block = rows * depth
    span = 2 * block + rows
    shared = pieces(taps)[1] * rows
    pairs = count // 2
    send = pl.pallas_call(
        pack_kernel,
        out_shape=jax.ShapeDtypeStruct((count, span + shared, height), BF16),
        in_specs=[HBM, HBM, HBM],
        out_specs=VMEM,
        scratch_shapes=[
            pltpu.VMEM(activations.shape, BF16),
            pltpu.VMEM(out_grad.shape, BF16),
            pltpu.VMEM((taps, rows, channels), BF16),
            pltpu.VMEM((block, height), F32),
            pltpu.SemaphoreType.DMA((3,)),
        ],
        compiler_params=PARAMS,
        name="pack",
    )(*(pltpu.with_memory_space_constraint(x, pltpu.HBM) for x in (activations, out_grad, jnp.swapaxes(conv_weight, 1, 2))))
    got = lax.all_to_all(send, CH[::-1], 0, 0, tiled=True)
    own, own_filters = got[:, :span], got[:, span:]
    across_core = [(slab, slab ^ 1) for slab in range(slabs)]
    across = [(slab, slab ^ (2 if slab % 2 else 8)) for slab in range(slabs)]
    near_filters = lax.ppermute(own_filters, "gx", across)
    core_filters = lax.ppermute(own_filters, "gx", across_core)
    diagonal_filters = lax.ppermute(near_filters, "gx", across_core)
    swaps = [], []
    for side in range(2):
        chain = [
            slab * count + 2 * pair_of(pair, slab % 2, count) + side for slab in range(slabs) for pair in range(pairs)
        ]
        for at, device in enumerate(chain):
            after = chain[(at + 1) % len(chain)]
            swaps[at % 2].extend(((device, after), (after, device)))
    is_odd = odd(lax.axis_index("gx"), lax.axis_index("level")) == 1
    lower, upper = got[:, : block + rows], got[:, block:span]
    outer = lax.ppermute(jnp.where(is_odd, upper, lower), ("gx", *CH), swaps[1])
    inner = lax.ppermute(jnp.where(is_odd, lower, upper), ("gx", *CH), swaps[0])
    forward, backward = pl.pallas_call(
        functools.partial(prepare_kernel, taps=taps),
        out_shape=[jax.ShapeDtypeStruct((3 * channels, 9 * channels), BF16)] * 2,
        in_specs=[VMEM] * 4,
        out_specs=[VMEM, VMEM],
        scratch_shapes=[pltpu.VMEM((4, count, shared, channels), BF16)],
        cost_estimate=pl.CostEstimate(flops=0, bytes_accessed=4 * 2**20, transcendentals=0),
        compiler_params=PARAMS,
        name="prepare",
    )(own_filters, core_filters, near_filters, diagonal_filters)
    result = pl.pallas_call(
        functools.partial(conv_kernel, depth=depth),
        out_shape=jax.ShapeDtypeStruct((count, 2 * block, height), BF16),
        in_specs=[VMEM, VMEM, VMEM, VMEM, VMEM],
        out_specs=VMEM,
        scratch_shapes=[
            pltpu.VMEM((9 * channels, (depth + 1) * height), BF16),
            pltpu.VMEM((9 * channels, (depth + 1) * height), BF16),
            pltpu.VMEM((4, channels * depth, height), F32),
        ],
        compiler_params=PARAMS,
        name="conv",
    )(own, outer, inner, forward, backward)
    back = lax.all_to_all(result, CH[::-1], 0, 0, tiled=True)
    return pl.pallas_call(
        unpack_kernel,
        out_shape=(jax.ShapeDtypeStruct(activations.shape, BF16), jax.ShapeDtypeStruct(out_grad.shape, BF16)),
        in_specs=[VMEM],
        out_specs=(VMEM, VMEM),
        compiler_params=PARAMS,
        name="unpack",
    )(back)


def solution(mesh):
    slabs, count = mesh.shape["gx"], mesh.shape["ch"]
    mesh = Mesh(mesh.devices.reshape(slabs, count // 2, 2), ("gx", *CH))
    return jax.shard_map(
        functools.partial(local, slabs, count),
        mesh=mesh,
        in_specs=(P(CH, "gx", None, None), P(None, None, CH), P(CH, "gx", None, None)),
        out_specs=(P(CH, "gx", None, None), P(CH, "gx", None, None)),
        check_vma=False,
    )
```

```python
import functools

import jax
import jax.numpy as jnp
from jax import lax
from jax.experimental import pallas as pl
from jax.experimental.pallas import tpu as pltpu
from jax.sharding import Mesh, PartitionSpec as P


VMEM = pl.BlockSpec(memory_space=pltpu.VMEM)
HBM = pl.BlockSpec(memory_space=pltpu.HBM)
PARAMS = pltpu.CompilerParams(vmem_limit_bytes=16 * 2**20)
CH = ("level", "side")
F32 = jnp.float32
BF16 = jnp.bfloat16


def lanes(shape):
    return lax.broadcasted_iota(jnp.int32, shape, len(shape) - 1)


def pair_of(level, core, count):
    return level + core * (count // 2 - 1 - 2 * level)


def pieces(taps):
    return (0, taps // 2), (taps + 3) // 4


def places_of(slab):
    core, x, y = lax.rem(slab, 2), lax.rem(slab // 2, 2), slab // 8
    return core, y + core * (x - y), x + core * (y - x)


def odd(slab, level):
    return lax.rem(slab + level, 2)


def rank_of(chip, count):
    return chip % 2 * (count // 2) + chip // 2


def both(first, second):
    size = first.shape[-1]
    early = lanes(first.shape) < size // 2
    turned_first, turned_second = (pltpu.roll(x, size // 2, x.ndim - 1) for x in (first, second))
    return jnp.where(early, first, turned_second), jnp.where(early, turned_first, second)


def pack_kernel(act_hbm, grad_hbm, weight_hbm, send_ref, act_ref, grad_ref, weight_ref, rows_ref, sems):
    copies = [
        pltpu.make_async_copy(source, target, sems.at[at])
        for at, (source, target) in enumerate(
            ((act_hbm, act_ref), (grad_hbm, grad_ref), (weight_hbm, weight_ref))
        )
    ]
    for copy in copies:
        copy.start()
    core = lax.rem(lax.axis_index("gx"), 2)
    count, (rows, _, depth, height) = send_ref.shape[0], act_ref.shape
    taps, _, fan = weight_ref.shape
    block = rows * depth
    side = height // 2
    copies[0].wait()
    copies[1].wait()
    lane = lanes((rows, height))
    for level in range(count // 2):
        pair = pair_of(level, core, count)
        edges = [jnp.zeros((rows, height), F32) for _ in range(2)]
        for plane in range(2):
            maps = []
            for tensor, ref in enumerate((act_ref, grad_ref)):
                values = ref[:, 2 * pair + plane].reshape(block, height).astype(F32)
                maps.append(values)
                rows_ref[...] = values
                for z in range(depth):
                    column = rows_ref[pl.ds(z, rows, stride=depth), :]
                    spot = side * plane + 8 * tensor + z
                    for half in range(2):
                        edge = side - half
                        turned = pltpu.roll(column, (spot - edge) % height, 1)
                        edges[half] = jnp.where(lane == spot, turned, edges[half])
            place = plane + lax.rem(pair, 2) * (1 - 2 * plane)
            start = pl.multiple_of(place * (block + rows), 8)
            for half, values in enumerate(both(*maps)):
                send_ref[rank_of(2 * level + half, count), pl.ds(start, block), :] = values.astype(BF16)
        for half in range(2):
            send_ref[rank_of(2 * level + half, count), block : block + rows, :] = edges[half].astype(BF16)
    copies[2].wait()
    _, place, _ = places_of(lax.axis_index("gx"))
    (_, second), size = pieces(taps)
    filters = weight_ref[pl.ds(core * second + place * size, size)].reshape(size * rows, fan)
    for chip in range(count):
        send_ref[chip, 2 * block + rows :, :] = filters


def prepare_kernel(own_ref, core_ref, near_ref, diagonal_ref, forward_ref, backward_ref, filters_ref, *, taps):
    count, _, channels = own_ref.shape
    rows = channels // count
    core, place, other = places_of(lax.axis_index("gx"))
    (_, second), size = pieces(taps)
    for chip in range(count):
        at = rank_of(chip, count)
        filters_ref[2 * core + place, chip] = own_ref[at]
        filters_ref[2 * core + 1 - place, chip] = near_ref[at]
        filters_ref[2 - 2 * core + other, chip] = core_ref[at]
        filters_ref[3 - 2 * core - other, chip] = diagonal_ref[at]

    def spot(index):
        return slice(index * channels, (index + 1) * channels)

    for a in range(3):
        for b in range(3):
            for c in range(3):
                tap = 9 * a + 3 * b + c
                half = 0 if tap < 2 * size else 1
                part, at = divmod(tap - half * second, size)
                matrix = filters_ref[2 * half + part, :, at * rows : (at + 1) * rows, :].reshape(channels, channels)
                forward_ref[spot(b), spot(3 * c + a)] = matrix
                backward_ref[spot(b), spot(3 * c + a)] = matrix.T


def conv_kernel(own_ref, outer_ref, inner_ref, forward_ref, backward_ref, send_ref,
                forward_cells_ref, backward_cells_ref, wide_ref, *, depth):
    count, span, height = own_ref.shape
    rows = span // (2 * depth + 1)
    block = rows * depth
    channels = count * rows
    side = height // 2
    right = lax.axis_index("side")
    cells_refs = (forward_cells_ref, backward_cells_ref)

    def spot(index):
        return slice(index * channels, (index + 1) * channels)

    lane = lanes((channels, height))
    early = lane < side
    within = lane % side

    is_odd = odd(lax.axis_index("gx"), lax.axis_index("level"))

    def edge_of(ref, start):
        parts = [ref[rank_of(chip, count), start : start + rows, :] for chip in range(count)]
        return jnp.concatenate(parts).astype(F32)

    own_edge, outer_edge, inner_edge = edge_of(own_ref, block), edge_of(outer_ref, block), edge_of(inner_ref, 0)
    low_edge = jnp.where(is_odd == 1, inner_edge, outer_edge)
    high_edge = jnp.where(is_odd == 1, outer_edge, inner_edge)
    edges = (
        pltpu.roll(jnp.where(early, own_edge, low_edge), side, 1),
        own_edge,
        pltpu.roll(jnp.where(early, high_edge, own_edge), side, 1),
    )
    planes = (
        (3 * is_odd, outer_ref, 0),
        (1 + is_odd, own_ref, 0),
        (2 - is_odd, own_ref, block + rows),
        (3 - 3 * is_odd, inner_ref, rows),
    )
    for at, ref, start in planes:
        for chip in range(count):
            values = ref[rank_of(chip, count), start : start + block, :].astype(F32)
            wide_ref[at, chip * block : (chip + 1) * block, :] = values

    for c in range(3):
        for tensor in range(2):
            direction = 1 - 2 * tensor
            outside = 0 if direction * (c - 1) < 0 else depth - 1
            if c != 1:
                cells_refs[tensor][3 * c * channels : 3 * (c + 1) * channels, outside * height : (outside + 1) * height] = (
                    jnp.zeros((3 * channels, height), BF16)
                )
            for a in range(3):
                edge = edges[1 + direction * (a - 1)]
                shift = 8 * tensor + direction * (c - 1)
                source = within + direction * (c - 1)
                inside = (within < depth) & (source >= 0) & (source < depth)
                moved = pltpu.roll(edge, -shift % height, 1)
                cells_refs[tensor][spot(3 * c + a), depth * height :] = jnp.where(inside, moved, 0.0).astype(BF16)
    for z in range(depth):
        pieces = [wide_ref[at, pl.ds(z, channels, stride=depth), :] for at in range(4)]
        for step in range(3):
            for tensor, values in enumerate(both_planes(pieces[step], pieces[step + 1], early, side)):
                direction = 1 - 2 * tensor
                a = 1 + direction * (step - 1)
                values = values.astype(BF16)
                for c in range(3):
                    target = z - direction * (c - 1)
                    if 0 <= target < depth:
                        cells_refs[tensor][spot(3 * c + a), target * height : (target + 1) * height] = values

    for tensor in range(2):
        direction = 1 - 2 * tensor
        filters_ref = (forward_ref, backward_ref)[tensor]
        sums = jnp.dot(filters_ref[...], cells_refs[tensor][:, : depth * height], preferred_element_type=F32)
        b = pl.multiple_of((1 + direction - 2 * direction * right) * channels, channels)
        beyond = jnp.dot(filters_ref[pl.ds(b, channels), :], cells_refs[tensor][:, depth * height :],
                         preferred_element_type=F32)
        border = jnp.where(right == 1, 0, side - 1)
        for z in range(depth):
            columns = slice(z * height, (z + 1) * height)
            before, middle, after = (sums[spot(b), columns] for b in (1 - direction, 1, 1 + direction))
            before = jnp.where(within == 0, 0.0, pltpu.roll(before, 1, 1))
            after = jnp.where(within == side - 1, 0.0, pltpu.roll(after, height - 1, 1))
            extra = jnp.where(within == border, pltpu.roll(beyond, border + (height - z), 1), 0.0)
            wide_ref[tensor, pl.ds(z, channels, stride=depth), :] = before + middle + after + extra
        for chip in range(count):
            result = wide_ref[tensor, chip * block : (chip + 1) * block, :].astype(BF16)
            send_ref[rank_of(chip, count), tensor * block : (tensor + 1) * block, :] = result


def both_planes(first, second, early, side):
    turned_first, turned_second = pltpu.roll(first, side, 1), pltpu.roll(second, side, 1)
    return jnp.where(early, first, turned_second), jnp.where(early, turned_first, second)


def unpack_kernel(got_ref, features_ref, gradient_ref):
    core = lax.rem(lax.axis_index("gx"), 2)
    count, _, height = got_ref.shape
    rows, _, depth, _ = features_ref.shape
    block = rows * depth
    for level in range(count // 2):
        pair = pair_of(level, core, count)
        for tensor, ref in enumerate((features_ref, gradient_ref)):
            start = tensor * block
            halves = [got_ref[rank_of(2 * level + side, count), start : start + block, :].astype(F32) for side in range(2)]
            for plane, values in enumerate(both(*halves)):
                ref[:, 2 * pair + plane] = values.astype(BF16).reshape(rows, depth, height)


def local(slabs, count, activations, conv_weight, out_grad):
    rows, _, depth, height = activations.shape
    taps, channels, _ = conv_weight.shape
    block = rows * depth
    span = 2 * block + rows
    shared = pieces(taps)[1] * rows
    pairs = count // 2
    send = pl.pallas_call(
        pack_kernel,
        out_shape=jax.ShapeDtypeStruct((count, span + shared, height), BF16),
        in_specs=[HBM, HBM, HBM],
        out_specs=VMEM,
        scratch_shapes=[
            pltpu.VMEM(activations.shape, BF16),
            pltpu.VMEM(out_grad.shape, BF16),
            pltpu.VMEM((taps, rows, channels), BF16),
            pltpu.VMEM((block, height), F32),
            pltpu.SemaphoreType.DMA((3,)),
        ],
        compiler_params=PARAMS,
        name="pack",
    )(*(pltpu.with_memory_space_constraint(x, pltpu.HBM) for x in (activations, out_grad, jnp.swapaxes(conv_weight, 1, 2))))
    got = lax.all_to_all(send, CH[::-1], 0, 0, tiled=True)
    own, own_filters = got[:, :span], got[:, span:]
    across_core = [(slab, slab ^ 1) for slab in range(slabs)]
    across = [(slab, slab ^ (2 if slab % 2 else 8)) for slab in range(slabs)]
    near_filters = lax.ppermute(own_filters, "gx", across)
    core_filters = lax.ppermute(own_filters, "gx", across_core)
    diagonal_filters = lax.ppermute(near_filters, "gx", across_core)
    swaps = [], []
    for side in range(2):
        chain = [
            slab * count + 2 * pair_of(pair, slab % 2, count) + side for slab in range(slabs) for pair in range(pairs)
        ]
        for at, device in enumerate(chain):
            after = chain[(at + 1) % len(chain)]
            swaps[at % 2].extend(((device, after), (after, device)))
    outer = lax.ppermute(got[:, : block + rows], ("gx", *CH), swaps[1])
    inner = lax.ppermute(got[:, block:span], ("gx", *CH), swaps[0])
    forward, backward = pl.pallas_call(
        functools.partial(prepare_kernel, taps=taps),
        out_shape=[jax.ShapeDtypeStruct((3 * channels, 9 * channels), BF16)] * 2,
        in_specs=[VMEM] * 4,
        out_specs=[VMEM, VMEM],
        scratch_shapes=[pltpu.VMEM((4, count, shared, channels), BF16)],
        cost_estimate=pl.CostEstimate(flops=0, bytes_accessed=4 * 2**20, transcendentals=0),
        compiler_params=PARAMS,
        name="prepare",
    )(own_filters, core_filters, near_filters, diagonal_filters)
    result = pl.pallas_call(
        functools.partial(conv_kernel, depth=depth),
        out_shape=jax.ShapeDtypeStruct((count, 2 * block, height), BF16),
        in_specs=[VMEM, VMEM, VMEM, VMEM, VMEM],
        out_specs=VMEM,
        scratch_shapes=[
            pltpu.VMEM((9 * channels, (depth + 1) * height), BF16),
            pltpu.VMEM((9 * channels, (depth + 1) * height), BF16),
            pltpu.VMEM((4, channels * depth, height), F32),
        ],
        compiler_params=PARAMS,
        name="conv",
    )(own, outer, inner, forward, backward)
    back = lax.all_to_all(result, CH[::-1], 0, 0, tiled=True)
    return pl.pallas_call(
        unpack_kernel,
        out_shape=(jax.ShapeDtypeStruct(activations.shape, BF16), jax.ShapeDtypeStruct(out_grad.shape, BF16)),
        in_specs=[VMEM],
        out_specs=(VMEM, VMEM),
        compiler_params=PARAMS,
        name="unpack",
    )(back)


def solution(mesh):
    slabs, count = mesh.shape["gx"], mesh.shape["ch"]
    mesh = Mesh(mesh.devices.reshape(slabs, count // 2, 2), ("gx", *CH))
    return jax.shard_map(
        functools.partial(local, slabs, count),
        mesh=mesh,
        in_specs=(P(CH, "gx", None, None), P(None, None, CH), P(CH, "gx", None, None)),
        out_specs=(P(CH, "gx", None, None), P(CH, "gx", None, None)),
        check_vma=False,
    )
```

```python
import functools

import jax
import jax.numpy as jnp
from jax import lax
from jax.experimental import pallas as pl
from jax.experimental.pallas import tpu as pltpu
from jax.sharding import Mesh, PartitionSpec as P


VMEM = pl.BlockSpec(memory_space=pltpu.VMEM)
HBM = pl.BlockSpec(memory_space=pltpu.HBM)
PARAMS = pltpu.CompilerParams(vmem_limit_bytes=16 * 2**20)
CH = ("level", "side")
F32 = jnp.float32
BF16 = jnp.bfloat16


def lanes(shape):
    return lax.broadcasted_iota(jnp.int32, shape, len(shape) - 1)


def pair_of(level, core, count):
    step = (level - 1) % (count // 2)
    return step + core * (count // 2 - 1 - 2 * step)


def level_of(pair, core, count):
    step = pair + core * (count // 2 - 1 - 2 * pair)
    return (step + 1) % (count // 2)


def pieces(taps):
    return (0, taps // 2), (taps + 3) // 4


def places_of(slab):
    core, x, y = lax.rem(slab, 2), lax.rem(slab // 2, 2), slab // 8
    return core, y + core * (x - y), x + core * (y - x)


def rising(slab, level):
    return lax.rem(slab + level, 2)


def rank_of(chip, count):
    return chip % 2 * (count // 2) + chip // 2


def both(first, second):
    size = first.shape[-1]
    early = lanes(first.shape) < size // 2
    turned_first, turned_second = (pltpu.roll(x, size // 2, x.ndim - 1) for x in (first, second))
    return jnp.where(early, first, turned_second), jnp.where(early, turned_first, second)


def pack_kernel(act_hbm, grad_hbm, weight_hbm, send_ref, act_ref, grad_ref, weight_ref, rows_ref, sems):
    copies = [
        pltpu.make_async_copy(source, target, sems.at[at])
        for at, (source, target) in enumerate(
            ((act_hbm, act_ref), (grad_hbm, grad_ref), (weight_hbm, weight_ref))
        )
    ]
    for copy in copies:
        copy.start()
    core = lax.rem(lax.axis_index("gx"), 2)
    count, (rows, _, depth, height) = send_ref.shape[0], act_ref.shape
    taps, _, fan = weight_ref.shape
    block = rows * depth
    side = height // 2
    copies[0].wait()
    copies[1].wait()
    lane = lanes((rows, height))
    for level in range(count // 2):
        pair = pair_of(level, core, count)
        edges = [jnp.zeros((rows, height), F32) for _ in range(2)]
        for plane in range(2):
            maps = []
            for tensor, ref in enumerate((act_ref, grad_ref)):
                values = ref[:, 2 * pair + plane].reshape(block, height).astype(F32)
                maps.append(values)
                rows_ref[...] = values
                for z in range(depth):
                    column = rows_ref[pl.ds(z, rows, stride=depth), :]
                    spot = side * plane + 8 * tensor + z
                    for half in range(2):
                        edge = side - half
                        turned = pltpu.roll(column, (spot - edge) % height, 1)
                        edges[half] = jnp.where(lane == spot, turned, edges[half])
            place = plane + (1 - lax.rem(pair, 2)) * (1 - 2 * plane)
            start = pl.multiple_of(place * (block + rows), 8)
            for half, values in enumerate(both(*maps)):
                send_ref[rank_of(2 * level + half, count), pl.ds(start, block), :] = values.astype(BF16)
        for half in range(2):
            send_ref[rank_of(2 * level + half, count), block : block + rows, :] = edges[half].astype(BF16)
    copies[2].wait()
    _, place, _ = places_of(lax.axis_index("gx"))
    (_, second), size = pieces(taps)
    filters = weight_ref[pl.ds(core * second + place * size, size)].reshape(size * rows, fan)
    for chip in range(count):
        send_ref[chip, 2 * block + rows :, :] = filters


def prepare_kernel(own_ref, core_ref, near_ref, diagonal_ref, forward_ref, backward_ref, filters_ref, *, taps):
    count, _, channels = own_ref.shape
    rows = channels // count
    core, place, other = places_of(lax.axis_index("gx"))
    (_, second), size = pieces(taps)
    for chip in range(count):
        at = rank_of(chip, count)
        filters_ref[2 * core + place, chip] = own_ref[at]
        filters_ref[2 * core + 1 - place, chip] = near_ref[at]
        filters_ref[2 - 2 * core + other, chip] = core_ref[at]
        filters_ref[3 - 2 * core - other, chip] = diagonal_ref[at]

    def spot(index):
        return slice(index * channels, (index + 1) * channels)

    for a in range(3):
        for b in range(3):
            for c in range(3):
                tap = 9 * a + 3 * b + c
                half = 0 if tap < 2 * size else 1
                part, at = divmod(tap - half * second, size)
                matrix = filters_ref[2 * half + part, :, at * rows : (at + 1) * rows, :].reshape(channels, channels)
                forward_ref[spot(b), spot(3 * c + a)] = matrix
                backward_ref[spot(b), spot(3 * c + a)] = matrix.T


def conv_kernel(own_ref, outer_ref, inner_ref, forward_ref, backward_ref, send_ref,
                forward_cells_ref, backward_cells_ref, wide_ref, *, depth):
    count, span, height = own_ref.shape
    rows = span // (2 * depth + 1)
    block = rows * depth
    channels = count * rows
    side = height // 2
    right = lax.axis_index("side")
    cells_refs = (forward_cells_ref, backward_cells_ref)

    def spot(index):
        return slice(index * channels, (index + 1) * channels)

    lane = lanes((channels, height))
    early = lane < side
    within = lane % side

    is_rising = rising(lax.axis_index("gx"), lax.axis_index("level"))

    def edge_of(ref, start):
        parts = [ref[rank_of(chip, count), start : start + rows, :] for chip in range(count)]
        return jnp.concatenate(parts).astype(F32)

    own_edge, outer_edge, inner_edge = edge_of(own_ref, block), edge_of(outer_ref, block), edge_of(inner_ref, 0)
    low_edge = jnp.where(is_rising == 1, inner_edge, outer_edge)
    high_edge = jnp.where(is_rising == 1, outer_edge, inner_edge)
    edges = (
        pltpu.roll(jnp.where(early, own_edge, low_edge), side, 1),
        own_edge,
        pltpu.roll(jnp.where(early, high_edge, own_edge), side, 1),
    )
    planes = (
        (3 * is_rising, outer_ref, 0),
        (1 + is_rising, own_ref, 0),
        (2 - is_rising, own_ref, block + rows),
        (3 - 3 * is_rising, inner_ref, rows),
    )
    for at, ref, start in planes:
        for chip in range(count):
            values = ref[rank_of(chip, count), start : start + block, :].astype(F32)
            wide_ref[at, chip * block : (chip + 1) * block, :] = values

    for c in range(3):
        for tensor in range(2):
            direction = 1 - 2 * tensor
            outside = 0 if direction * (c - 1) < 0 else depth - 1
            if c != 1:
                cells_refs[tensor][3 * c * channels : 3 * (c + 1) * channels, outside * height : (outside + 1) * height] = (
                    jnp.zeros((3 * channels, height), BF16)
                )
            for a in range(3):
                edge = edges[1 + direction * (a - 1)]
                shift = 8 * tensor + direction * (c - 1)
                source = within + direction * (c - 1)
                inside = (within < depth) & (source >= 0) & (source < depth)
                moved = pltpu.roll(edge, -shift % height, 1)
                cells_refs[tensor][spot(3 * c + a), depth * height :] = jnp.where(inside, moved, 0.0).astype(BF16)
    for z in range(depth):
        pieces = [wide_ref[at, pl.ds(z, channels, stride=depth), :] for at in range(4)]
        for step in range(3):
            for tensor, values in enumerate(both_planes(pieces[step], pieces[step + 1], early, side)):
                direction = 1 - 2 * tensor
                a = 1 + direction * (step - 1)
                values = values.astype(BF16)
                for c in range(3):
                    target = z - direction * (c - 1)
                    if 0 <= target < depth:
                        cells_refs[tensor][spot(3 * c + a), target * height : (target + 1) * height] = values

    for tensor in range(2):
        direction = 1 - 2 * tensor
        filters_ref = (forward_ref, backward_ref)[tensor]
        sums = jnp.dot(filters_ref[...], cells_refs[tensor][:, : depth * height], preferred_element_type=F32)
        b = pl.multiple_of((1 + direction - 2 * direction * right) * channels, channels)
        beyond = jnp.dot(filters_ref[pl.ds(b, channels), :], cells_refs[tensor][:, depth * height :],
                         preferred_element_type=F32)
        border = jnp.where(right == 1, 0, side - 1)
        for z in range(depth):
            columns = slice(z * height, (z + 1) * height)
            before, middle, after = (sums[spot(b), columns] for b in (1 - direction, 1, 1 + direction))
            before = jnp.where(within == 0, 0.0, pltpu.roll(before, 1, 1))
            after = jnp.where(within == side - 1, 0.0, pltpu.roll(after, height - 1, 1))
            extra = jnp.where(within == border, pltpu.roll(beyond, border + (height - z), 1), 0.0)
            wide_ref[tensor, pl.ds(z, channels, stride=depth), :] = before + middle + after + extra
        for chip in range(count):
            result = wide_ref[tensor, chip * block : (chip + 1) * block, :].astype(BF16)
            send_ref[rank_of(chip, count), tensor * block : (tensor + 1) * block, :] = result


def both_planes(first, second, early, side):
    turned_first, turned_second = pltpu.roll(first, side, 1), pltpu.roll(second, side, 1)
    return jnp.where(early, first, turned_second), jnp.where(early, turned_first, second)


def unpack_kernel(got_ref, features_ref, gradient_ref):
    core = lax.rem(lax.axis_index("gx"), 2)
    count, _, height = got_ref.shape
    rows, _, depth, _ = features_ref.shape
    block = rows * depth
    for level in range(count // 2):
        pair = pair_of(level, core, count)
        for tensor, ref in enumerate((features_ref, gradient_ref)):
            start = tensor * block
            halves = [got_ref[rank_of(2 * level + side, count), start : start + block, :].astype(F32) for side in range(2)]
            for plane, values in enumerate(both(*halves)):
                ref[:, 2 * pair + plane] = values.astype(BF16).reshape(rows, depth, height)


def local(slabs, count, activations, conv_weight, out_grad):
    rows, _, depth, height = activations.shape
    taps, channels, _ = conv_weight.shape
    block = rows * depth
    span = 2 * block + rows
    shared = pieces(taps)[1] * rows
    pairs = count // 2
    send = pl.pallas_call(
        pack_kernel,
        out_shape=jax.ShapeDtypeStruct((count, span + shared, height), BF16),
        in_specs=[HBM, HBM, HBM],
        out_specs=VMEM,
        scratch_shapes=[
            pltpu.VMEM(activations.shape, BF16),
            pltpu.VMEM(out_grad.shape, BF16),
            pltpu.VMEM((taps, rows, channels), BF16),
            pltpu.VMEM((block, height), F32),
            pltpu.SemaphoreType.DMA((3,)),
        ],
        compiler_params=PARAMS,
        name="pack",
    )(*(pltpu.with_memory_space_constraint(x, pltpu.HBM) for x in (activations, out_grad, jnp.swapaxes(conv_weight, 1, 2))))
    got = lax.all_to_all(send, CH[::-1], 0, 0, tiled=True)
    own, own_filters = got[:, :span], got[:, span:]
    across_core = [(slab, slab ^ 1) for slab in range(slabs)]
    across = [(slab, slab ^ (2 if slab % 2 else 8)) for slab in range(slabs)]
    near_filters = lax.ppermute(own_filters, "gx", across)
    core_filters = lax.ppermute(own_filters, "gx", across_core)
    diagonal_filters = lax.ppermute(near_filters, "gx", across_core)
    swaps = [], []
    for side in range(2):
        chain = [
            slab * count + 2 * level_of(pair, slab % 2, count) + side for slab in range(slabs) for pair in range(pairs)
        ]
        for at, device in enumerate(chain):
            after = chain[(at + 1) % len(chain)]
            swaps[at % 2].extend(((device, after), (after, device)))
    outer = lax.ppermute(got[:, : block + rows], ("gx", *CH), swaps[0])
    inner = lax.ppermute(got[:, block:span], ("gx", *CH), swaps[1])
    forward, backward = pl.pallas_call(
        functools.partial(prepare_kernel, taps=taps),
        out_shape=[jax.ShapeDtypeStruct((3 * channels, 9 * channels), BF16)] * 2,
        in_specs=[VMEM] * 4,
        out_specs=[VMEM, VMEM],
        scratch_shapes=[pltpu.VMEM((4, count, shared, channels), BF16)],
        cost_estimate=pl.CostEstimate(flops=0, bytes_accessed=4 * 2**20, transcendentals=0),
        compiler_params=PARAMS,
        name="prepare",
    )(own_filters, core_filters, near_filters, diagonal_filters)
    result = pl.pallas_call(
        functools.partial(conv_kernel, depth=depth),
        out_shape=jax.ShapeDtypeStruct((count, 2 * block, height), BF16),
        in_specs=[VMEM, VMEM, VMEM, VMEM, VMEM],
        out_specs=VMEM,
        scratch_shapes=[
            pltpu.VMEM((9 * channels, (depth + 1) * height), BF16),
            pltpu.VMEM((9 * channels, (depth + 1) * height), BF16),
            pltpu.VMEM((4, channels * depth, height), F32),
        ],
        compiler_params=PARAMS,
        name="conv",
    )(own, outer, inner, forward, backward)
    back = lax.all_to_all(result, CH[::-1], 0, 0, tiled=True)
    return pl.pallas_call(
        unpack_kernel,
        out_shape=(jax.ShapeDtypeStruct(activations.shape, BF16), jax.ShapeDtypeStruct(out_grad.shape, BF16)),
        in_specs=[VMEM],
        out_specs=(VMEM, VMEM),
        compiler_params=PARAMS,
        name="unpack",
    )(back)


def solution(mesh):
    slabs, count = mesh.shape["gx"], mesh.shape["ch"]
    mesh = Mesh(mesh.devices.reshape(slabs, count // 2, 2), ("gx", *CH))
    return jax.shard_map(
        functools.partial(local, slabs, count),
        mesh=mesh,
        in_specs=(P(CH, "gx", None, None), P(None, None, CH), P(CH, "gx", None, None)),
        out_specs=(P(CH, "gx", None, None), P(CH, "gx", None, None)),
        check_vma=False,
    )
```

```python
import functools

import jax
import jax.numpy as jnp
from jax import lax
from jax.experimental import pallas as pl
from jax.experimental.pallas import tpu as pltpu
from jax.sharding import Mesh, PartitionSpec as P


VMEM = pl.BlockSpec(memory_space=pltpu.VMEM)
HBM = pl.BlockSpec(memory_space=pltpu.HBM)
PARAMS = pltpu.CompilerParams(vmem_limit_bytes=16 * 2**20)
CH = ("upper", "lower", "side")
ORDER = ("side", "lower", "upper")
F32 = jnp.float32
BF16 = jnp.bfloat16


def lanes(shape):
    return lax.broadcasted_iota(jnp.int32, shape, len(shape) - 1)


def pair_of(level, core, count):
    return level + core * (count // 2 - 1 - 2 * level)


def pieces(taps):
    return (0, taps // 2), (taps + 3) // 4


def places_of(slab):
    core, x, y = lax.rem(slab, 2), lax.rem(slab // 2, 2), slab // 8
    return core, y + core * (x - y), x + core * (y - x)


def odd(slab, level):
    return lax.rem(slab + level, 2)


def rank_of(chip, count):
    level, side = chip // 2, chip % 2
    levels = count // 2
    return side * levels + level % (levels // 2) * 2 + level // (levels // 2)


def both(first, second):
    size = first.shape[-1]
    early = lanes(first.shape) < size // 2
    turned_first, turned_second = (pltpu.roll(x, size // 2, x.ndim - 1) for x in (first, second))
    return jnp.where(early, first, turned_second), jnp.where(early, turned_first, second)


def pack_kernel(act_hbm, grad_hbm, weight_hbm, send_ref, act_ref, grad_ref, weight_ref, rows_ref, sems):
    copies = [
        pltpu.make_async_copy(source, target, sems.at[at])
        for at, (source, target) in enumerate(
            ((act_hbm, act_ref), (grad_hbm, grad_ref), (weight_hbm, weight_ref))
        )
    ]
    for copy in copies:
        copy.start()
    core = lax.rem(lax.axis_index("gx"), 2)
    count, (rows, _, depth, height) = send_ref.shape[0], act_ref.shape
    taps, _, fan = weight_ref.shape
    block = rows * depth
    side = height // 2
    copies[0].wait()
    copies[1].wait()
    lane = lanes((rows, height))
    for level in range(count // 2):
        pair = pair_of(level, core, count)
        edges = [jnp.zeros((rows, height), F32) for _ in range(2)]
        for plane in range(2):
            maps = []
            for tensor, ref in enumerate((act_ref, grad_ref)):
                values = ref[:, 2 * pair + plane].reshape(block, height).astype(F32)
                maps.append(values)
                rows_ref[...] = values
                for z in range(depth):
                    column = rows_ref[pl.ds(z, rows, stride=depth), :]
                    spot = side * plane + 8 * tensor + z
                    for half in range(2):
                        edge = side - half
                        turned = pltpu.roll(column, (spot - edge) % height, 1)
                        edges[half] = jnp.where(lane == spot, turned, edges[half])
            place = plane + lax.rem(pair, 2) * (1 - 2 * plane)
            start = pl.multiple_of(place * (block + rows), 8)
            for half, values in enumerate(both(*maps)):
                send_ref[rank_of(2 * level + half, count), pl.ds(start, block), :] = values.astype(BF16)
        for half in range(2):
            send_ref[rank_of(2 * level + half, count), block : block + rows, :] = edges[half].astype(BF16)
    copies[2].wait()
    _, place, _ = places_of(lax.axis_index("gx"))
    (_, second), size = pieces(taps)
    filters = weight_ref[pl.ds(core * second + place * size, size)].reshape(size * rows, fan)
    for chip in range(count):
        send_ref[chip, 2 * block + rows :, :] = filters


def prepare_kernel(own_ref, core_ref, near_ref, diagonal_ref, forward_ref, backward_ref, filters_ref, *, taps):
    count, _, channels = own_ref.shape
    rows = channels // count
    core, place, other = places_of(lax.axis_index("gx"))
    (_, second), size = pieces(taps)
    for chip in range(count):
        at = rank_of(chip, count)
        filters_ref[2 * core + place, chip] = own_ref[at]
        filters_ref[2 * core + 1 - place, chip] = near_ref[at]
        filters_ref[2 - 2 * core + other, chip] = core_ref[at]
        filters_ref[3 - 2 * core - other, chip] = diagonal_ref[at]

    def spot(index):
        return slice(index * channels, (index + 1) * channels)

    for a in range(3):
        for b in range(3):
            for c in range(3):
                tap = 9 * a + 3 * b + c
                half = 0 if tap < 2 * size else 1
                part, at = divmod(tap - half * second, size)
                matrix = filters_ref[2 * half + part, :, at * rows : (at + 1) * rows, :].reshape(channels, channels)
                forward_ref[spot(b), spot(3 * c + a)] = matrix
                backward_ref[spot(b), spot(3 * c + a)] = matrix.T


def conv_kernel(own_ref, outer_ref, inner_ref, forward_ref, backward_ref, send_ref,
                forward_cells_ref, backward_cells_ref, wide_ref, *, depth):
    count, span, height = own_ref.shape
    rows = span // (2 * depth + 1)
    block = rows * depth
    channels = count * rows
    side = height // 2
    right = lax.axis_index("side")
    cells_refs = (forward_cells_ref, backward_cells_ref)

    def spot(index):
        return slice(index * channels, (index + 1) * channels)

    lane = lanes((channels, height))
    early = lane < side
    within = lane % side

    is_odd = odd(lax.axis_index("gx"), lax.axis_index("lower"))

    def edge_of(ref, start):
        parts = [ref[rank_of(chip, count), start : start + rows, :] for chip in range(count)]
        return jnp.concatenate(parts).astype(F32)

    own_edge, outer_edge, inner_edge = edge_of(own_ref, block), edge_of(outer_ref, block), edge_of(inner_ref, 0)
    low_edge = jnp.where(is_odd == 1, inner_edge, outer_edge)
    high_edge = jnp.where(is_odd == 1, outer_edge, inner_edge)
    edges = (
        pltpu.roll(jnp.where(early, own_edge, low_edge), side, 1),
        own_edge,
        pltpu.roll(jnp.where(early, high_edge, own_edge), side, 1),
    )
    planes = (
        (3 * is_odd, outer_ref, 0),
        (1 + is_odd, own_ref, 0),
        (2 - is_odd, own_ref, block + rows),
        (3 - 3 * is_odd, inner_ref, rows),
    )
    for at, ref, start in planes:
        for chip in range(count):
            values = ref[rank_of(chip, count), start : start + block, :].astype(F32)
            wide_ref[at, chip * block : (chip + 1) * block, :] = values

    for c in range(3):
        for tensor in range(2):
            direction = 1 - 2 * tensor
            outside = 0 if direction * (c - 1) < 0 else depth - 1
            if c != 1:
                cells_refs[tensor][3 * c * channels : 3 * (c + 1) * channels, outside * height : (outside + 1) * height] = (
                    jnp.zeros((3 * channels, height), BF16)
                )
            for a in range(3):
                edge = edges[1 + direction * (a - 1)]
                shift = 8 * tensor + direction * (c - 1)
                source = within + direction * (c - 1)
                inside = (within < depth) & (source >= 0) & (source < depth)
                moved = pltpu.roll(edge, -shift % height, 1)
                cells_refs[tensor][spot(3 * c + a), depth * height :] = jnp.where(inside, moved, 0.0).astype(BF16)
    for z in range(depth):
        pieces = [wide_ref[at, pl.ds(z, channels, stride=depth), :] for at in range(4)]
        for step in range(3):
            for tensor, values in enumerate(both_planes(pieces[step], pieces[step + 1], early, side)):
                direction = 1 - 2 * tensor
                a = 1 + direction * (step - 1)
                values = values.astype(BF16)
                for c in range(3):
                    target = z - direction * (c - 1)
                    if 0 <= target < depth:
                        cells_refs[tensor][spot(3 * c + a), target * height : (target + 1) * height] = values

    for tensor in range(2):
        direction = 1 - 2 * tensor
        filters_ref = (forward_ref, backward_ref)[tensor]
        sums = jnp.dot(filters_ref[...], cells_refs[tensor][:, : depth * height], preferred_element_type=F32)
        b = pl.multiple_of((1 + direction - 2 * direction * right) * channels, channels)
        beyond = jnp.dot(filters_ref[pl.ds(b, channels), :], cells_refs[tensor][:, depth * height :],
                         preferred_element_type=F32)
        border = jnp.where(right == 1, 0, side - 1)
        for z in range(depth):
            columns = slice(z * height, (z + 1) * height)
            before, middle, after = (sums[spot(b), columns] for b in (1 - direction, 1, 1 + direction))
            before = jnp.where(within == 0, 0.0, pltpu.roll(before, 1, 1))
            after = jnp.where(within == side - 1, 0.0, pltpu.roll(after, height - 1, 1))
            extra = jnp.where(within == border, pltpu.roll(beyond, border + (height - z), 1), 0.0)
            wide_ref[tensor, pl.ds(z, channels, stride=depth), :] = before + middle + after + extra
        for chip in range(count):
            result = wide_ref[tensor, chip * block : (chip + 1) * block, :].astype(BF16)
            send_ref[rank_of(chip, count), tensor * block : (tensor + 1) * block, :] = result


def both_planes(first, second, early, side):
    turned_first, turned_second = pltpu.roll(first, side, 1), pltpu.roll(second, side, 1)
    return jnp.where(early, first, turned_second), jnp.where(early, turned_first, second)


def unpack_kernel(got_ref, features_ref, gradient_ref):
    core = lax.rem(lax.axis_index("gx"), 2)
    count, _, height = got_ref.shape
    rows, _, depth, _ = features_ref.shape
    block = rows * depth
    for level in range(count // 2):
        pair = pair_of(level, core, count)
        for tensor, ref in enumerate((features_ref, gradient_ref)):
            start = tensor * block
            halves = [got_ref[rank_of(2 * level + side, count), start : start + block, :].astype(F32) for side in range(2)]
            for plane, values in enumerate(both(*halves)):
                ref[:, 2 * pair + plane] = values.astype(BF16).reshape(rows, depth, height)


def local(slabs, count, activations, conv_weight, out_grad):
    rows, _, depth, height = activations.shape
    taps, channels, _ = conv_weight.shape
    block = rows * depth
    span = 2 * block + rows
    shared = pieces(taps)[1] * rows
    pairs = count // 2
    send = pl.pallas_call(
        pack_kernel,
        out_shape=jax.ShapeDtypeStruct((count, span + shared, height), BF16),
        in_specs=[HBM, HBM, HBM],
        out_specs=VMEM,
        scratch_shapes=[
            pltpu.VMEM(activations.shape, BF16),
            pltpu.VMEM(out_grad.shape, BF16),
            pltpu.VMEM((taps, rows, channels), BF16),
            pltpu.VMEM((block, height), F32),
            pltpu.SemaphoreType.DMA((3,)),
        ],
        compiler_params=PARAMS,
        name="pack",
    )(*(pltpu.with_memory_space_constraint(x, pltpu.HBM) for x in (activations, out_grad, jnp.swapaxes(conv_weight, 1, 2))))
    got = lax.all_to_all(send, ORDER, 0, 0, tiled=True)
    own, own_filters = got[:, :span], got[:, span:]
    across_core = [(slab, slab ^ 1) for slab in range(slabs)]
    across = [(slab, slab ^ (2 if slab % 2 else 8)) for slab in range(slabs)]
    near_filters = lax.ppermute(own_filters, "gx", across)
    core_filters = lax.ppermute(own_filters, "gx", across_core)
    diagonal_filters = lax.ppermute(near_filters, "gx", across_core)
    swaps = [], []
    for side in range(2):
        chain = [
            slab * count + 2 * pair_of(pair, slab % 2, count) + side for slab in range(slabs) for pair in range(pairs)
        ]
        for at, device in enumerate(chain):
            after = chain[(at + 1) % len(chain)]
            swaps[at % 2].extend(((device, after), (after, device)))
    outer = lax.ppermute(got[:, : block + rows], ("gx", *CH), swaps[1])
    inner = lax.ppermute(got[:, block:span], ("gx", *CH), swaps[0])
    forward, backward = pl.pallas_call(
        functools.partial(prepare_kernel, taps=taps),
        out_shape=[jax.ShapeDtypeStruct((3 * channels, 9 * channels), BF16)] * 2,
        in_specs=[VMEM] * 4,
        out_specs=[VMEM, VMEM],
        scratch_shapes=[pltpu.VMEM((4, count, shared, channels), BF16)],
        cost_estimate=pl.CostEstimate(flops=0, bytes_accessed=4 * 2**20, transcendentals=0),
        compiler_params=PARAMS,
        name="prepare",
    )(own_filters, core_filters, near_filters, diagonal_filters)
    result = pl.pallas_call(
        functools.partial(conv_kernel, depth=depth),
        out_shape=jax.ShapeDtypeStruct((count, 2 * block, height), BF16),
        in_specs=[VMEM, VMEM, VMEM, VMEM, VMEM],
        out_specs=VMEM,
        scratch_shapes=[
            pltpu.VMEM((9 * channels, (depth + 1) * height), BF16),
            pltpu.VMEM((9 * channels, (depth + 1) * height), BF16),
            pltpu.VMEM((4, channels * depth, height), F32),
        ],
        compiler_params=PARAMS,
        name="conv",
    )(own, outer, inner, forward, backward)
    back = lax.all_to_all(result, ORDER, 0, 0, tiled=True)
    return pl.pallas_call(
        unpack_kernel,
        out_shape=(jax.ShapeDtypeStruct(activations.shape, BF16), jax.ShapeDtypeStruct(out_grad.shape, BF16)),
        in_specs=[VMEM],
        out_specs=(VMEM, VMEM),
        compiler_params=PARAMS,
        name="unpack",
    )(back)


def solution(mesh):
    slabs, count = mesh.shape["gx"], mesh.shape["ch"]
    mesh = Mesh(mesh.devices.reshape(slabs, 2, count // 4, 2), ("gx", *CH))
    return jax.shard_map(
        functools.partial(local, slabs, count),
        mesh=mesh,
        in_specs=(P(CH, "gx", None, None), P(None, None, CH), P(CH, "gx", None, None)),
        out_specs=(P(CH, "gx", None, None), P(CH, "gx", None, None)),
        check_vma=False,
    )
```

```python
import functools

import jax
import jax.numpy as jnp
from jax import lax
from jax.experimental import pallas as pl
from jax.experimental.pallas import tpu as pltpu
from jax.sharding import Mesh, PartitionSpec as P


VMEM = pl.BlockSpec(memory_space=pltpu.VMEM)
HBM = pl.BlockSpec(memory_space=pltpu.HBM)
PARAMS = pltpu.CompilerParams(vmem_limit_bytes=16 * 2**20)
CH = ("level", "side")
F32 = jnp.float32
BF16 = jnp.bfloat16


def lanes(shape):
    return lax.broadcasted_iota(jnp.int32, shape, len(shape) - 1)


def pair_of(level, core, count):
    return level + core * (count // 2 - 1 - 2 * level)


def pieces(taps):
    return (0, taps // 2), (taps + 3) // 4


def places_of(slab):
    core, x, y = lax.rem(slab, 2), lax.rem(slab // 2, 2), slab // 8
    return core, y + core * (x - y), x + core * (y - x)


def odd(slab, level):
    return lax.rem(slab + level, 2)


def rank_of(chip, count):
    return chip % 2 * (count // 2) + chip // 2


def both(first, second):
    size = first.shape[-1]
    early = lanes(first.shape) < size // 2
    turned_first, turned_second = (pltpu.roll(x, size // 2, x.ndim - 1) for x in (first, second))
    return jnp.where(early, first, turned_second), jnp.where(early, turned_first, second)


def pack_kernel(act_hbm, grad_hbm, weight_hbm, send_ref, act_ref, grad_ref, weight_ref, rows_ref, sems):
    copies = [
        pltpu.make_async_copy(source, target, sems.at[at])
        for at, (source, target) in enumerate(
            ((act_hbm, act_ref), (grad_hbm, grad_ref), (weight_hbm, weight_ref))
        )
    ]
    for copy in copies:
        copy.start()
    core = lax.rem(lax.axis_index("gx"), 2)
    count, (rows, _, depth, height) = send_ref.shape[0], act_ref.shape
    taps, _, fan = weight_ref.shape
    block = rows * depth
    side = height // 2
    copies[0].wait()
    copies[1].wait()
    lane = lanes((rows, height))
    for level in range(count // 2):
        pair = pair_of(level, core, count)
        edges = [jnp.zeros((rows, height), F32) for _ in range(2)]
        for plane in range(2):
            maps = []
            for tensor, ref in enumerate((act_ref, grad_ref)):
                values = ref[:, 2 * pair + plane].reshape(block, height).astype(F32)
                maps.append(values)
                rows_ref[...] = values
                for z in range(depth):
                    column = rows_ref[pl.ds(z, rows, stride=depth), :]
                    spot = side * plane + 8 * tensor + z
                    for half in range(2):
                        edge = side - half
                        turned = pltpu.roll(column, (spot - edge) % height, 1)
                        edges[half] = jnp.where(lane == spot, turned, edges[half])
            place = plane + lax.rem(pair, 2) * (1 - 2 * plane)
            start = pl.multiple_of(place * (block + rows), 8)
            for half, values in enumerate(both(*maps)):
                send_ref[rank_of(2 * level + half, count), pl.ds(start, block), :] = values.astype(BF16)
        for half in range(2):
            send_ref[rank_of(2 * level + half, count), block : block + rows, :] = edges[half].astype(BF16)
    copies[2].wait()
    _, place, _ = places_of(lax.axis_index("gx"))
    (_, second), size = pieces(taps)
    filters = weight_ref[pl.ds(core * second + place * size, size)].reshape(size * rows, fan)
    for chip in range(count):
        send_ref[chip, 2 * block + rows :, :] = filters


def prepare_kernel(own_ref, core_ref, near_ref, diagonal_ref, forward_ref, backward_ref, filters_ref, *, taps):
    count, _, channels = own_ref.shape
    rows = channels // count
    core, place, other = places_of(lax.axis_index("gx"))
    (_, second), size = pieces(taps)
    for chip in range(count):
        at = rank_of(chip, count)
        filters_ref[2 * core + place, chip] = own_ref[at]
        filters_ref[2 * core + 1 - place, chip] = near_ref[at]
        filters_ref[2 - 2 * core + other, chip] = core_ref[at]
        filters_ref[3 - 2 * core - other, chip] = diagonal_ref[at]

    def spot(index):
        return slice(index * channels, (index + 1) * channels)

    for a in range(3):
        for b in range(3):
            for c in range(3):
                tap = 9 * a + 3 * b + c
                half = 0 if tap < 2 * size else 1
                part, at = divmod(tap - half * second, size)
                matrix = filters_ref[2 * half + part, :, at * rows : (at + 1) * rows, :].reshape(channels, channels)
                forward_ref[spot(b), spot(3 * c + a)] = matrix
                backward_ref[spot(b), spot(3 * c + a)] = matrix.T


def conv_kernel(own_ref, outer_ref, inner_ref, forward_ref, backward_ref, send_ref,
                forward_cells_ref, backward_cells_ref, wide_ref, sums_ref, *, depth):
    count, span, height = own_ref.shape
    rows = span // (2 * depth + 1)
    block = rows * depth
    channels = count * rows
    side = height // 2
    right = lax.axis_index("side")
    cells_refs = (forward_cells_ref, backward_cells_ref)

    def spot(index):
        return slice(index * channels, (index + 1) * channels)

    lane = lanes((channels, height))
    early = lane < side
    within = lane % side

    is_odd = odd(lax.axis_index("gx"), lax.axis_index("level"))

    def edge_of(ref, start):
        parts = [ref[rank_of(chip, count), start : start + rows, :] for chip in range(count)]
        return jnp.concatenate(parts).astype(F32)

    own_edge, outer_edge, inner_edge = edge_of(own_ref, block), edge_of(outer_ref, block), edge_of(inner_ref, 0)
    low_edge = jnp.where(is_odd == 1, inner_edge, outer_edge)
    high_edge = jnp.where(is_odd == 1, outer_edge, inner_edge)
    edges = (
        pltpu.roll(jnp.where(early, own_edge, low_edge), side, 1),
        own_edge,
        pltpu.roll(jnp.where(early, high_edge, own_edge), side, 1),
    )
    planes = (
        (3 * is_odd, outer_ref, 0),
        (1 + is_odd, own_ref, 0),
        (2 - is_odd, own_ref, block + rows),
        (3 - 3 * is_odd, inner_ref, rows),
    )
    for at, ref, start in planes:
        for chip in range(count):
            values = ref[rank_of(chip, count), start : start + block, :].astype(F32)
            wide_ref[at, chip * block : (chip + 1) * block, :] = values

    def gather(tensor):
        direction = 1 - 2 * tensor
        cells_ref = cells_refs[tensor]
        for c in range(3):
            outside = 0 if direction * (c - 1) < 0 else depth - 1
            if c != 1:
                cells_ref[3 * c * channels : 3 * (c + 1) * channels, outside * height : (outside + 1) * height] = (
                    jnp.zeros((3 * channels, height), BF16)
                )
            for a in range(3):
                edge = edges[1 + direction * (a - 1)]
                shift = 8 * tensor + direction * (c - 1)
                source = within + direction * (c - 1)
                inside = (within < depth) & (source >= 0) & (source < depth)
                moved = pltpu.roll(edge, -shift % height, 1)
                cells_ref[spot(3 * c + a), depth * height :] = jnp.where(inside, moved, 0.0).astype(BF16)
        for z in range(depth):
            pieces = [wide_ref[at, pl.ds(z, channels, stride=depth), :] for at in range(4)]
            for step in range(3):
                values = both_planes(pieces[step], pieces[step + 1], early, side)[tensor].astype(BF16)
                a = 1 + direction * (step - 1)
                for c in range(3):
                    target = z - direction * (c - 1)
                    if 0 <= target < depth:
                        cells_ref[spot(3 * c + a), target * height : (target + 1) * height] = values

    def multiply(tensor):
        direction = 1 - 2 * tensor
        filters_ref, cells_ref = (forward_ref, backward_ref)[tensor], cells_refs[tensor]
        sums = jnp.dot(filters_ref[...], cells_ref[:, : depth * height], preferred_element_type=F32)
        b = pl.multiple_of((1 + direction - 2 * direction * right) * channels, channels)
        beyond = jnp.dot(filters_ref[pl.ds(b, channels), :], cells_ref[:, depth * height :], preferred_element_type=F32)
        return sums, beyond

    def finish(tensor, sums, beyond):
        direction = 1 - 2 * tensor
        border = jnp.where(right == 1, 0, side - 1)
        for z in range(depth):
            columns = slice(z * height, (z + 1) * height)
            before, middle, after = (sums[spot(b), columns] for b in (1 - direction, 1, 1 + direction))
            before = jnp.where(within == 0, 0.0, pltpu.roll(before, 1, 1))
            after = jnp.where(within == side - 1, 0.0, pltpu.roll(after, height - 1, 1))
            extra = jnp.where(within == border, pltpu.roll(beyond, border + (height - z), 1), 0.0)
            sums_ref[tensor, pl.ds(z, channels, stride=depth), :] = before + middle + after + extra
        for chip in range(count):
            result = sums_ref[tensor, chip * block : (chip + 1) * block, :].astype(BF16)
            send_ref[rank_of(chip, count), tensor * block : (tensor + 1) * block, :] = result

    gather(0)
    first = multiply(0)
    gather(1)
    second = multiply(1)
    finish(0, *first)
    finish(1, *second)


def both_planes(first, second, early, side):
    turned_first, turned_second = pltpu.roll(first, side, 1), pltpu.roll(second, side, 1)
    return jnp.where(early, first, turned_second), jnp.where(early, turned_first, second)


def unpack_kernel(got_ref, features_ref, gradient_ref):
    core = lax.rem(lax.axis_index("gx"), 2)
    count, _, height = got_ref.shape
    rows, _, depth, _ = features_ref.shape
    block = rows * depth
    for level in range(count // 2):
        pair = pair_of(level, core, count)
        for tensor, ref in enumerate((features_ref, gradient_ref)):
            start = tensor * block
            halves = [got_ref[rank_of(2 * level + side, count), start : start + block, :].astype(F32) for side in range(2)]
            for plane, values in enumerate(both(*halves)):
                ref[:, 2 * pair + plane] = values.astype(BF16).reshape(rows, depth, height)


def local(slabs, count, activations, conv_weight, out_grad):
    rows, _, depth, height = activations.shape
    taps, channels, _ = conv_weight.shape
    block = rows * depth
    span = 2 * block + rows
    shared = pieces(taps)[1] * rows
    pairs = count // 2
    send = pl.pallas_call(
        pack_kernel,
        out_shape=jax.ShapeDtypeStruct((count, span + shared, height), BF16),
        in_specs=[HBM, HBM, HBM],
        out_specs=VMEM,
        scratch_shapes=[
            pltpu.VMEM(activations.shape, BF16),
            pltpu.VMEM(out_grad.shape, BF16),
            pltpu.VMEM((taps, rows, channels), BF16),
            pltpu.VMEM((block, height), F32),
            pltpu.SemaphoreType.DMA((3,)),
        ],
        compiler_params=PARAMS,
        name="pack",
    )(*(pltpu.with_memory_space_constraint(x, pltpu.HBM) for x in (activations, out_grad, jnp.swapaxes(conv_weight, 1, 2))))
    got = lax.all_to_all(send, CH[::-1], 0, 0, tiled=True)
    own, own_filters = got[:, :span], got[:, span:]
    across_core = [(slab, slab ^ 1) for slab in range(slabs)]
    across = [(slab, slab ^ (2 if slab % 2 else 8)) for slab in range(slabs)]
    near_filters = lax.ppermute(own_filters, "gx", across)
    core_filters = lax.ppermute(own_filters, "gx", across_core)
    diagonal_filters = lax.ppermute(near_filters, "gx", across_core)
    swaps = [], []
    for side in range(2):
        chain = [
            slab * count + 2 * pair_of(pair, slab % 2, count) + side for slab in range(slabs) for pair in range(pairs)
        ]
        for at, device in enumerate(chain):
            after = chain[(at + 1) % len(chain)]
            swaps[at % 2].extend(((device, after), (after, device)))
    outer = lax.ppermute(got[:, : block + rows], ("gx", *CH), swaps[1])
    inner = lax.ppermute(got[:, block:span], ("gx", *CH), swaps[0])
    forward, backward = pl.pallas_call(
        functools.partial(prepare_kernel, taps=taps),
        out_shape=[jax.ShapeDtypeStruct((3 * channels, 9 * channels), BF16)] * 2,
        in_specs=[VMEM] * 4,
        out_specs=[VMEM, VMEM],
        scratch_shapes=[pltpu.VMEM((4, count, shared, channels), BF16)],
        cost_estimate=pl.CostEstimate(flops=0, bytes_accessed=4 * 2**20, transcendentals=0),
        compiler_params=pltpu.CompilerParams(vmem_limit_bytes=16 * 2**20),
        name="prepare",
    )(own_filters, core_filters, near_filters, diagonal_filters)
    result = pl.pallas_call(
        functools.partial(conv_kernel, depth=depth),
        out_shape=jax.ShapeDtypeStruct((count, 2 * block, height), BF16),
        in_specs=[VMEM, VMEM, VMEM, VMEM, VMEM],
        out_specs=VMEM,
        scratch_shapes=[
            pltpu.VMEM((9 * channels, (depth + 1) * height), BF16),
            pltpu.VMEM((9 * channels, (depth + 1) * height), BF16),
            pltpu.VMEM((4, channels * depth, height), F32),
            pltpu.VMEM((2, channels * depth, height), F32),
        ],
        compiler_params=PARAMS,
        name="conv",
    )(own, outer, inner, forward, backward)
    back = lax.all_to_all(result, CH[::-1], 0, 0, tiled=True)
    return pl.pallas_call(
        unpack_kernel,
        out_shape=(jax.ShapeDtypeStruct(activations.shape, BF16), jax.ShapeDtypeStruct(out_grad.shape, BF16)),
        in_specs=[VMEM],
        out_specs=(VMEM, VMEM),
        compiler_params=PARAMS,
        name="unpack",
    )(back)


def solution(mesh):
    slabs, count = mesh.shape["gx"], mesh.shape["ch"]
    mesh = Mesh(mesh.devices.reshape(slabs, count // 2, 2), ("gx", *CH))
    return jax.shard_map(
        functools.partial(local, slabs, count),
        mesh=mesh,
        in_specs=(P(CH, "gx", None, None), P(None, None, CH), P(CH, "gx", None, None)),
        out_specs=(P(CH, "gx", None, None), P(CH, "gx", None, None)),
        check_vma=False,
    )
```
